128 devices in a mesh: row: 16 (over x, y), col: 8 (over z, core).
Axes of the slice: x: 4, y: 4, z: 4, core: 2. Of those that a mesh axis runs over, the one named last changes fastest.
Arguments:
- hidden_input: bfloat16 [8192, 4096], P('row', 'col'), may hold values from -6 to 6
- input_norm_gain: bfloat16 [4096], replicated, may hold values from 0.5 to 1.5
- query_norm_gain: bfloat16 [128], replicated, may hold values from 0.099609375 to 1.8984375
- key_norm_gain: bfloat16 [128], replicated, may hold values from 0.5 to 1.5
- query_key_value_weight: bfloat16 [4096, 6144], P('row', 'col'), may hold values from -0.09375 to 0.09375
- output_weight: bfloat16 [4096, 4096], P('row', 'col'), may hold values from -0.25 to 0.25
- adapter_down_maps: bfloat16 [16, 32, 4096], P('row'), may hold values from -0.09375 to 0.09375
- adapter_up_maps: bfloat16 [16, 16, 5120], P('row', None, 'col'), may hold values from -1.5 to 1.5
- output_down_maps: bfloat16 [16, 16, 4096], P('row', None, 'col'), may hold values from -0.25 to 0.25
- output_up_maps: bfloat16 [16, 16, 4096], P('row'), may hold values from -1.5 to 1.5
- prompt_adapter: int32 [64], P('row'), may hold values from 0 to 15
- adapter_position: int32 [16], replicated, may hold values from 0 to 15, each once
- prompt_length: int32 [16, 4], P('row'), may hold values from 1 to 256, 512 in all within a row
- cache_length: int32 [64], P('row'), may hold values from 0 to 1024, as said below
- page_owner_row: int32 [256, 1], replicated, may hold values from 0 to 15; in each aligned block of 16 rows (0 to 15, 16 to 31, ...) at most 2 rows name the same one
- page_store_index: int32 [256], replicated, may hold values from 0 to 7
- cache_page_store: bfloat16 [128, 2, 128, 1024], P('row', None, None, 'col'), may hold values from -160 to 160, as said below
Outputs:
- hidden_output: bfloat16 [8192, 4096], P('row', 'col')
- new_cache: bfloat16 [2, 8192, 1024], P(None, 'row', 'col')
The draws below stay inside these ranges and needn't reach their ends.
Inputs may be any that keep to these rules, and one draw needn't show every extreme that they name: `adapter_position`: a permutation of the slots. `prompt_length`: each row of 4 lengths sums to 512; the largest of each row is exactly 256. `cache_length`: among the 4 prompts of each row group exactly 2 have a cached prefix, longer than 896; the others have 0; some prompt has exactly 1024. `page_owner_row`: in each aligned block of 16 requests (those of one row group) no holder is named more than 2 times, and in some block some holder exactly 2 times. `cache_page_store`: finite values.
All inputs are finite; a program needn't handle non-finite values.
Results may differ from the reference program's by a relative error of at most 0.018.
The reference program's roundings to bfloat16 on the way count: a program that leaves them out, or rounds other values in their place, can miss the bound.
Values may be sent and summed in bfloat16 or wider, within the bound.
No kernel may reach another device: no remote copies, remote signals or barrier semaphores. Data moves between devices by JAX's collectives and lax.ppermute only.
A program may use at most 128 MiB of HBM per device.

```python
import math
import jax
import jax.numpy as jnp
import numpy as np
from jax import lax

MODEL_WIDTH = 4096
QUERY_HEADS = 32
KEY_VALUE_HEADS = 8
HEAD_WIDTH = 128
ADAPTER_RANK = 16
TOK_ROW = 512
PROMPTS_ROW = 4
CACHED_ROW = 2
PAGE = 128
WIN = 1024
SINKS = 4
CAP = 2
PAGES_DEV = 8
REQ = 16
TOKENS = 8192
PROMPTS = 64
ADAPTER_COUNT = 16
PAGES = 128
N_ROW = 16


def draw_cache_length(key, part):
    key_order = jax.random.fold_in(key, 11)
    key_amount = jax.random.fold_in(key, 12)
    group_count = PROMPTS // PROMPTS_ROW
    ordering = jax.vmap(lambda single: jax.random.permutation(single, PROMPTS_ROW))(jax.random.split(key_order, group_count))
    amounts = WIN - jax.random.randint(key_amount, (group_count, PROMPTS_ROW), 0, PAGE)
    leading = (jnp.arange(group_count)[:, None] == 0) & (ordering == 0)
    amounts = jnp.where(leading, WIN, amounts)
    return jnp.where(ordering < CACHED_ROW, amounts, 0).reshape(PROMPTS).astype(jnp.int32)


def draw_cache_page_store(key, part):
    key_base = jax.random.fold_in(key, 21)
    full_shape = (PAGES, 2, PAGE, KEY_VALUE_HEADS * HEAD_WIDTH)
    return jnp.clip(jax.random.normal(key_base, full_shape, jnp.float32), -4.0, 4.0).astype(jnp.bfloat16)


def plant(result, key, least, top_value):
    place = [jax.random.randint(jax.random.fold_in(key, axis), (), 0, length) for axis, length in enumerate(result.shape)]
    widest = result.shape.index(max(result.shape))
    neighbour = place[:widest] + [(place[widest] + 1) % result.shape[widest]] + place[widest + 1:]
    return result.at[tuple(place)].set(least).at[tuple(neighbour)].set(top_value)


def block_scale(stream_key, extent, cuts, smallest, top_value):
    loudness, own = 1.0, jax.random.fold_in(stream_key, 6)
    for dim, blocks in cuts:
        draws = jnp.exp(jax.random.uniform(jax.random.fold_in(own, dim), (blocks,), jnp.float32, smallest / len(cuts), top_value / len(cuts)))
        loudness = loudness * jnp.repeat(draws, extent[dim] // blocks).reshape([-1 if axis == dim else 1 for axis in range(len(extent))])
    return loudness


def length_profile(amount, total, limit, slope):
    weights = [(1 << 20) // math.isqrt(rank ** slope) + 1 for rank in range(2, amount + 1)]
    spare, given = total - limit - (amount - 1), [1] * (amount - 1)
    while spare > 0:
        candidates = [i for i in range(amount - 1) if given[i] < limit]
        mass, budget = sum([weights[i] for i in candidates]), spare
        for i in candidates:
            addition = min(limit - given[i], max(1, budget * weights[i] // mass), spare)
            given[i] = given[i] + addition
            spare = spare - addition
    return np.array([limit] + given)


def uneven_parts(stream_key, amount, total, bound, skew):
    if amount == 2:
        one = jax.random.randint(stream_key, (), max(1, total - bound), min(bound, total - 1) + 1)
        return jnp.stack([one, total - one])
    tallies = jnp.asarray(length_profile(amount, total, bound, skew), jnp.int32)
    couples = (amount - 1) // 2
    source_of, sink = tallies[1:1 + 2 * couples:2], tallies[2:2 + 2 * couples:2]
    room = jnp.minimum(source_of - 1, bound - sink)
    shifted = jax.random.randint(jax.random.fold_in(stream_key, 1), (couples,), 0, 1 << 20) % (room + 1)
    tallies = tallies.at[1:1 + 2 * couples:2].set(source_of - shifted).at[2:2 + 2 * couples:2].set(sink + shifted)
    return tallies[jax.random.permutation(jax.random.fold_in(stream_key, 2), amount)]


def routed_block(key, own, number, rows, amount, top, reach, lean):
    sequence = jax.random.permutation(key, amount)
    heavy_load, common = portions_of(amount, rows * top, reach, lean, True), portions_of(amount, rows * top, reach, lean, False)
    places = jnp.arange(amount)

    def named(sizes, turn):
        used = int((sizes > 0).sum())
        fixed = max(1, used // 4)
        moved = fixed + (places - fixed + turn * (used - fixed)) % max(1, amount - fixed)
        return jnp.zeros((amount,), jnp.int32).at[sequence[jnp.where(places < fixed, places, moved)]].set(jnp.asarray(sizes, jnp.int32))

    sizes = jnp.where(number % 4 == 0, named(heavy_load, number // 4), named(common, number - number // 4 - 1))
    mixed = jax.random.permutation(jax.random.fold_in(own, 3), amount)
    giver, sink = mixed[0:amount // 2 * 2:2], mixed[1:amount // 2 * 2:2]
    room = jnp.minimum(sizes[giver] - 1, reach - sizes[sink]) // 2
    room = jnp.where((giver == sequence[0]) | (sink == sequence[0]) | (sizes[sink] == 0), 0, jnp.maximum(room, 0))
    moved = jax.random.randint(jax.random.fold_in(own, 4), (amount // 2,), 0, 1 << 20) % (room + 1)
    sizes = sizes.at[giver].add(-moved).at[sink].add(moved)
    items = jnp.searchsorted(jnp.cumsum(sizes), jnp.arange(rows * top), side="right").astype(jnp.int32)
    grid = items.reshape(top, rows).T
    grid = grid[jax.random.permutation(jax.random.fold_in(own, 1), rows)]
    turn = jax.random.randint(jax.random.fold_in(own, 2), (rows, 1), 0, top)
    return jnp.take_along_axis(grid, (jnp.arange(top)[None, :] + turn) % top, axis=1)


def portions_of(number_of, total, most, lean, full):
    portions = [(1 << 20) // math.isqrt(grade ** lean) + 1 for grade in range(1, number_of + 1)]
    largest = most if full else min(most, max(-(-total // number_of), total * portions[0] // sum(portions)))
    least = 1 if total - largest >= number_of - 1 else 0
    counts, rest = [largest] + [least] * (number_of - 1), total - largest - least * (number_of - 1)
    while rest > 0:
        movable = [i for i in range(1, number_of) if counts[i] < largest] or [i for i in range(1, number_of) if counts[i] < most]
        mass, left = sum([portions[i] for i in movable]), rest
        for i in movable:
            extra = min(most - counts[i], max(1, left * portions[i] // mass), rest)
            counts[i] = counts[i] + extra
            rest = rest - extra
    return np.array(counts)


def scatter_about(stream_key, shape, width, bound, cuts=(), kind=jnp.bfloat16):
    entries = width * jax.random.normal(stream_key, shape, jnp.float32)
    if cuts:
        entries = entries * block_scale(stream_key, shape, cuts, -0.22, 0.18)
    return jnp.clip(entries, -bound, bound).astype(kind)


def setup_inputs(seed: int = 0) -> dict:
    arg_keys = jax.random.split(jax.random.key(seed), 18)
    hidden_input = scatter_about(arg_keys[0], (TOKENS, MODEL_WIDTH), 1.0, 6.0, ((0, 16), (1, 8)))
    input_norm_gain = jnp.clip(1.0 + 0.1 * jax.random.normal(arg_keys[1], (MODEL_WIDTH,), jnp.float32), 0.5, 1.5).astype(jnp.bfloat16)
    query_norm_gain = jnp.clip(1.0 + 0.18 * jax.random.normal(arg_keys[2], (HEAD_WIDTH,), jnp.float32), 0.099609375, 1.8984375).astype(jnp.bfloat16)
    key_norm_gain = jnp.clip(1.0 + 0.1 * jax.random.normal(arg_keys[3], (HEAD_WIDTH,), jnp.float32), 0.5, 1.5).astype(jnp.bfloat16)
    query_key_value_weight = scatter_about(arg_keys[4], (MODEL_WIDTH, KEY_VALUE_HEADS * (QUERY_HEADS // KEY_VALUE_HEADS + 2) * HEAD_WIDTH), MODEL_WIDTH ** -0.5, 0.09375, ((0, 16), (1, 8)))
    output_weight = scatter_about(arg_keys[5], (QUERY_HEADS * HEAD_WIDTH, MODEL_WIDTH), (HEAD_WIDTH * QUERY_HEADS // 8) ** -0.5, 0.25, ((0, 16), (1, 8)))
    adapter_down_maps = scatter_about(arg_keys[6], (ADAPTER_COUNT, 2 * ADAPTER_RANK, MODEL_WIDTH), MODEL_WIDTH ** -0.5, 0.09375, ((0, 16),))
    adapter_up_maps = scatter_about(arg_keys[7], (ADAPTER_COUNT, ADAPTER_RANK, KEY_VALUE_HEADS * (QUERY_HEADS // KEY_VALUE_HEADS + 1) * HEAD_WIDTH), ADAPTER_RANK ** -0.5, 1.5, ((0, 16), (2, 8)))
    output_down_maps = scatter_about(arg_keys[8], (ADAPTER_COUNT, ADAPTER_RANK, QUERY_HEADS * HEAD_WIDTH), (HEAD_WIDTH * QUERY_HEADS // 8) ** -0.5, 0.25, ((0, 16), (2, 8)))
    output_up_maps = scatter_about(arg_keys[9], (ADAPTER_COUNT, ADAPTER_RANK, MODEL_WIDTH), ADAPTER_RANK ** -0.5, 1.5, ((0, 16),))
    prompt_adapter = plant(jax.random.randint(arg_keys[10], (PROMPTS,), 0, ADAPTER_COUNT), jax.random.fold_in(arg_keys[10], 1), 0, ADAPTER_COUNT - 1).astype(jnp.int32)
    adapter_position = jax.random.permutation(arg_keys[11], ADAPTER_COUNT).astype(jnp.int32)
    prompt_length = jax.vmap(lambda own: uneven_parts(own, PROMPTS_ROW, TOK_ROW, TOK_ROW // 2, 2))(jax.random.split(arg_keys[12], N_ROW)).reshape((N_ROW, PROMPTS_ROW)).astype(jnp.int32)
    cache_length = draw_cache_length(jax.random.fold_in(arg_keys[17], 71), 0)
    page_owner_row_keys = jax.random.split(jax.random.fold_in(arg_keys[14], 1), (N_ROW * REQ) // REQ)
    page_owner_row_turns = jax.random.permutation(jax.random.fold_in(arg_keys[14], 3), (N_ROW * REQ) // REQ)
    page_owner_row = jax.vmap(lambda own, number: routed_block(jax.random.fold_in(arg_keys[14], 2), own, number, REQ, N_ROW, 1, CAP, 2))(page_owner_row_keys, page_owner_row_turns).reshape((N_ROW * REQ, 1))
    page_store_index = plant(jax.random.randint(arg_keys[15], (N_ROW * REQ,), 0, PAGES_DEV), jax.random.fold_in(arg_keys[15], 1), 0, PAGES_DEV - 1).astype(jnp.int32)
    cache_page_store = draw_cache_page_store(jax.random.fold_in(arg_keys[17], 71), 0)
    return {"hidden_input": hidden_input, "input_norm_gain": input_norm_gain, "query_norm_gain": query_norm_gain, "key_norm_gain": key_norm_gain, "query_key_value_weight": query_key_value_weight, "output_weight": output_weight, "adapter_down_maps": adapter_down_maps, "adapter_up_maps": adapter_up_maps, "output_down_maps": output_down_maps, "output_up_maps": output_up_maps, "prompt_adapter": prompt_adapter, "adapter_position": adapter_position, "prompt_length": prompt_length, "cache_length": cache_length, "page_owner_row": page_owner_row, "page_store_index": page_store_index, "cache_page_store": cache_page_store}


EPSILON = 1e-06
ROPE_BASE = 1000000.0
ADAPTER_SCALE = 0.5

def rms_norm(tensor, gain_vector):
    scale_back = lax.rsqrt(lax.optimization_barrier(jnp.mean(tensor * tensor, axis=-1, keepdims=True)) + EPSILON)
    return tensor * scale_back * gain_vector.astype(jnp.float32)

def rotate(tensor, position):
    half_width = tensor.shape[-1] // 2
    frequency = ROPE_BASE ** (-2.0 * jnp.arange(half_width, dtype=jnp.float32) / tensor.shape[-1])
    angles = position.astype(jnp.float32)[:, None] * frequency[None, :]
    cosine = jnp.cos(angles)[:, None, :]
    sine_part = jnp.sin(angles)[:, None, :]
    front_half = tensor[..., :half_width]
    back_half = tensor[..., half_width:]
    return jnp.concatenate([front_half * cosine - back_half * sine_part, back_half * cosine + front_half * sine_part], axis=-1)

def token_meta(lengths, cached, token_count):
    end_index = jnp.cumsum(lengths, dtype=jnp.int32)
    starts = end_index - lengths
    token_index = jnp.arange(token_count, dtype=jnp.int32)
    prompt_id = lax.optimization_barrier(jnp.sum((token_index[:, None] >= end_index[None, :]).astype(jnp.int32), axis=1, dtype=jnp.int32))
    onehot = prompt_id[:, None] == jnp.arange(lengths.shape[0], dtype=jnp.int32)[None, :]
    start_at = lax.optimization_barrier(jnp.sum(jnp.where(onehot, starts[None, :], 0), axis=1, dtype=jnp.int32))
    prefix = lax.optimization_barrier(jnp.sum(jnp.where(onehot, cached[None, :], 0), axis=1, dtype=jnp.int32))
    return (prompt_id, (prefix + token_index - start_at).astype(jnp.int32), onehot)

def cache_meta(cached, requests, page_size):
    pages_each = WIN // page_size
    has_cache = (cached > 0).astype(jnp.int32)
    order_rank = jnp.cumsum(has_cache, dtype=jnp.int32) - 1
    prompt_ids = jnp.arange(cached.shape[0], dtype=jnp.int32)
    request_ids = jnp.arange(requests, dtype=jnp.int32)
    owns_request = (has_cache[None, :] > 0) & (order_rank[None, :] == (request_ids // pages_each)[:, None])
    owners = lax.optimization_barrier(jnp.sum(jnp.where(owns_request, prompt_ids[None, :], 0), axis=1, dtype=jnp.int32))
    owner_len = lax.optimization_barrier(jnp.sum(jnp.where(owns_request, cached[None, :], 0), axis=1, dtype=jnp.int32))
    within = jnp.arange(page_size, dtype=jnp.int32)
    key_pos = (request_ids % pages_each * page_size)[:, None] + within[None, :]
    key_prompt = jnp.broadcast_to(owners[:, None], (requests, page_size)).reshape(-1)
    key_valid = key_pos < owner_len[:, None]
    return (key_prompt, key_pos.reshape(-1), key_valid.reshape(-1))

def attend(queries, key_rows, values, query_prompt, query_pos, key_prompt, key_pos, key_valid):
    scores = lax.dot_general(queries, key_rows, (((1,), (1,)), ((), ())), preferred_element_type=jnp.float32)
    scores = scores / math.sqrt(queries.shape[-1])
    visible = (key_prompt[None, :] == query_prompt[:, None]) & (key_pos[None, :] <= query_pos[:, None]) & key_valid[None, :]
    visible = visible & ((key_pos[None, :] < SINKS) | (key_pos[None, :] > query_pos[:, None] - WIN))
    scores = jnp.where(visible, scores, -jnp.inf)
    row_max = lax.optimization_barrier(jnp.max(scores, axis=1, keepdims=True))
    weights = jnp.exp(scores - row_max)
    weights = (weights / lax.optimization_barrier(jnp.sum(weights, axis=1, keepdims=True))).astype(jnp.bfloat16)
    return jnp.dot(weights, values, preferred_element_type=jnp.float32).astype(jnp.bfloat16)

def attend_group(queries, keys_new, values_new, prompt_id, position, cached, fetched):
    token_count, group_count, group_width, head_size = queries.shape
    requests = fetched.shape[0]
    page_size = fetched.shape[2]
    key_prompt_c, key_pos_c, key_valid_c = cache_meta(cached, requests, page_size)
    key_prompt = jnp.concatenate([prompt_id, key_prompt_c])
    key_pos = jnp.concatenate([position, key_pos_c])
    key_valid = jnp.concatenate([jnp.ones((token_count,), jnp.bool_), key_valid_c])
    cache_keys = fetched[:, 0].reshape(requests * page_size, group_count, head_size)
    cache_values = fetched[:, 1].reshape(requests * page_size, group_count, head_size)
    keys_all = jnp.concatenate([keys_new, cache_keys], axis=0)
    values_all = jnp.concatenate([values_new, cache_values], axis=0)
    row_count = token_count * group_width
    block_rows = min(512, row_count)
    query_prompt = jnp.repeat(prompt_id, group_width).reshape(-1, block_rows)
    query_pos = jnp.repeat(position, group_width).reshape(-1, block_rows)
    outputs = []
    for group_index in range(group_count):
        query_blocks = queries[:, group_index].reshape(-1, block_rows, head_size)
        group_keys = keys_all[:, group_index]
        group_values = values_all[:, group_index]

        def one_block(block_items):
            return attend(block_items[0], group_keys, group_values, block_items[1], block_items[2], key_prompt, key_pos, key_valid)
        outputs.append(lax.map(one_block, (query_blocks, query_prompt, query_pos)).reshape(token_count, group_width, head_size))
    return jnp.stack(outputs, axis=1)

def adapter_change(normalized, selector, adapter_down_maps, adapter_up_maps, group_width):
    adapter_list, twice_rank, feature_total = adapter_down_maps.shape
    rank_width = twice_rank // 2
    rank_features = lax.dot_general(normalized, adapter_down_maps.reshape(adapter_list * twice_rank, feature_total), (((1,), (1,)), ((), ())), preferred_element_type=jnp.float32)
    rank_features = rank_features.reshape(-1, adapter_list, 2, rank_width)
    rank_features = jnp.where(selector[:, :, None, None], rank_features, 0.0).astype(jnp.bfloat16)
    group_count = adapter_up_maps.shape[2] // ((group_width + 1) * HEAD_WIDTH)
    up_pieces = adapter_up_maps.reshape(adapter_list, rank_width, group_count, group_width + 1, HEAD_WIDTH)
    up_query = up_pieces[:, :, :, :group_width, :].reshape(adapter_list * rank_width, group_count * group_width * HEAD_WIDTH)
    up_value = up_pieces[:, :, :, group_width, :].reshape(adapter_list * rank_width, group_count * HEAD_WIDTH)
    query_change = jnp.dot(rank_features[:, :, 0, :].reshape(-1, adapter_list * rank_width), up_query, preferred_element_type=jnp.float32)
    value_change = jnp.dot(rank_features[:, :, 1, :].reshape(-1, adapter_list * rank_width), up_value, preferred_element_type=jnp.float32)
    return (query_change.reshape(-1, group_count, group_width, HEAD_WIDTH), value_change.reshape(-1, group_count, HEAD_WIDTH))

def project_heads(base_out, query_change, value_change, query_norm_gain, key_norm_gain, position, group_width):
    token_count = base_out.shape[0]
    group_count = base_out.shape[1] // ((group_width + 2) * HEAD_WIDTH)
    column_list = base_out.reshape(token_count, group_count, group_width + 2, HEAD_WIDTH)
    unrotated_query = column_list[:, :, :group_width, :] + ADAPTER_SCALE * query_change
    raw_key = column_list[:, :, group_width, :]
    unnormed_value = column_list[:, :, group_width + 1, :] + ADAPTER_SCALE * value_change
    queries = rotate(rms_norm(unrotated_query, query_norm_gain).reshape(token_count, group_count * group_width, HEAD_WIDTH), position)
    queries = queries.astype(jnp.bfloat16).reshape(token_count, group_count, group_width, HEAD_WIDTH)
    keys_new = rotate(rms_norm(raw_key, key_norm_gain), position).astype(jnp.bfloat16)
    values_new = unnormed_value.astype(jnp.bfloat16)
    return (queries, keys_new, values_new)

def output_change(attention_output, selector, output_down_maps, output_up_maps):
    adapter_list, rank_width, head_columns = output_down_maps.shape
    reduced_sum = lax.dot_general(attention_output, output_down_maps.reshape(adapter_list * rank_width, head_columns), (((1,), (1,)), ((), ())), preferred_element_type=jnp.float32)
    reduced_sum = jnp.where(selector[:, :, None], reduced_sum.reshape(-1, adapter_list, rank_width), 0.0).reshape(-1, adapter_list * rank_width)
    return jnp.dot(reduced_sum, output_up_maps.reshape(adapter_list * rank_width, -1).astype(jnp.float32), precision=lax.Precision.HIGHEST)

def reference(hidden_input, input_norm_gain, query_norm_gain, key_norm_gain, query_key_value_weight, output_weight, adapter_down_maps, adapter_up_maps, output_down_maps, output_up_maps, prompt_adapter, adapter_position, prompt_length, cache_length, page_owner_row, page_store_index, cache_page_store):
    group_width = QUERY_HEADS // KEY_VALUE_HEADS
    tokens_all = hidden_input.shape[0]
    adapter_list = adapter_down_maps.shape[0]
    residual_input = hidden_input.astype(jnp.float32)
    normalized = rms_norm(residual_input, input_norm_gain).astype(jnp.bfloat16)
    base_out = jnp.dot(normalized, query_key_value_weight, preferred_element_type=jnp.float32)
    cached_rows = cache_length.reshape(N_ROW, PROMPTS_ROW)
    prompt_id, position, onehot = jax.vmap(lambda lengths, cached: token_meta(lengths, cached, TOK_ROW))(prompt_length, cached_rows)
    adapter_rows = prompt_adapter.reshape(N_ROW, PROMPTS_ROW)
    adapter_ids = jnp.arange(adapter_list, dtype=jnp.int32)
    slot_prompt = lax.optimization_barrier(jnp.sum(jnp.where(adapter_rows[:, :, None] == adapter_ids[None, None, :], adapter_position[None, None, :], 0), axis=2, dtype=jnp.int32))
    slot_token = lax.optimization_barrier(jnp.sum(jnp.where(onehot, slot_prompt[:, None, :], 0), axis=2, dtype=jnp.int32)).reshape(tokens_all)
    selector = slot_token[:, None] == adapter_ids[None, :]
    query_change, value_change = adapter_change(normalized, selector, adapter_down_maps, adapter_up_maps, group_width)
    queries, keys_new, values_new = project_heads(base_out, query_change, value_change, query_norm_gain, key_norm_gain, position.reshape(tokens_all), group_width)
    new_cache = jnp.stack([keys_new.reshape(tokens_all, KEY_VALUE_HEADS * HEAD_WIDTH), values_new.reshape(tokens_all, KEY_VALUE_HEADS * HEAD_WIDTH)])
    holders = page_owner_row.reshape(N_ROW, REQ)
    slot_ids = page_store_index.reshape(N_ROW, REQ)

    def one_group(group_items):
        group_queries, group_keys, group_values, group_prompt, group_pos, group_cached, group_holders, group_slots = group_items
        fetched = jnp.take(cache_page_store, group_holders * PAGES_DEV + group_slots, axis=0)
        return attend_group(group_queries, group_keys, group_values, group_prompt, group_pos, group_cached, fetched)
    attention_output = lax.map(one_group, (queries.reshape(N_ROW, TOK_ROW, KEY_VALUE_HEADS, group_width, HEAD_WIDTH), keys_new.reshape(N_ROW, TOK_ROW, KEY_VALUE_HEADS, HEAD_WIDTH), values_new.reshape(N_ROW, TOK_ROW, KEY_VALUE_HEADS, HEAD_WIDTH), prompt_id, position, cached_rows, holders, slot_ids))
    attention_output = attention_output.reshape(tokens_all, QUERY_HEADS * HEAD_WIDTH)
    projected_rows = jnp.dot(attention_output, output_weight, preferred_element_type=jnp.float32)
    adapter_output = output_change(attention_output, selector, output_down_maps, output_up_maps)
    hidden_output = (residual_input + projected_rows + ADAPTER_SCALE * adapter_output).astype(jnp.bfloat16)
    return (hidden_output, new_cache)
```

```python
import math

import jax
import jax.numpy as jnp
import numpy as np
from jax import lax
from jax.experimental import pallas as pl
from jax.experimental.pallas import tpu as pltpu
from jax.sharding import PartitionSpec as P

HEAD = 128
GROUP = 4
WIN = 1024
SINKS = 4
PAGE = 128
EPSILON = 1e-06
ROPE_BASE = 1000000.0
TOK = 512
FEAT = 512
PROMPTS = 4
BF = jnp.bfloat16
F32 = jnp.float32
NEG = -1e30


def perm_x(k):
    return [(i, (i // 4 + k) % 4 * 4 + i % 4) for i in range(16)]


def perm_y(k):
    return [(i, i // 4 * 4 + (i % 4 + k) % 4) for i in range(16)]


def perm_z(k):
    return [(i, (i // 2 + k) % 4 * 2 + i % 2) for i in range(8)]


SWAP = [(i, i ^ 1) for i in range(8)]


def ring4(block, axis, perm, half):
    before = lax.ppermute(block, axis, perm(1))
    after = lax.ppermute(block, axis, perm(-1))
    far_low = lax.ppermute(before[:half], axis, perm(1))
    far_high = lax.ppermute(after[half:], axis, perm(-1))
    return before, after, jnp.concatenate([far_low, far_high], axis=0)


def gather_col(block, half):
    other = lax.ppermute(block, "col", SWAP)
    out = [block, other]
    for piece in ring4(block, "col", perm_z, half):
        out += [piece, lax.ppermute(piece, "col", SWAP)]
    return out


def col_order():
    me = lax.axis_index("col")
    chip, core = me // 2, me % 2
    return jnp.stack([(chip + d) % 4 * 2 + (core + s) % 2 for d in (0, 3, 1, 2) for s in (0, 1)]).astype(jnp.int32)


def vmem(n):
    return pltpu.CompilerParams(vmem_limit_bytes=n << 20)


def whole(*shape):
    return pl.BlockSpec(shape, lambda *_: (0,) * len(shape))


def pick_body(index_ref, store_ref, out_ref, sems):
    copies = [
        pltpu.make_async_copy(store_ref.at[index_ref[i]], out_ref.at[i], sems.at[i])
        for i in range(out_ref.shape[0])
    ]
    for copy in copies:
        copy.start()
    for copy in copies:
        copy.wait()


def pick_pages(store, index):
    count = index.shape[0]
    return pl.pallas_call(
        pick_body,
        out_shape=jax.ShapeDtypeStruct((count,) + store.shape[1:], store.dtype),
        grid_spec=pltpu.PrefetchScalarGridSpec(
            num_scalar_prefetch=1,
            grid=(1,),
            in_specs=[pl.BlockSpec(memory_space=pl.ANY)],
            out_specs=pl.BlockSpec(memory_space=pl.ANY),
            scratch_shapes=[pltpu.SemaphoreType.DMA((count,))],
        ),
        name="pick_pages",
    )(index, store)


def select_body(sx_ref, sy_ref, y0, y1, y2, y3, maps_ref, up_ref, oup_ref):
    up_ref[...] = jnp.zeros_like(up_ref)
    for p in range(PROMPTS):
        for k, ref in enumerate((y0, y1, y2, y3)):

            @pl.when(sy_ref[p] == k)
            def _():
                x = sx_ref[p]
                maps_ref[p * 32 : p * 32 + 32, :] = ref[x, 0:32, :FEAT]
                maps_ref[128 + p * 16 : 128 + p * 16 + 16, :] = ref[x, 48:64, :FEAT]
                up_ref[p * 32 : p * 32 + 16, :512] = ref[x, 32:48, :512]
                up_ref[p * 32 + 16 : p * 32 + 32, 512:] = ref[x, 32:48, 512:]
                oup_ref[p * 16 : p * 16 + 16, :] = ref[x, 64:80, :FEAT]


def select_slots(sx, sy, pieces):
    return pl.pallas_call(
        select_body,
        out_shape=(
            jax.ShapeDtypeStruct((192, FEAT), BF),
            jax.ShapeDtypeStruct((128, 640), BF),
            jax.ShapeDtypeStruct((64, FEAT), BF),
        ),
        grid_spec=pltpu.PrefetchScalarGridSpec(
            num_scalar_prefetch=2,
            grid=(1,),
            in_specs=[whole(4, 80, 640)] * 4,
            out_specs=(whole(192, FEAT), whole(128, 640), whole(64, FEAT)),
        ),
        name="select_slots",
    )(sx, sy, *pieces)


def norm_body(order_ref, *refs):
    blocks, maps = refs[:8], refs[8:16]
    gain_ref, prompt_ref, normed_ref, low_ref = refs[16:]
    values = [b[...].astype(F32) for b in blocks]
    total = sum(jnp.sum(v * v, axis=-1, keepdims=True) for v in values)
    scale = lax.rsqrt(total * (1.0 / (8 * FEAT)) + EPSILON)
    low = jnp.zeros(low_ref.shape, F32)
    for b in range(8):
        gain = gain_ref[pl.ds(order_ref[b], 1), :]
        normed = (values[b] * scale * gain).astype(BF)
        normed_ref[order_ref[b]] = normed
        low += lax.dot_general(normed, maps[b][:128, :], (((1,), (1,)), ((), ())), preferred_element_type=F32)
    mine = lax.broadcasted_iota(jnp.int32, low.shape, 1) // 32 == prompt_ref[...]
    low_ref[...] = jnp.where(mine, low, 0.0).astype(BF)


def norm_low(order, blocks, maps, gain, prompt):
    rows = 128
    return pl.pallas_call(
        norm_body,
        out_shape=(jax.ShapeDtypeStruct((8, TOK, FEAT), BF), jax.ShapeDtypeStruct((TOK, 128), BF)),
        grid_spec=pltpu.PrefetchScalarGridSpec(
            num_scalar_prefetch=1,
            grid=(TOK // rows,),
            in_specs=[pl.BlockSpec((rows, FEAT), lambda i, o: (i, 0))] * 8
            + [whole(192, FEAT)] * 8
            + [whole(8, FEAT), pl.BlockSpec((rows, 1), lambda i, o: (i, 0))],
            out_specs=(
                pl.BlockSpec((8, rows, FEAT), lambda i, o: (0, i, 0)),
                pl.BlockSpec((rows, 128), lambda i, o: (i, 0)),
            ),
        ),
        compiler_params=vmem(32),
        name="norm_low",
    )(order, *blocks, *maps, gain, prompt)


def qkv_body(normed_ref, w_ref, low_ref, up_ref, cos_ref, sin_ref, qg_ref, kg_ref, q_ref, kv_ref, acc):
    step = pl.program_id(0)
    part = jnp.dot(normed_ref[0], w_ref[...], preferred_element_type=F32)

    @pl.when(step == 0)
    def _():
        acc[...] = part

    @pl.when(step > 0)
    def _():
        acc[...] += part

    @pl.when(step == pl.num_programs(0) - 1)
    def _():
        change = 0.5 * jnp.dot(low_ref[...], up_ref[...], preferred_element_type=F32)
        cos, sin = cos_ref[...], sin_ref[...]

        def finish(raw, gain):
            scale = lax.rsqrt(jnp.mean(raw * raw, axis=-1, keepdims=True) + EPSILON)
            x = raw * scale * gain
            return (x * cos + pltpu.roll(x, HEAD // 2, 1) * sin).astype(BF)

        for h in range(GROUP):
            cut = slice(h * HEAD, (h + 1) * HEAD)
            q_ref[h] = finish(acc[:, cut] + change[:, cut], qg_ref[...])
        kv_ref[0] = finish(acc[:, 512:640], kg_ref[...])
        kv_ref[1] = (acc[:, 640:768] + change[:, 512:640]).astype(BF)


def project(normed, weight, low, up, cos, sin, q_gain, k_gain):
    return pl.pallas_call(
        qkv_body,
        out_shape=(jax.ShapeDtypeStruct((GROUP, TOK, HEAD), BF), jax.ShapeDtypeStruct((2, TOK, HEAD), BF)),
        grid=(8,),
        in_specs=[
            pl.BlockSpec((1, TOK, FEAT), lambda k: (k, 0, 0)),
            pl.BlockSpec((FEAT, 768), lambda k: (k, 0)),
            whole(TOK, 128),
            whole(128, 640),
            whole(TOK, HEAD),
            whole(TOK, HEAD),
            whole(1, HEAD),
            whole(1, HEAD),
        ],
        out_specs=(whole(GROUP, TOK, HEAD), whole(2, TOK, HEAD)),
        scratch_shapes=[pltpu.VMEM((TOK, 768), F32)],
        compiler_params=vmem(32),
        name="project",
    )(normed, weight, low, up, cos, sin, q_gain, k_gain)


BLOCK = 64
SCALE2 = math.log2(math.e) / math.sqrt(HEAD)


def attend_body(page_ref, need_ref, length_ref, q_ref, kv_ref, pages_ref, begin_ref, own_ref, pos_ref, out_ref, m_ref, l_ref, acc_ref):
    rows = GROUP * BLOCK
    for t in range(TOK // BLOCK):
        lo, hi = max(0, t * BLOCK - 256), (t + 1) * BLOCK
        cut = slice(t * BLOCK, hi)
        q = q_ref[:, cut, :].reshape(rows, HEAD)
        s = lax.dot_general(q, kv_ref[0, lo:hi, :], (((1,), (1,)), ((), ())), preferred_element_type=F32)
        key = lo + lax.broadcasted_iota(jnp.int32, (BLOCK, hi - lo), 1)
        token = t * BLOCK + lax.broadcasted_iota(jnp.int32, (BLOCK, hi - lo), 0)
        seen = (key <= token) & (key >= begin_ref[cut, :])
        s = jnp.where(seen[None], s.reshape(GROUP, BLOCK, hi - lo), NEG).reshape(rows, hi - lo)
        m = jnp.max(s, axis=1, keepdims=True)
        w = jnp.exp2((s - m) * SCALE2)
        m_ref[...] = m
        l_ref[...] = jnp.sum(w, axis=1, keepdims=True)
        acc_ref[...] = jnp.dot(w.astype(BF), kv_ref[1, lo:hi, :], preferred_element_type=F32)
        for j in range(2):

            @pl.when(need_ref[t * 2 + j] > 0)
            def _():
                mine = own_ref[cut, :] == j
                least = jnp.where(mine, pos_ref[cut, :] - WIN, 1 << 30)
                sink = jnp.where(mine, SINKS, 0)
                pieces = []
                for k in range(8):
                    page = page_ref[j * 8 + k]
                    c = lax.dot_general(q, pages_ref[page, 0], (((1,), (1,)), ((), ())), preferred_element_type=F32)
                    at = k * PAGE + lax.broadcasted_iota(jnp.int32, (BLOCK, PAGE), 1)
                    ok = at > least
                    if k == 0:
                        ok = ok | (at < sink)
                    ok = ok & (at < length_ref[j])
                    pieces.append(jnp.where(ok[None], c.reshape(GROUP, BLOCK, PAGE), NEG).reshape(rows, PAGE))
                top = pieces[0]
                for c in pieces[1:]:
                    top = jnp.maximum(top, c)
                m_old = m_ref[...]
                m_new = jnp.maximum(m_old, jnp.max(top, axis=1, keepdims=True))
                fade = jnp.exp2((m_old - m_new) * SCALE2)
                total = jnp.zeros((rows, PAGE), F32)
                acc = acc_ref[...] * fade
                for k in range(8):
                    page = page_ref[j * 8 + k]
                    w = jnp.exp2((pieces[k] - m_new) * SCALE2)
                    total += w
                    acc += jnp.dot(w.astype(BF), pages_ref[page, 1], preferred_element_type=F32)
                m_ref[...] = m_new
                l_ref[...] = l_ref[...] * fade + jnp.sum(total, axis=1, keepdims=True)
                acc_ref[...] = acc

        done = (acc_ref[...] * (1.0 / l_ref[...])).astype(BF)
        for h in range(GROUP):
            out_ref[cut, h * HEAD : (h + 1) * HEAD] = done[h * BLOCK : (h + 1) * BLOCK, :]


def attention(page, need, length, q, kv, pages, begin, own, pos):
    rows = GROUP * BLOCK
    return pl.pallas_call(
        attend_body,
        out_shape=jax.ShapeDtypeStruct((TOK, FEAT), BF),
        grid_spec=pltpu.PrefetchScalarGridSpec(
            num_scalar_prefetch=3,
            grid=(1,),
            in_specs=[
                whole(GROUP, TOK, HEAD),
                whole(2, TOK, HEAD),
                whole(32, 2, PAGE, HEAD),
                whole(TOK, 1),
                whole(TOK, 1),
                whole(TOK, 1),
            ],
            out_specs=whole(TOK, FEAT),
            scratch_shapes=[pltpu.VMEM((rows, 1), F32), pltpu.VMEM((rows, 1), F32), pltpu.VMEM((rows, HEAD), F32)],
        ),
        compiler_params=vmem(32),
        name="attention",
    )(page, need, length, q, kv, pages, begin, own, pos)


def out_body(order_ref, *refs):
    blocks, maps = refs[:8], refs[8:16]
    w_ref, oup_ref, prompt_ref, hidden_ref, out_ref = refs[16:]
    total = hidden_ref[...].astype(F32)
    low = jnp.zeros((total.shape[0], 64), F32)
    for b in range(8):
        x = blocks[b][...]
        total += jnp.dot(x, w_ref[order_ref[b]], preferred_element_type=F32)
        low += lax.dot_general(x, maps[b][128:192, :], (((1,), (1,)), ((), ())), preferred_element_type=F32)
    mine = lax.broadcasted_iota(jnp.int32, low.shape, 1) // 16 == prompt_ref[...]
    low = jnp.where(mine, low, 0.0)
    change = jnp.dot(low, oup_ref[...].astype(F32), precision=lax.Precision.HIGHEST, preferred_element_type=F32)
    out_ref[...] = (total + 0.5 * change).astype(BF)


def output(order, blocks, maps, weight, oup, prompt, hidden):
    rows = 128
    tok = pl.BlockSpec((rows, FEAT), lambda i, o: (i, 0))
    return pl.pallas_call(
        out_body,
        out_shape=jax.ShapeDtypeStruct((TOK, FEAT), BF),
        grid_spec=pltpu.PrefetchScalarGridSpec(
            num_scalar_prefetch=1,
            grid=(TOK // rows,),
            in_specs=[tok] * 8
            + [whole(192, FEAT)] * 8
            + [whole(8, FEAT, FEAT), whole(64, FEAT), pl.BlockSpec((rows, 1), lambda i, o: (i, 0)), tok],
            out_specs=tok,
        ),
        compiler_params=vmem(40),
        name="output",
    )(order, *blocks, *maps, weight, oup, prompt, hidden)


def token_tables(lengths, cached):
    ends = [lengths[0]]
    for p in range(1, PROMPTS):
        ends.append(ends[-1] + lengths[p])
    has = [(cached[p] > 0).astype(jnp.int32) for p in range(PROMPTS)]
    rank, count = [], jnp.int32(0)
    for p in range(PROMPTS):
        rank.append(jnp.where(has[p] > 0, count, -1))
        count = count + has[p]
    token = lax.broadcasted_iota(jnp.int32, (TOK, 1), 0)
    prompt = sum((token >= ends[p]).astype(jnp.int32) for p in range(PROMPTS))
    begin = jnp.zeros_like(token)
    prefix = jnp.zeros_like(token)
    own = jnp.full_like(token, -1)
    for p in range(PROMPTS):
        hit = prompt == p
        begin = jnp.where(hit, ends[p] - lengths[p], begin)
        prefix = jnp.where(hit, cached[p], prefix)
        own = jnp.where(hit, rank[p], own)
    need, used = [], []
    first = jnp.arange(TOK // BLOCK, dtype=jnp.int32) * BLOCK
    for j in range(2):
        start = sum(jnp.where(rank[p] == j, ends[p] - lengths[p], 0) for p in range(PROMPTS))
        end = sum(jnp.where(rank[p] == j, ends[p], 0) for p in range(PROMPTS))
        used.append(sum(jnp.where(rank[p] == j, cached[p], 0) for p in range(PROMPTS)))
        need.append(((start < first + BLOCK) & (end > first)).astype(jnp.int32))
    return prompt, begin, prefix + token - begin, own, jnp.stack(need, axis=1).reshape(-1), jnp.stack(used)


def page_tables(owner_row, store_index):
    me = lax.axis_index("row")
    owner = owner_row.reshape(16, 16)
    store = store_index.reshape(16, 16)
    same = (owner[:, :, None] == owner[:, None, :]) & (
        jnp.arange(16)[None, None, :] < jnp.arange(16)[None, :, None]
    )
    rank = jnp.sum(same.astype(jnp.int32), axis=2)
    out = jnp.stack(
        [jnp.sum(jnp.where((owner == me) & (rank == s), store, 0), axis=1) for s in range(2)], axis=1
    ).reshape(32)
    mine = jnp.arange(16)[:, None] == me
    place = jnp.sum(jnp.where(mine, owner * 2 + rank, 0), axis=0)
    return out.astype(jnp.int32), place.astype(jnp.int32)


def on_device(
    hidden_input,
    input_norm_gain,
    query_norm_gain,
    key_norm_gain,
    query_key_value_weight,
    output_weight,
    adapter_down_maps,
    adapter_up_maps,
    output_down_maps,
    output_up_maps,
    prompt_adapter,
    adapter_position,
    prompt_length,
    cache_length,
    page_owner_row,
    page_store_index,
    cache_page_store,
):
    row, col = lax.axis_index("row"), lax.axis_index("col")
    weight = lax.all_gather(query_key_value_weight, "row", axis=0, tiled=True)

    going, place = page_tables(page_owner_row, page_store_index)
    sent = pick_pages(cache_page_store, going).reshape(16, 2 * 2 * PAGE, HEAD)
    pages = lax.all_to_all(sent, "row", 0, 0).reshape(32, 2, PAGE, HEAD)

    order = col_order()
    blocks = gather_col(hidden_input, 256)

    def wide(x):
        return jnp.pad(x, ((0, 0), (0, 640 - x.shape[1])))

    small = jnp.concatenate(
        [
            wide(lax.dynamic_slice(adapter_down_maps[0], (0, col * FEAT), (32, FEAT))),
            adapter_up_maps[0],
            wide(output_down_maps[0]),
            wide(lax.dynamic_slice(output_up_maps[0], (0, col * FEAT), (16, FEAT))),
        ],
        axis=0,
    )
    along_x = jnp.concatenate([small, *ring4(small, "row", perm_x, 48)], axis=0)
    pieces = [p.reshape(4, 80, 640) for p in (along_x, *ring4(along_x, "row", perm_y, 160))]
    adapter_ids = jnp.arange(16, dtype=jnp.int32)
    slot = jnp.sum(jnp.where(prompt_adapter[:, None] == adapter_ids[None, :], adapter_position[None, :], 0), axis=1)

    def turn(d):
        d = d % 4
        return jnp.where(d == 0, 0, jnp.where(d == 3, 1, jnp.where(d == 1, 2, 3))).astype(jnp.int32)

    maps, up, oup = select_slots(turn(slot // 4 - row // 4 + 4), turn(slot % 4 - row % 4 + 4), pieces)
    maps = gather_col(maps, 96)

    prompt, begin, position, own, need, used = token_tables(prompt_length[0], cache_length)
    frequency = ROPE_BASE ** (-2.0 * jnp.arange(HEAD // 2, dtype=F32) / HEAD)
    angles = position.astype(F32) * frequency[None, :]
    cos, sin = jnp.cos(angles), jnp.sin(angles)
    cos = jnp.concatenate([cos, cos], axis=1)
    sin = jnp.concatenate([-sin, sin], axis=1)

    normed, low = norm_low(order, blocks, maps, input_norm_gain.astype(F32).reshape(8, FEAT), prompt)
    weight, later = lax.optimization_barrier((weight, output_weight))
    out_weight = lax.all_gather(later, "row", axis=0, tiled=True)
    q, new_cache = project(
        normed,
        weight,
        low,
        up,
        cos,
        sin,
        query_norm_gain.astype(F32)[None, :],
        key_norm_gain.astype(F32)[None, :],
    )
    attended = attention(place, need, used, q, new_cache, pages, begin, own, position)
    attended = gather_col(attended, 256)
    hidden_output = output(order, attended, maps, out_weight.reshape(8, FEAT, FEAT), oup, prompt, hidden_input)
    return hidden_output, new_cache


def solution(mesh):
    return jax.shard_map(
        on_device,
        mesh=mesh,
        in_specs=(
            P("row", "col"),
            P(),
            P(),
            P(),
            P("row", "col"),
            P("row", "col"),
            P("row", None, None),
            P("row", None, "col"),
            P("row", None, "col"),
            P("row", None, None),
            P("row"),
            P(),
            P("row", None),
            P("row"),
            P(),
            P(),
            P("row", None, None, "col"),
        ),
        out_specs=(P("row", "col"), P(None, "row", "col")),
        check_vma=False,
    )
```

```python
import math

import jax
import jax.numpy as jnp
from jax import lax
from jax.experimental import pallas as pl
from jax.experimental.pallas import tpu as pltpu
from jax.sharding import PartitionSpec as P

HEAD = 128
GROUP = 4
WIN = 1024
SINKS = 4
PAGE = 128
EPSILON = 1e-06
ROPE_BASE = 1000000.0
TOK = 512
FEAT = 512
PROMPTS = 4
BF = jnp.bfloat16
F32 = jnp.float32
NEG = -1e30


def perm_x(k):
    return [(i, (i // 4 + k) % 4 * 4 + i % 4) for i in range(16)]


def perm_y(k):
    return [(i, i // 4 * 4 + (i % 4 + k) % 4) for i in range(16)]


def perm_z(k):
    return [(i, (i // 2 + k) % 4 * 2 + i % 2) for i in range(8)]


SWAP = [(i, i ^ 1) for i in range(8)]


def ring4(block, axis, perm, half):
    before = lax.ppermute(block, axis, perm(1))
    after = lax.ppermute(block, axis, perm(-1))
    far_low = lax.ppermute(before[:half], axis, perm(1))
    far_high = lax.ppermute(after[half:], axis, perm(-1))
    return before, after, jnp.concatenate([far_low, far_high], axis=0)


def gather_col(block, half):
    other = lax.ppermute(block, "col", SWAP)
    out = [block, other]
    for piece in ring4(block, "col", perm_z, half):
        out += [piece, lax.ppermute(piece, "col", SWAP)]
    return out


def col_order(col):
    chip, core = col // 2, col % 2
    return [lax.rem(chip + d, 4) * 2 + lax.rem(core + s, 2) for d in (0, 3, 1, 2) for s in (0, 1)]


def prompt_rows(length_ref):
    start, rows = jnp.int32(0), []
    for p in range(PROMPTS):
        rows.append((start, start + length_ref[0, p]))
        start = start + length_ref[0, p]
    return rows


def per_token(rows, values, token, default=0):
    out = jnp.full(token.shape, default, jnp.int32)
    for (start, end), value in zip(rows, values):
        out = jnp.where((token >= start) & (token < end), value, out)
    return out


def in_hbm(x):
    return pltpu.with_memory_space_constraint(x, pltpu.HBM)


def vmem(n):
    return pltpu.CompilerParams(vmem_limit_bytes=n << 20)


def whole(*shape):
    return pl.BlockSpec(shape, lambda *_: (0,) * len(shape))


def pick_body(me_ref, owner_ref, index_ref, store_ref, out_ref):
    def group(r, carry):
        first, second, count = jnp.int32(0), jnp.int32(0), jnp.int32(0)
        for q in range(16):
            hit = owner_ref[r * 16 + q, 0] == me_ref[0]
            index = index_ref[r * 16 + q]
            first = jnp.where(hit & (count == 0), index, first)
            second = jnp.where(hit & (count == 1), index, second)
            count = count + hit.astype(jnp.int32)
        out_ref[r, 0] = store_ref[first]
        out_ref[r, 1] = store_ref[second]
        return carry

    lax.fori_loop(0, 16, group, 0)


def pick_pages(me, owner, index, store):
    return pl.pallas_call(
        pick_body,
        out_shape=jax.ShapeDtypeStruct((16, 2) + store.shape[1:], store.dtype),
        grid_spec=pltpu.PrefetchScalarGridSpec(
            num_scalar_prefetch=3,
            grid=(1,),
            in_specs=[whole(*store.shape)],
            out_specs=whole(16, 2, *store.shape[1:]),
        ),
        compiler_params=vmem(10),
        name="pick_pages",
    )(me, owner, index, store)


def pack_body(me_ref, down_ref, up_ref, odown_ref, oup_ref, out_ref):
    piece = jnp.zeros((80, 640), BF)
    out_ref[0] = piece
    out_ref[0, 0:32, :FEAT] = down_ref[0]
    out_ref[0, 32:48, :] = up_ref[0]
    out_ref[0, 48:64, :FEAT] = odown_ref[0]
    out_ref[0, 64:80, :FEAT] = oup_ref[0]
    for r in range(1, 16):
        out_ref[r] = out_ref[0]


def pack_slots(me, down, up, odown, oup):
    return pl.pallas_call(
        pack_body,
        out_shape=jax.ShapeDtypeStruct((16, 80, 640), BF),
        grid_spec=pltpu.PrefetchScalarGridSpec(
            num_scalar_prefetch=1,
            grid=(1,),
            in_specs=[
                pl.BlockSpec((1, 32, FEAT), lambda i, me: (0, 0, me[1])),
                whole(1, 16, 640),
                whole(1, 16, FEAT),
                pl.BlockSpec((1, 16, FEAT), lambda i, me: (0, 0, me[1])),
            ],
            out_specs=whole(16, 80, 640),
        ),
        name="pack_slots",
    )(me, down, up, odown, oup)


def select_body(adapter_ref, position_ref, slots_ref, maps_ref, up_ref, oup_ref):
    up_ref[...] = jnp.zeros_like(up_ref)
    for p in range(PROMPTS):
        slot = position_ref[adapter_ref[p]]
        maps_ref[p * 32 : p * 32 + 32, :] = slots_ref[slot, 0:32, :FEAT]
        maps_ref[128 + p * 16 : 128 + p * 16 + 16, :] = slots_ref[slot, 48:64, :FEAT]
        up_ref[p * 32 : p * 32 + 16, :512] = slots_ref[slot, 32:48, :512]
        up_ref[p * 32 + 16 : p * 32 + 32, 512:] = slots_ref[slot, 32:48, 512:]
        oup_ref[p * 16 : p * 16 + 16, :] = slots_ref[slot, 64:80, :FEAT]


def select_slots(adapter, position, slots):
    return pl.pallas_call(
        select_body,
        out_shape=(
            jax.ShapeDtypeStruct((192, FEAT), BF),
            jax.ShapeDtypeStruct((128, 640), BF),
            jax.ShapeDtypeStruct((64, FEAT), BF),
        ),
        grid_spec=pltpu.PrefetchScalarGridSpec(
            num_scalar_prefetch=2,
            grid=(1,),
            in_specs=[whole(16, 80, 640)],
            out_specs=(whole(192, FEAT), whole(128, 640), whole(64, FEAT)),
        ),
        name="select_slots",
    )(adapter, position, slots)


def norm_body(me_ref, length_ref, *refs):
    blocks, maps = refs[:8], refs[8:16]
    gain_ref, normed_ref, low_ref = refs[16:]
    order = col_order(me_ref[1])
    values = [b[...].astype(F32) for b in blocks]
    total = sum(jnp.sum(v * v, axis=-1, keepdims=True) for v in values)
    scale = lax.rsqrt(total * (1.0 / (8 * FEAT)) + EPSILON)
    low = jnp.zeros(low_ref.shape, F32)
    for b in range(8):
        gain = gain_ref[order[b]].astype(F32)
        normed = (values[b] * scale * gain).astype(BF)
        normed_ref[order[b]] = normed
        low += lax.dot_general(normed, maps[b][:128, :], (((1,), (1,)), ((), ())), preferred_element_type=F32)
    token = pl.program_id(0) * low.shape[0] + lax.broadcasted_iota(jnp.int32, low.shape, 0)
    prompt = per_token(prompt_rows(length_ref), range(PROMPTS), token)
    mine = lax.broadcasted_iota(jnp.int32, low.shape, 1) // 32 == prompt
    low_ref[...] = jnp.where(mine, low, 0.0).astype(BF)


def norm_low(me, lengths, blocks, maps, gain):
    rows = 128
    return pl.pallas_call(
        norm_body,
        out_shape=(jax.ShapeDtypeStruct((8, TOK, FEAT), BF), jax.ShapeDtypeStruct((TOK, 128), BF)),
        grid_spec=pltpu.PrefetchScalarGridSpec(
            num_scalar_prefetch=2,
            grid=(TOK // rows,),
            in_specs=[pl.BlockSpec((rows, FEAT), lambda i, *_: (i, 0))] * 8
            + [whole(192, FEAT)] * 8
            + [whole(8, 1, FEAT)],
            out_specs=(
                pl.BlockSpec((8, rows, FEAT), lambda i, *_: (0, i, 0)),
                pl.BlockSpec((rows, 128), lambda i, *_: (i, 0)),
            ),
        ),
        compiler_params=vmem(20),
        name="norm_low",
    )(me, lengths, *blocks, *maps, gain)


def qkv_body(normed_ref, w_ref, low_ref, up_ref, rope_ref, qg_ref, kg_ref, q_ref, kv_ref, acc):
    step = pl.program_id(0)
    part = jnp.dot(normed_ref[0], w_ref[...], preferred_element_type=F32)

    @pl.when(step == 0)
    def _():
        acc[...] = part

    @pl.when(step > 0)
    def _():
        acc[...] += part

    @pl.when(step == pl.num_programs(0) - 1)
    def _():
        change = 0.5 * jnp.dot(low_ref[...], up_ref[...], preferred_element_type=F32)
        rope = rope_ref[...]
        front = lax.broadcasted_iota(jnp.int32, rope.shape, 1) < HEAD // 2
        swapped = pltpu.roll(rope, HEAD // 2, 1)
        cos, sin = jnp.where(front, rope, swapped), jnp.where(front, -swapped, rope)

        def finish(raw, gain):
            scale = lax.rsqrt(jnp.mean(raw * raw, axis=-1, keepdims=True) + EPSILON)
            x = raw * scale * gain
            return (x * cos + pltpu.roll(x, HEAD // 2, 1) * sin).astype(BF)

        for h in range(GROUP):
            cut = slice(h * HEAD, (h + 1) * HEAD)
            q_ref[h] = finish(acc[:, cut] + change[:, cut], qg_ref[...].astype(F32))
        kv_ref[0] = finish(acc[:, 512:640], kg_ref[...].astype(F32))
        kv_ref[1] = (acc[:, 640:768] + change[:, 512:640]).astype(BF)


def project(normed, weight, low, up, rope, q_gain, k_gain):
    return pl.pallas_call(
        qkv_body,
        out_shape=(jax.ShapeDtypeStruct((GROUP, TOK, HEAD), BF), jax.ShapeDtypeStruct((2, TOK, HEAD), BF)),
        grid=(8,),
        in_specs=[
            pl.BlockSpec((1, TOK, FEAT), lambda k: (k, 0, 0)),
            pl.BlockSpec((FEAT, 768), lambda k: (k, 0)),
            whole(TOK, 128),
            whole(128, 640),
            whole(TOK, HEAD),
            whole(1, HEAD),
            whole(1, HEAD),
        ],
        out_specs=(whole(GROUP, TOK, HEAD), whole(2, TOK, HEAD)),
        scratch_shapes=[pltpu.VMEM((TOK, 768), F32)],
        compiler_params=vmem(16),
        name="project",
    )(in_hbm(normed), in_hbm(weight), low, up, rope, q_gain, k_gain)


BLOCK = 64
SCALE2 = math.log2(math.e) / math.sqrt(HEAD)


def attend_body(me_ref, length_ref, cache_ref, owner_ref, q_ref, kv_ref, pages_ref, out_ref, m_ref, l_ref, acc_ref, page_ref):
    rows, span = GROUP * BLOCK, 256 + BLOCK
    base = me_ref[0] * 16
    for i in range(16):
        holder, rank = owner_ref[base + i, 0], jnp.int32(0)
        for k in range(i):
            rank = rank + (owner_ref[base + k, 0] == holder).astype(jnp.int32)
        page_ref[i] = holder * 2 + rank
    prompts = prompt_rows(length_ref)
    begins = [start for start, _ in prompts]
    count, ranks = jnp.int32(0), []
    for p in range(PROMPTS):
        has = cache_ref[p] > 0
        ranks.append(jnp.where(has, count, -1))
        count = count + has.astype(jnp.int32)
    owners = []
    for j in range(2):
        pick = [(ranks[p] == j).astype(jnp.int32) for p in range(PROMPTS)]
        owners.append(tuple(sum(k * v for k, v in zip(pick, vs)) for vs in zip(*((s, e, cache_ref[p]) for p, (s, e) in enumerate(prompts)))))

    def block(t, carry):
        start = pl.multiple_of(t * BLOCK, BLOCK)
        lo = pl.multiple_of(jnp.maximum(start - 256, 0), BLOCK)
        cut = pl.ds(start, BLOCK)
        q = q_ref[:, cut, :].reshape(rows, HEAD)
        s = lax.dot_general(q, kv_ref[0, pl.ds(lo, span), :], (((1,), (1,)), ((), ())), preferred_element_type=F32)
        key = lo + lax.broadcasted_iota(jnp.int32, (BLOCK, span), 1)
        token = start + lax.broadcasted_iota(jnp.int32, (BLOCK, span), 0)
        column = start + lax.broadcasted_iota(jnp.int32, (BLOCK, 1), 0)
        begin = per_token(prompts, begins, column)
        seen = (key <= token) & (key >= begin)
        s = jnp.where(seen[None], s.reshape(GROUP, BLOCK, span), NEG).reshape(rows, span)
        m = jnp.max(s, axis=1, keepdims=True)
        w = jnp.exp2((s - m) * SCALE2)
        m_ref[...] = m
        l_ref[...] = jnp.sum(w, axis=1, keepdims=True)
        acc_ref[...] = jnp.dot(w.astype(BF), kv_ref[1, pl.ds(lo, span), :], preferred_element_type=F32)

        def cached(j):
            first, last, length = owners[j]
            mine = (column >= first) & (column < last)
            least = jnp.where(mine, length + column - first - WIN, 1 << 30)
            sink = jnp.where(mine, SINKS, 0)
            pieces = []
            for k in range(8):
                page = page_ref[j * 8 + k]
                c = lax.dot_general(q, pages_ref[page, 0], (((1,), (1,)), ((), ())), preferred_element_type=F32)
                at = k * PAGE + lax.broadcasted_iota(jnp.int32, (BLOCK, PAGE), 1)
                ok = at > least
                if k == 0:
                    ok = ok | (at < sink)
                ok = ok & (at < length)
                pieces.append(jnp.where(ok[None], c.reshape(GROUP, BLOCK, PAGE), NEG).reshape(rows, PAGE))
            top = pieces[0]
            for c in pieces[1:]:
                top = jnp.maximum(top, c)
            m_old = m_ref[...]
            m_new = jnp.maximum(m_old, jnp.max(top, axis=1, keepdims=True))
            fade = jnp.exp2((m_old - m_new) * SCALE2)
            total = jnp.zeros((rows, PAGE), F32)
            acc = acc_ref[...] * fade
            for k in range(8):
                page = page_ref[j * 8 + k]
                w = jnp.exp2((pieces[k] - m_new) * SCALE2)
                total += w
                acc += jnp.dot(w.astype(BF), pages_ref[page, 1], preferred_element_type=F32)
            m_ref[...] = m_new
            l_ref[...] = l_ref[...] * fade + jnp.sum(total, axis=1, keepdims=True)
            acc_ref[...] = acc

        for j in range(2):
            pl.when((owners[j][0] < start + BLOCK) & (owners[j][1] > start))(lambda j=j: cached(j))

        done = (acc_ref[...] * (1.0 / l_ref[...])).astype(BF)
        for h in range(GROUP):
            out_ref[cut, h * HEAD : (h + 1) * HEAD] = done[h * BLOCK : (h + 1) * BLOCK, :]
        return carry

    lax.fori_loop(0, TOK // BLOCK, block, 0)


def attention(me, lengths, cached, owner, q, kv, pages):
    rows = GROUP * BLOCK
    return pl.pallas_call(
        attend_body,
        out_shape=jax.ShapeDtypeStruct((TOK, FEAT), BF),
        grid_spec=pltpu.PrefetchScalarGridSpec(
            num_scalar_prefetch=4,
            grid=(1,),
            in_specs=[whole(GROUP, TOK, HEAD), whole(2, TOK, HEAD), whole(32, 2, PAGE, HEAD)],
            out_specs=whole(TOK, FEAT),
            scratch_shapes=[
                pltpu.VMEM((rows, 1), F32),
                pltpu.VMEM((rows, 1), F32),
                pltpu.VMEM((rows, HEAD), F32),
                pltpu.SMEM((16,), jnp.int32),
            ],
        ),
        compiler_params=vmem(16),
        name="attention",
    )(me, lengths, cached, owner, q, kv, pages)


def out_body(me_ref, length_ref, *refs):
    blocks, maps = refs[:8], refs[8:16]
    w_ref, oup_ref, hidden_ref, out_ref = refs[16:]
    order = col_order(me_ref[1])
    total = hidden_ref[...].astype(F32)
    low = jnp.zeros((total.shape[0], 64), F32)
    for b in range(8):
        x = blocks[b][...]
        total += jnp.dot(x, w_ref[order[b]], preferred_element_type=F32)
        low += lax.dot_general(x, maps[b][128:192, :], (((1,), (1,)), ((), ())), preferred_element_type=F32)
    token = pl.program_id(0) * low.shape[0] + lax.broadcasted_iota(jnp.int32, low.shape, 0)
    prompt = per_token(prompt_rows(length_ref), range(PROMPTS), token)
    mine = lax.broadcasted_iota(jnp.int32, low.shape, 1) // 16 == prompt
    low = jnp.where(mine, low, 0.0)
    change = jnp.dot(low, oup_ref[...].astype(F32), precision=lax.Precision.HIGHEST, preferred_element_type=F32)
    out_ref[...] = (total + 0.5 * change).astype(BF)


def output(me, lengths, blocks, maps, weight, oup, hidden):
    rows = 128
    tok = pl.BlockSpec((rows, FEAT), lambda i, *_: (i, 0))
    return pl.pallas_call(
        out_body,
        out_shape=jax.ShapeDtypeStruct((TOK, FEAT), BF),
        grid_spec=pltpu.PrefetchScalarGridSpec(
            num_scalar_prefetch=2,
            grid=(TOK // rows,),
            in_specs=[tok] * 8 + [whole(192, FEAT)] * 8 + [whole(8, FEAT, FEAT), whole(64, FEAT), tok],
            out_specs=tok,
        ),
        compiler_params=vmem(24),
        name="output",
    )(me, lengths, *map(in_hbm, blocks), *map(in_hbm, maps), in_hbm(weight), in_hbm(oup), in_hbm(hidden))


def on_device(
    hidden_input,
    input_norm_gain,
    query_norm_gain,
    key_norm_gain,
    query_key_value_weight,
    output_weight,
    adapter_down_maps,
    adapter_up_maps,
    output_down_maps,
    output_up_maps,
    prompt_adapter,
    adapter_position,
    prompt_length,
    cache_length,
    page_owner_row,
    page_store_index,
    cache_page_store,
):
    me = jnp.stack([lax.axis_index("row"), lax.axis_index("col")]).astype(jnp.int32)
    weight = lax.all_gather(query_key_value_weight, "row", axis=0, tiled=True)

    slots = pack_slots(me, adapter_down_maps, adapter_up_maps, output_down_maps, output_up_maps)
    slots = lax.all_to_all(slots, "row", 0, 0)

    picked = pick_pages(me, page_owner_row, page_store_index, cache_page_store)
    picked, slots = lax.optimization_barrier((picked, slots))
    pages = lax.all_to_all(picked.reshape(16, 4 * PAGE, HEAD), "row", 0, 0).reshape(32, 2, PAGE, HEAD)

    blocks = gather_col(hidden_input, 256)

    maps, up, oup = select_slots(prompt_adapter, adapter_position, slots)
    maps = gather_col(maps, 96)

    token = lax.broadcasted_iota(jnp.int32, (TOK, HEAD), 0)
    position, start = token, jnp.int32(0)
    for p in range(PROMPTS):
        end = start + prompt_length[0, p]
        position = jnp.where((token >= start) & (token < end), token - start + cache_length[p], position)
        start = end
    frequency = ROPE_BASE ** (-2.0 * jnp.arange(HEAD // 2, dtype=F32) / HEAD)
    angles = position.astype(F32) * jnp.concatenate([frequency, frequency])[None, :]
    front = lax.broadcasted_iota(jnp.int32, (TOK, HEAD), 1) < HEAD // 2
    rope = jnp.where(front, jnp.cos(angles), jnp.sin(angles))

    normed, low = norm_low(me, prompt_length, blocks, maps, input_norm_gain.reshape(8, 1, FEAT))
    weight, later, normed, low, pages, rope, up = lax.optimization_barrier(
        (weight, output_weight, normed, low, pages, rope, up)
    )
    out_weight = lax.all_gather(later, "row", axis=0, tiled=True)
    q, new_cache = project(
        normed, weight, low, up, rope, query_norm_gain[None, :], key_norm_gain[None, :]
    )
    attended = attention(me, prompt_length, cache_length, page_owner_row, q, new_cache, pages)
    attended = gather_col(attended, 256)
    hidden_output = output(
        me, prompt_length, attended, maps, out_weight.reshape(8, FEAT, FEAT), oup, hidden_input
    )
    return hidden_output, new_cache


def solution(mesh):
    return jax.shard_map(
        on_device,
        mesh=mesh,
        in_specs=(
            P("row", "col"),
            P(),
            P(),
            P(),
            P("row", "col"),
            P("row", "col"),
            P("row", None, None),
            P("row", None, "col"),
            P("row", None, "col"),
            P("row", None, None),
            P("row"),
            P(),
            P("row", None),
            P("row"),
            P(),
            P(),
            P("row", None, None, "col"),
        ),
        out_specs=(P("row", "col"), P(None, "row", "col")),
        check_vma=False,
    )
```

```python
import math

import jax
import jax.numpy as jnp
from jax import lax
from jax.experimental import pallas as pl
from jax.experimental.pallas import tpu as pltpu
from jax.sharding import PartitionSpec as P

HEAD = 128
GROUP = 4
WIN = 1024
SINKS = 4
PAGE = 128
EPSILON = 1e-06
ROPE_BASE = 1000000.0
TOK = 512
FEAT = 512
PROMPTS = 4
BF = jnp.bfloat16
F32 = jnp.float32
NEG = -1e30


def perm_x(k):
    return [(i, (i // 4 + k) % 4 * 4 + i % 4) for i in range(16)]


def perm_y(k):
    return [(i, i // 4 * 4 + (i % 4 + k) % 4) for i in range(16)]


def perm_z(k):
    return [(i, (i // 2 + k) % 4 * 2 + i % 2) for i in range(8)]


SWAP = [(i, i ^ 1) for i in range(8)]


def ring4(block, axis, perm, half):
    before = lax.ppermute(block, axis, perm(1))
    after = lax.ppermute(block, axis, perm(-1))
    far_low = lax.ppermute(before[:half], axis, perm(1))
    far_high = lax.ppermute(after[half:], axis, perm(-1))
    return before, after, jnp.concatenate([far_low, far_high], axis=0)


def gather_col(block, half):
    other = lax.ppermute(block, "col", SWAP)
    out = [block, other]
    for piece in ring4(block, "col", perm_z, half):
        out += [piece, lax.ppermute(piece, "col", SWAP)]
    return out


def col_order(col):
    chip, core = col // 2, col % 2
    return [lax.rem(chip + d, 4) * 2 + lax.rem(core + s, 2) for d in (0, 3, 1, 2) for s in (0, 1)]


def prompt_rows(length_ref):
    start, rows = jnp.int32(0), []
    for p in range(PROMPTS):
        rows.append((start, start + length_ref[0, p]))
        start = start + length_ref[0, p]
    return rows


def per_token(rows, values, token, default=0):
    out = jnp.full(token.shape, default, jnp.int32)
    for (start, end), value in zip(rows, values):
        out = jnp.where((token >= start) & (token < end), value, out)
    return out


def in_hbm(x):
    return pltpu.with_memory_space_constraint(x, pltpu.HBM)


def vmem(n):
    return pltpu.CompilerParams(vmem_limit_bytes=n << 20)


def whole(*shape):
    return pl.BlockSpec(shape, lambda *_: (0,) * len(shape))


def pick_body(me_ref, owner_ref, index_ref, store_ref, out_ref):
    def group(r, carry):
        first, second, count = jnp.int32(0), jnp.int32(0), jnp.int32(0)
        for q in range(16):
            hit = owner_ref[r * 16 + q, 0] == me_ref[0]
            index = index_ref[r * 16 + q]
            first = jnp.where(hit & (count == 0), index, first)
            second = jnp.where(hit & (count == 1), index, second)
            count = count + hit.astype(jnp.int32)
        out_ref[r, 0] = store_ref[first]
        out_ref[r, 1] = store_ref[second]
        return carry

    lax.fori_loop(0, 16, group, 0)


def pick_pages(me, owner, index, store):
    return pl.pallas_call(
        pick_body,
        out_shape=jax.ShapeDtypeStruct((16, 2) + store.shape[1:], store.dtype),
        grid_spec=pltpu.PrefetchScalarGridSpec(
            num_scalar_prefetch=3,
            grid=(1,),
            in_specs=[whole(*store.shape)],
            out_specs=whole(16, 2, *store.shape[1:]),
        ),
        compiler_params=vmem(10),
        name="pick_pages",
    )(me, owner, index, store)


def pack_body(me_ref, qkv_ref, wo_ref, up_ref, oup_ref, down_ref, odown_ref, wide_ref, slots_ref):
    wide_ref[:256, :768] = qkv_ref[...]
    wide_ref[:256, 768:] = wo_ref[...]
    wide_ref[256:, :640] = up_ref[0]
    wide_ref[256:, 640:1152] = oup_ref[0]
    wide_ref[256:, 1152:] = jnp.zeros((16, 128), BF)
    for r in range(16):
        slots_ref[r, :32, :] = down_ref[0]
        slots_ref[r, 32:, :] = odown_ref[0]


def pack(me, qkv, wo, up, oup, down, odown):
    return pl.pallas_call(
        pack_body,
        out_shape=(jax.ShapeDtypeStruct((272, 1280), BF), jax.ShapeDtypeStruct((16, 48, FEAT), BF)),
        grid_spec=pltpu.PrefetchScalarGridSpec(
            num_scalar_prefetch=1,
            grid=(1,),
            in_specs=[
                whole(256, 768),
                whole(256, FEAT),
                whole(1, 16, 640),
                pl.BlockSpec((1, 16, FEAT), lambda i, me: (0, 0, me[1])),
                pl.BlockSpec((1, 32, FEAT), lambda i, me: (0, 0, me[1])),
                whole(1, 16, FEAT),
            ],
            out_specs=(whole(272, 1280), whole(16, 48, FEAT)),
        ),
        name="pack",
    )(me, qkv, wo, up, oup, down, odown)


def select_body(adapter_ref, position_ref, slots_ref, maps_ref):
    for p in range(PROMPTS):
        slot = position_ref[adapter_ref[p]]
        maps_ref[p * 32 : p * 32 + 32, :] = slots_ref[slot, :32, :]
        maps_ref[128 + p * 16 : 128 + p * 16 + 16, :] = slots_ref[slot, 32:, :]


def select_slots(adapter, position, slots):
    return pl.pallas_call(
        select_body,
        out_shape=jax.ShapeDtypeStruct((192, FEAT), BF),
        grid_spec=pltpu.PrefetchScalarGridSpec(
            num_scalar_prefetch=2,
            grid=(1,),
            in_specs=[whole(16, 48, FEAT)],
            out_specs=whole(192, FEAT),
        ),
        name="select_slots",
    )(adapter, position, slots)


def norm_body(me_ref, length_ref, *refs):
    blocks, maps = refs[:8], refs[8:16]
    gain_ref, normed_ref, low_ref = refs[16:]
    order = col_order(me_ref[1])
    values = [b[...].astype(F32) for b in blocks]
    total = sum(jnp.sum(v * v, axis=-1, keepdims=True) for v in values)
    scale = lax.rsqrt(total * (1.0 / (8 * FEAT)) + EPSILON)
    low = jnp.zeros(low_ref.shape, F32)
    for b in range(8):
        gain = gain_ref[order[b]].astype(F32)
        normed = (values[b] * scale * gain).astype(BF)
        normed_ref[order[b] // 2, :, pl.ds(pl.multiple_of(order[b] % 2 * FEAT, FEAT), FEAT)] = normed
        low += lax.dot_general(normed, maps[b][:128, :], (((1,), (1,)), ((), ())), preferred_element_type=F32)
    token = pl.program_id(0) * low.shape[0] + lax.broadcasted_iota(jnp.int32, low.shape, 0)
    prompt = per_token(prompt_rows(length_ref), range(PROMPTS), token)
    mine = lax.broadcasted_iota(jnp.int32, low.shape, 1) // 32 == prompt
    low_ref[...] = jnp.where(mine, low, 0.0).astype(BF)


def norm_low(me, lengths, blocks, maps, gain):
    rows = 128
    return pl.pallas_call(
        norm_body,
        out_shape=(pltpu.HBM((4, TOK, 2 * FEAT), BF), pltpu.HBM((TOK, 128), BF)),
        grid_spec=pltpu.PrefetchScalarGridSpec(
            num_scalar_prefetch=2,
            grid=(TOK // rows,),
            in_specs=[pl.BlockSpec((rows, FEAT), lambda i, *_: (i, 0))] * 8
            + [whole(192, FEAT)] * 8
            + [whole(8, 1, FEAT)],
            out_specs=(
                pl.BlockSpec((4, rows, 2 * FEAT), lambda i, *_: (0, i, 0)),
                pl.BlockSpec((rows, 128), lambda i, *_: (i, 0)),
            ),
        ),
        compiler_params=vmem(20),
        name="norm_low",
    )(me, lengths, *blocks, *maps, gain)


def qkv_body(adapter_ref, position_ref, normed_ref, w_ref, low_ref, rope_ref, qg_ref, kg_ref, q_ref, kv_ref, x, w, up, acc, sems):
    copies = []
    for k in range(4):
        copies.append(pltpu.make_async_copy(normed_ref.at[k], x.at[k], sems.at[2 * k]))
        rows = w_ref.at[pl.ds(4 * k, 4), pl.ds(0, 256), pl.ds(0, 768)]
        copies.append(pltpu.make_async_copy(rows, w.at[k], sems.at[2 * k + 1]))
    for p in range(PROMPTS):
        slot = position_ref[adapter_ref[p]]
        copies.append(pltpu.make_async_copy(w_ref.at[slot, pl.ds(256, 16), pl.ds(0, 640)], up.at[p], sems.at[8 + p]))
    for copy in copies:
        copy.start()
    for k in range(4):
        copies[2 * k].wait()
        copies[2 * k + 1].wait()
        part = jnp.dot(x[k], w[k].reshape(1024, 768), preferred_element_type=F32)
        if k == 0:
            acc[...] = part
        else:
            acc[...] += part
    for copy in copies[8:]:
        copy.wait()
    low = low_ref[...]
    q_change = jnp.zeros((TOK, 512), F32)
    v_change = jnp.zeros((TOK, HEAD), F32)
    for p in range(PROMPTS):
        q_change += jnp.dot(low[:, p * 32 : p * 32 + 16], up[p, :, :512], preferred_element_type=F32)
        v_change += jnp.dot(low[:, p * 32 + 16 : p * 32 + 32], up[p, :, 512:], preferred_element_type=F32)
    rope = rope_ref[...]
    front = lax.broadcasted_iota(jnp.int32, rope.shape, 1) < HEAD // 2
    swapped = pltpu.roll(rope, HEAD // 2, 1)
    cos, sin = jnp.where(front, rope, swapped), jnp.where(front, -swapped, rope)

    def finish(raw, gain):
        scale = lax.rsqrt(jnp.mean(raw * raw, axis=-1, keepdims=True) + EPSILON)
        x = raw * scale * gain
        return (x * cos + pltpu.roll(x, HEAD // 2, 1) * sin).astype(BF)

    for h in range(GROUP):
        cut = slice(h * HEAD, (h + 1) * HEAD)
        q_ref[h] = finish(acc[:, cut] + 0.5 * q_change[:, cut], qg_ref[...].astype(F32))
    kv_ref[0] = finish(acc[:, 512:640], kg_ref[...].astype(F32))
    kv_ref[1] = (acc[:, 640:768] + 0.5 * v_change).astype(BF)


def project(adapter, position, normed, weight, low, rope, q_gain, k_gain):
    hbm = pl.BlockSpec(memory_space=pl.ANY)
    return pl.pallas_call(
        qkv_body,
        out_shape=(jax.ShapeDtypeStruct((GROUP, TOK, HEAD), BF), jax.ShapeDtypeStruct((2, TOK, HEAD), BF)),
        grid_spec=pltpu.PrefetchScalarGridSpec(
            num_scalar_prefetch=2,
            grid=(1,),
            in_specs=[hbm, hbm, whole(TOK, 128), whole(TOK, HEAD), whole(1, HEAD), whole(1, HEAD)],
            out_specs=(whole(GROUP, TOK, HEAD), whole(2, TOK, HEAD)),
            scratch_shapes=[
                pltpu.VMEM((4, TOK, 1024), BF),
                pltpu.VMEM((4, 4, 256, 768), BF),
                pltpu.VMEM((PROMPTS, 16, 640), BF),
                pltpu.VMEM((TOK, 768), F32),
                pltpu.SemaphoreType.DMA((12,)),
            ],
        ),
        compiler_params=vmem(28),
        name="project",
    )(adapter, position, in_hbm(normed), in_hbm(weight), in_hbm(low), in_hbm(rope), in_hbm(q_gain), in_hbm(k_gain))


BLOCK = 64
SCALE2 = math.log2(math.e) / math.sqrt(HEAD)


def attend_body(me_ref, length_ref, cache_ref, owner_ref, q_ref, kv_ref, pages_ref, out_ref, m_ref, l_ref, acc_ref, cached_ref, sems):
    rows, span = GROUP * BLOCK, 256 + BLOCK
    base = me_ref[0] * 16
    copies = []
    for i in range(16):
        holder, rank = owner_ref[base + i, 0], jnp.int32(0)
        for k in range(i):
            rank = rank + (owner_ref[base + k, 0] == holder).astype(jnp.int32)
        page = holder * 2 + jnp.minimum(rank, 1)
        for h in range(2):
            into = cached_ref.at[h, i // 8, pl.ds(i % 8 * PAGE, PAGE)]
            copies.append(pltpu.make_async_copy(pages_ref.at[page, h], into, sems.at[2 * i + h]))
    for copy in copies:
        copy.start()
    prompts = prompt_rows(length_ref)
    begins = [start for start, _ in prompts]
    count, ranks = jnp.int32(0), []
    for p in range(PROMPTS):
        has = cache_ref[p] > 0
        ranks.append(jnp.where(has, count, -1))
        count = count + has.astype(jnp.int32)
    owners = []
    for j in range(2):
        mine = [(ranks[p] == j).astype(jnp.int32) for p in range(PROMPTS)]
        owners.append(
            (
                sum(mine[p] * prompts[p][0] for p in range(PROMPTS)),
                sum(mine[p] * prompts[p][1] for p in range(PROMPTS)),
                sum(mine[p] * cache_ref[p] for p in range(PROMPTS)),
            )
        )
    for copy in copies:
        copy.wait()

    def block(t, carry):
        start = pl.multiple_of(t * BLOCK, BLOCK)
        lo = pl.multiple_of(jnp.maximum(start - 256, 0), BLOCK)
        cut = pl.ds(start, BLOCK)
        q = q_ref[:, cut, :].reshape(rows, HEAD)
        token = start + (lax.broadcasted_iota(jnp.int32, (rows, 1), 0) & (BLOCK - 1))
        begin = per_token(prompts, begins, token)
        s = lax.dot_general(q, kv_ref[0, pl.ds(lo, span), :], (((1,), (1,)), ((), ())), preferred_element_type=F32)
        key = lo + lax.broadcasted_iota(jnp.int32, (rows, span), 1)
        s = jnp.where((key <= token) & (key >= begin), s, NEG)
        m = jnp.max(s, axis=1, keepdims=True)
        w = jnp.exp2((s - m) * SCALE2)
        m_ref[...] = m
        l_ref[...] = jnp.sum(w, axis=1, keepdims=True)
        acc_ref[...] = jnp.dot(w.astype(BF), kv_ref[1, pl.ds(lo, span), :], preferred_element_type=F32)

        def cached(j):
            first, last, length = owners[j]
            mine = (token >= first) & (token < last)
            s = lax.dot_general(q, cached_ref[0, j], (((1,), (1,)), ((), ())), preferred_element_type=F32)
            at = lax.broadcasted_iota(jnp.int32, (rows, 256), 1)
            head = jnp.where((at > length + token - first - WIN) | (at < SINKS), s[:, :256], NEG)
            at = WIN - PAGE + lax.broadcasted_iota(jnp.int32, (rows, PAGE), 1)
            tail = jnp.where(at < length, s[:, WIN - PAGE :], NEG)
            s = jnp.concatenate([head, s[:, 256 : WIN - PAGE], tail], axis=1)
            m_old = m_ref[...]
            m_new = jnp.where(mine, jnp.maximum(m_old, jnp.max(s, axis=1, keepdims=True)), m_old)
            fade = jnp.exp2((m_old - m_new) * SCALE2)
            w = jnp.exp2((s - jnp.where(mine, m_new, -NEG)) * SCALE2)
            m_ref[...] = m_new
            l_ref[...] = l_ref[...] * fade + jnp.sum(w, axis=1, keepdims=True)
            acc_ref[...] = acc_ref[...] * fade + jnp.dot(w.astype(BF), cached_ref[1, j], preferred_element_type=F32)

        for j in range(2):
            pl.when((owners[j][0] < start + BLOCK) & (owners[j][1] > start))(lambda j=j: cached(j))

        done = (acc_ref[...] * (1.0 / l_ref[...])).astype(BF)
        for h in range(GROUP):
            out_ref[cut, h * HEAD : (h + 1) * HEAD] = done[h * BLOCK : (h + 1) * BLOCK, :]
        return carry

    lax.fori_loop(0, TOK // BLOCK, block, 0)


def attention(me, lengths, cached, owner, q, kv, pages):
    rows = GROUP * BLOCK
    return pl.pallas_call(
        attend_body,
        out_shape=jax.ShapeDtypeStruct((TOK, FEAT), BF),
        grid_spec=pltpu.PrefetchScalarGridSpec(
            num_scalar_prefetch=4,
            grid=(1,),
            in_specs=[
                whole(GROUP, TOK, HEAD),
                whole(2, TOK, HEAD),
                pl.BlockSpec(memory_space=pl.ANY),
            ],
            out_specs=whole(TOK, FEAT),
            scratch_shapes=[
                pltpu.VMEM((rows, 1), F32),
                pltpu.VMEM((rows, 1), F32),
                pltpu.VMEM((rows, HEAD), F32),
                pltpu.VMEM((2, 2, WIN, HEAD), BF),
                pltpu.SemaphoreType.DMA((32,)),
            ],
        ),
        compiler_params=vmem(16),
        name="attention",
    )(me, lengths, cached, owner, q, kv, in_hbm(pages))


def out_body(me_ref, length_ref, adapter_ref, position_ref, *refs):
    blocks, maps = refs[:8], refs[8:16]
    weight_ref, hidden_ref, out_ref, w, oup, sems = refs[16:]
    order = col_order(me_ref[1])

    def copies():
        out = []
        for b in range(8):
            rows = weight_ref.at[pl.ds(2 * order[b], 2), pl.ds(0, 256), pl.ds(768, FEAT)]
            out.append(pltpu.make_async_copy(rows, w.at[b], sems.at[b]))
        for p in range(PROMPTS):
            slot = position_ref[adapter_ref[p]]
            rows = weight_ref.at[slot, pl.ds(256, 16), pl.ds(640, FEAT)]
            out.append(pltpu.make_async_copy(rows, oup.at[pl.ds(p * 16, 16)], sems.at[8 + p]))
        return out

    @pl.when(pl.program_id(0) == 0)
    def _():
        todo = copies()
        for copy in todo:
            copy.start()
        for copy in todo:
            copy.wait()

    total = hidden_ref[...].astype(F32)
    low = jnp.zeros((total.shape[0], 64), F32)
    for b in range(8):
        x = blocks[b][...]
        total += jnp.dot(x, w[b].reshape(FEAT, FEAT), preferred_element_type=F32)
        low += lax.dot_general(x, maps[b][128:192, :], (((1,), (1,)), ((), ())), preferred_element_type=F32)
    token = pl.program_id(0) * low.shape[0] + lax.broadcasted_iota(jnp.int32, low.shape, 0)
    prompt = per_token(prompt_rows(length_ref), range(PROMPTS), token)
    mine = lax.broadcasted_iota(jnp.int32, low.shape, 1) // 16 == prompt
    low = jnp.where(mine, low, 0.0)
    change = jnp.dot(low, oup[...].astype(F32), precision=lax.Precision.HIGHEST, preferred_element_type=F32)
    out_ref[...] = (total + 0.5 * change).astype(BF)


def output(me, lengths, adapter, position, blocks, maps, weight, hidden):
    rows = 256
    tok = pl.BlockSpec((rows, FEAT), lambda i, *_: (i, 0))
    return pl.pallas_call(
        out_body,
        out_shape=jax.ShapeDtypeStruct((TOK, FEAT), BF),
        grid_spec=pltpu.PrefetchScalarGridSpec(
            num_scalar_prefetch=4,
            grid=(TOK // rows,),
            in_specs=[tok] * 8 + [whole(192, FEAT)] * 8 + [pl.BlockSpec(memory_space=pl.ANY), tok],
            out_specs=tok,
            scratch_shapes=[
                pltpu.VMEM((8, 2, 256, FEAT), BF),
                pltpu.VMEM((64, FEAT), BF),
                pltpu.SemaphoreType.DMA((12,)),
            ],
        ),
        compiler_params=vmem(24),
        name="output",
    )(me, lengths, adapter, position, *blocks, *maps, in_hbm(weight), hidden)


def on_device(
    hidden_input,
    input_norm_gain,
    query_norm_gain,
    key_norm_gain,
    query_key_value_weight,
    output_weight,
    adapter_down_maps,
    adapter_up_maps,
    output_down_maps,
    output_up_maps,
    prompt_adapter,
    adapter_position,
    prompt_length,
    cache_length,
    page_owner_row,
    page_store_index,
    cache_page_store,
):
    me = jnp.stack([lax.axis_index("row"), lax.axis_index("col")]).astype(jnp.int32)
    wide, slots = pack(
        me,
        query_key_value_weight,
        output_weight,
        adapter_up_maps,
        output_up_maps,
        adapter_down_maps,
        output_down_maps,
    )
    weight = lax.all_gather(wide, "row", axis=0)
    slots = lax.all_to_all(slots, "row", 0, 0)

    picked = pick_pages(me, page_owner_row, page_store_index, cache_page_store)
    picked, slots = lax.optimization_barrier((picked, slots))
    pages = lax.all_to_all(picked.reshape(16, 4 * PAGE, HEAD), "row", 0, 0).reshape(32, 2, PAGE, HEAD)

    blocks = gather_col(hidden_input, 256)

    maps = select_slots(prompt_adapter, adapter_position, slots)
    maps = gather_col(maps, 96)

    token = lax.broadcasted_iota(jnp.int32, (TOK, HEAD), 0)
    position, start = token, jnp.int32(0)
    for p in range(PROMPTS):
        end = start + prompt_length[0, p]
        position = jnp.where((token >= start) & (token < end), token - start + cache_length[p], position)
        start = end
    frequency = ROPE_BASE ** (-2.0 * jnp.arange(HEAD // 2, dtype=F32) / HEAD)
    angles = position.astype(F32) * jnp.concatenate([frequency, frequency])[None, :]
    front = lax.broadcasted_iota(jnp.int32, (TOK, HEAD), 1) < HEAD // 2
    rope = jnp.where(front, jnp.cos(angles), jnp.sin(angles))

    normed, low = norm_low(me, prompt_length, blocks, maps, input_norm_gain.reshape(8, 1, FEAT))
    weight, normed, low, pages, rope = lax.optimization_barrier((weight, normed, low, pages, rope))
    q, new_cache = project(
        prompt_adapter,
        adapter_position,
        normed,
        weight,
        low,
        rope,
        query_norm_gain[None, :],
        key_norm_gain[None, :],
    )
    attended = attention(me, prompt_length, cache_length, page_owner_row, q, new_cache, pages)
    attended = gather_col(attended, 256)
    hidden_output = output(
        me, prompt_length, prompt_adapter, adapter_position, attended, maps, weight, hidden_input
    )
    return hidden_output, new_cache


def solution(mesh):
    return jax.shard_map(
        on_device,
        mesh=mesh,
        in_specs=(
            P("row", "col"),
            P(),
            P(),
            P(),
            P("row", "col"),
            P("row", "col"),
            P("row", None, None),
            P("row", None, "col"),
            P("row", None, "col"),
            P("row", None, None),
            P("row"),
            P(),
            P("row", None),
            P("row"),
            P(),
            P(),
            P("row", None, None, "col"),
        ),
        out_specs=(P("row", "col"), P(None, "row", "col")),
        check_vma=False,
    )
```

```python
import math

import jax
import jax.numpy as jnp
from jax import lax
from jax.experimental import pallas as pl
from jax.experimental.pallas import tpu as pltpu
from jax.sharding import PartitionSpec as P

HEAD = 128
GROUP = 4
WIN = 1024
SINKS = 4
PAGE = 128
EPSILON = 1e-06
ROPE_BASE = 1000000.0
TOK = 512
FEAT = 512
PROMPTS = 4
BF = jnp.bfloat16
F32 = jnp.float32
NEG = -1e30


def perm_x(k):
    return [(i, (i // 4 + k) % 4 * 4 + i % 4) for i in range(16)]


def perm_y(k):
    return [(i, i // 4 * 4 + (i % 4 + k) % 4) for i in range(16)]


def perm_z(k):
    return [(i, (i // 2 + k) % 4 * 2 + i % 2) for i in range(8)]


SWAP = [(i, i ^ 1) for i in range(8)]


def ring_far(before, after, axis, perm, half):
    far_low = lax.ppermute(before[:half], axis, perm(1))
    far_high = lax.ppermute(after[half:], axis, perm(-1))
    return jnp.concatenate([far_low, far_high], axis=0)


def ring4(block, axis, perm, half):
    before = lax.ppermute(block, axis, perm(1))
    after = lax.ppermute(block, axis, perm(-1))
    return before, after, ring_far(before, after, axis, perm, half)


def swap(block):
    return lax.ppermute(block, "col", SWAP)


def gather_col(block, half):
    out = [block, swap(block)]
    for piece in ring4(block, "col", perm_z, half):
        out += [piece, swap(piece)]
    return out


def col_order(col):
    chip, core = col // 2, col % 2
    return [lax.rem(chip + d, 4) * 2 + lax.rem(core + s, 2) for d in (0, 3, 1, 2) for s in (0, 1)]


def prompt_rows(length_ref):
    start, rows = jnp.int32(0), []
    for p in range(PROMPTS):
        rows.append((start, start + length_ref[0, p]))
        start = start + length_ref[0, p]
    return rows


def per_token(rows, values, token, default=0):
    out = jnp.full(token.shape, default, jnp.int32)
    for (start, end), value in zip(rows, values):
        out = jnp.where((token >= start) & (token < end), value, out)
    return out


def in_hbm(x):
    return pltpu.with_memory_space_constraint(x, pltpu.HBM)


def vmem(n):
    return pltpu.CompilerParams(vmem_limit_bytes=n << 20)


def whole(*shape):
    return pl.BlockSpec(shape, lambda *_: (0,) * len(shape))


def pick_body(me_ref, owner_ref, index_ref, store_ref, out_ref, place_ref):
    def group(r, carry):
        first, second, count = jnp.int32(0), jnp.int32(0), jnp.int32(0)
        for q in range(16):
            hit = owner_ref[r * 16 + q, 0] == me_ref[0]
            index = index_ref[r * 16 + q]
            first = jnp.where(hit & (count == 0), index, first)
            second = jnp.where(hit & (count == 1), index, second)
            count = count + hit.astype(jnp.int32)
        out_ref[r, 0] = store_ref[first]
        out_ref[r, 1] = store_ref[second]
        return carry

    lax.fori_loop(0, 16, group, 0)
    for i in range(16):
        holder, rank = owner_ref[me_ref[0] * 16 + i, 0], jnp.int32(0)
        for k in range(i):
            rank = jnp.where(owner_ref[me_ref[0] * 16 + k, 0] == holder, 1, rank)
        place_ref[i] = holder * 2 + rank


def pick_pages(me, owner, index, store):
    return pl.pallas_call(
        pick_body,
        out_shape=(
            jax.ShapeDtypeStruct((16, 2) + store.shape[1:], store.dtype),
            jax.ShapeDtypeStruct((16,), jnp.int32),
        ),
        grid_spec=pltpu.PrefetchScalarGridSpec(
            num_scalar_prefetch=3,
            grid=(1,),
            in_specs=[whole(*store.shape)],
            out_specs=(whole(16, 2, *store.shape[1:]), pl.BlockSpec(memory_space=pltpu.SMEM)),
        ),
        compiler_params=vmem(10),
        name="pick_pages",
    )(me, owner, index, store)


def pack_body(me_ref, qkv_ref, wo_ref, up_ref, oup_ref, down_ref, odown_ref, wide_ref, slots_ref):
    wide_ref[:256, :768] = qkv_ref[...]
    wide_ref[:256, 768:] = wo_ref[...]
    wide_ref[256:, :640] = up_ref[0]
    wide_ref[256:, 640:1152] = oup_ref[0]
    wide_ref[256:, 1152:] = jnp.zeros((16, 128), BF)
    for r in range(16):
        slots_ref[r, :32, :] = down_ref[0]
        slots_ref[r, 32:, :] = odown_ref[0]


def pack(me, qkv, wo, up, oup, down, odown):
    return pl.pallas_call(
        pack_body,
        out_shape=(jax.ShapeDtypeStruct((272, 1280), BF), jax.ShapeDtypeStruct((16, 48, FEAT), BF)),
        grid_spec=pltpu.PrefetchScalarGridSpec(
            num_scalar_prefetch=1,
            grid=(1,),
            in_specs=[
                whole(256, 768),
                whole(256, FEAT),
                whole(1, 16, 640),
                pl.BlockSpec((1, 16, FEAT), lambda i, me: (0, 0, me[1])),
                pl.BlockSpec((1, 32, FEAT), lambda i, me: (0, 0, me[1])),
                whole(1, 16, FEAT),
            ],
            out_specs=(whole(272, 1280), whole(16, 48, FEAT)),
        ),
        name="pack",
    )(me, qkv, wo, up, oup, down, odown)


def select_body(adapter_ref, position_ref, slots_ref, maps_ref):
    for p in range(PROMPTS):
        slot = position_ref[adapter_ref[p]]
        maps_ref[p * 32 : p * 32 + 32, :] = slots_ref[slot, :32, :]
        maps_ref[128 + p * 16 : 128 + p * 16 + 16, :] = slots_ref[slot, 32:, :]


def select_slots(adapter, position, slots):
    return pl.pallas_call(
        select_body,
        out_shape=jax.ShapeDtypeStruct((192, FEAT), BF),
        grid_spec=pltpu.PrefetchScalarGridSpec(
            num_scalar_prefetch=2,
            grid=(1,),
            in_specs=[whole(16, 48, FEAT)],
            out_specs=whole(192, FEAT),
        ),
        name="select_slots",
    )(adapter, position, slots)


def norm_body(me_ref, length_ref, *refs):
    blocks, maps = refs[:8], refs[8:16]
    gain_ref, normed_ref, low_ref = refs[16:]
    order = col_order(me_ref[1])
    values = [b[...].astype(F32) for b in blocks]
    total = sum(jnp.sum(v * v, axis=-1, keepdims=True) for v in values)
    scale = lax.rsqrt(total * (1.0 / (8 * FEAT)) + EPSILON)
    low = jnp.zeros(low_ref.shape, F32)
    for b in range(8):
        gain = gain_ref[order[b]].astype(F32)
        normed = (values[b] * scale * gain).astype(BF)
        normed_ref[order[b] // 2, :, pl.ds(pl.multiple_of(order[b] % 2 * FEAT, FEAT), FEAT)] = normed
        low += lax.dot_general(normed, maps[b][:128, :], (((1,), (1,)), ((), ())), preferred_element_type=F32)
    token = pl.program_id(0) * low.shape[0] + lax.broadcasted_iota(jnp.int32, low.shape, 0)
    prompt = per_token(prompt_rows(length_ref), range(PROMPTS), token)
    mine = lax.broadcasted_iota(jnp.int32, low.shape, 1) // 32 == prompt
    low_ref[...] = jnp.where(mine, low, 0.0).astype(BF)


def norm_low(me, lengths, blocks, maps, gain):
    rows = 128
    return pl.pallas_call(
        norm_body,
        out_shape=(pltpu.HBM((4, TOK, 2 * FEAT), BF), pltpu.HBM((TOK, 128), BF)),
        grid_spec=pltpu.PrefetchScalarGridSpec(
            num_scalar_prefetch=2,
            grid=(TOK // rows,),
            in_specs=[pl.BlockSpec((rows, FEAT), lambda i, *_: (i, 0))] * 8
            + [whole(192, FEAT)] * 8
            + [whole(8, 1, FEAT)],
            out_specs=(
                pl.BlockSpec((4, rows, 2 * FEAT), lambda i, *_: (0, i, 0)),
                pl.BlockSpec((rows, 128), lambda i, *_: (i, 0)),
            ),
        ),
        compiler_params=vmem(20),
        name="norm_low",
    )(me, lengths, *blocks, *maps, gain)


BLOCK = 64
HALF = TOK // 2
SCALE2 = math.log2(math.e) / math.sqrt(HEAD)


def page_copies(place_ref, pages_ref, cached_ref, sems, base):
    copies = []
    for i in range(16):
        for h in range(2):
            into = cached_ref.at[h, i // 8, pl.ds(i % 8 * PAGE, PAGE)]
            copies.append(pltpu.make_async_copy(pages_ref.at[place_ref[i], h], into, sems.at[base + 2 * i + h]))
    return copies


def attend_half(half, length_ref, cache_ref, q_ref, kv_ref, cached_ref, out_ref, m_ref, l_ref, acc_ref):
    rows, span = GROUP * BLOCK, 256 + BLOCK
    prompts = prompt_rows(length_ref)
    begins = [start for start, _ in prompts]
    count, ranks = jnp.int32(0), []
    for p in range(PROMPTS):
        has = cache_ref[p] > 0
        ranks.append(jnp.where(has, count, -1))
        count = count + has.astype(jnp.int32)
    owners = []
    for j in range(2):
        mine = [(ranks[p] == j).astype(jnp.int32) for p in range(PROMPTS)]
        owners.append(
            (
                sum(mine[p] * prompts[p][0] for p in range(PROMPTS)),
                sum(mine[p] * prompts[p][1] for p in range(PROMPTS)),
                sum(mine[p] * cache_ref[p] for p in range(PROMPTS)),
            )
        )

    def block(t, carry):
        local = pl.multiple_of(t * BLOCK, BLOCK)
        start = local + half * HALF
        lo = pl.multiple_of(jnp.maximum(start - 256, 0), BLOCK)
        cut = pl.ds(local, BLOCK)
        q = q_ref[:, cut, :].reshape(rows, HEAD)
        token = start + (lax.broadcasted_iota(jnp.int32, (rows, 1), 0) & (BLOCK - 1))
        begin = per_token(prompts, begins, token)
        s = lax.dot_general(q, kv_ref[0, pl.ds(lo, span), :], (((1,), (1,)), ((), ())), preferred_element_type=F32)
        key = lo + lax.broadcasted_iota(jnp.int32, (rows, span), 1)
        s = jnp.where((key <= token) & (key >= begin), s, NEG)
        m = jnp.max(s, axis=1, keepdims=True)
        w = jnp.exp2((s - m) * SCALE2)
        m_ref[...] = m
        l_ref[...] = jnp.sum(w, axis=1, keepdims=True)
        acc_ref[...] = jnp.dot(w.astype(BF), kv_ref[1, pl.ds(lo, span), :], preferred_element_type=F32)

        def cached(j):
            first, last, length = owners[j]
            mine = (token >= first) & (token < last)
            s = lax.dot_general(q, cached_ref[0, j], (((1,), (1,)), ((), ())), preferred_element_type=F32)
            at = lax.broadcasted_iota(jnp.int32, (rows, 256), 1)
            head = jnp.where((at > length + token - first - WIN) | (at < SINKS), s[:, :256], NEG)
            at = WIN - PAGE + lax.broadcasted_iota(jnp.int32, (rows, PAGE), 1)
            tail = jnp.where(at < length, s[:, WIN - PAGE :], NEG)
            s = jnp.concatenate([head, s[:, 256 : WIN - PAGE], tail], axis=1)
            m_old = m_ref[...]
            m_new = jnp.where(mine, jnp.maximum(m_old, jnp.max(s, axis=1, keepdims=True)), m_old)
            fade = jnp.exp2((m_old - m_new) * SCALE2)
            w = jnp.exp2((s - jnp.where(mine, m_new, -NEG)) * SCALE2)
            m_ref[...] = m_new
            l_ref[...] = l_ref[...] * fade + jnp.sum(w, axis=1, keepdims=True)
            acc_ref[...] = acc_ref[...] * fade + jnp.dot(w.astype(BF), cached_ref[1, j], preferred_element_type=F32)

        for j in range(2):
            pl.when((owners[j][0] < start + BLOCK) & (owners[j][1] > start))(lambda j=j: cached(j))

        done = (acc_ref[...] * (1.0 / l_ref[...])).astype(BF)
        for h in range(GROUP):
            out_ref[cut, h * HEAD : (h + 1) * HEAD] = done[h * BLOCK : (h + 1) * BLOCK, :]
        return carry

    lax.fori_loop(0, HALF // BLOCK, block, 0)


ATTEND_SCRATCH = [
    pltpu.VMEM((GROUP * BLOCK, 1), F32),
    pltpu.VMEM((GROUP * BLOCK, 1), F32),
    pltpu.VMEM((GROUP * BLOCK, HEAD), F32),
    pltpu.VMEM((2, 2, WIN, HEAD), BF),
]


def first_body(
    length_ref, cache_ref, place_ref, adapter_ref, position_ref,
    normed_ref, w_ref, low_hbm, rope_hbm, gains_hbm, pages_ref,
    out_ref, q_late_ref, kv_ref,
    m_ref, l_ref, sum_ref, cached_ref, x, w, up, acc, q_early, low_ref, rope_ref, gains_ref, sems,
):
    def chunk(k):
        rows = w_ref.at[pl.ds(4 * k, 4), pl.ds(0, 256), pl.ds(0, 768)]
        return [
            pltpu.make_async_copy(normed_ref.at[k], x.at[k], sems.at[2 * k]),
            pltpu.make_async_copy(rows, w.at[k], sems.at[2 * k + 1]),
        ]

    chunks = [chunk(k) for k in range(4)]
    for copy in chunks[0]:
        copy.start()
    up[...] = jnp.zeros_like(up)
    maps = []
    for p in range(PROMPTS):
        slot = position_ref[adapter_ref[p]]
        q_part = w_ref.at[slot, pl.ds(256, 16), pl.ds(0, 512)]
        v_part = w_ref.at[slot, pl.ds(256, 16), pl.ds(512, HEAD)]
        maps.append(pltpu.make_async_copy(q_part, up.at[pl.ds(p * 32, 16), pl.ds(0, 512)], sems.at[8 + 2 * p]))
        maps.append(pltpu.make_async_copy(v_part, up.at[pl.ds(p * 32 + 16, 16), pl.ds(512, HEAD)], sems.at[9 + 2 * p]))
    maps.append(pltpu.make_async_copy(low_hbm, low_ref, sems.at[48]))
    maps.append(pltpu.make_async_copy(rope_hbm, rope_ref, sems.at[49]))
    maps.append(pltpu.make_async_copy(gains_hbm, gains_ref, sems.at[50]))
    for copy in chunks[1] + maps:
        copy.start()
    pages = page_copies(place_ref, pages_ref, cached_ref, sems, 16)
    for k in range(4):
        for copy in chunks[k]:
            copy.wait()
        if k + 2 < 4:
            for copy in chunks[k + 2]:
                copy.start()
        if k == 2:
            for copy in pages:
                copy.start()
        part = jnp.dot(x[k], w[k].reshape(1024, 768), preferred_element_type=F32)
        if k == 0:
            acc[...] = part
        else:
            acc[...] += part
    for copy in maps:
        copy.wait()
    change = 0.5 * jnp.dot(low_ref[...], up[...], preferred_element_type=F32)
    rope = rope_ref[...]
    front = lax.broadcasted_iota(jnp.int32, rope.shape, 1) < HEAD // 2
    swapped = pltpu.roll(rope, HEAD // 2, 1)
    cos, sin = jnp.where(front, rope, swapped), jnp.where(front, -swapped, rope)

    def finish(raw, gain):
        scale = lax.rsqrt(jnp.mean(raw * raw, axis=-1, keepdims=True) + EPSILON)
        x = raw * scale * gain
        return (x * cos + pltpu.roll(x, HEAD // 2, 1) * sin).astype(BF)

    for h in range(GROUP):
        cut = slice(h * HEAD, (h + 1) * HEAD)
        q = finish(acc[:, cut] + change[:, cut], gains_ref[0:1, :])
        q_early[h] = q[:HALF]
        q_late_ref[h] = q[HALF:]
    kv_ref[0] = finish(acc[:, 512:640], gains_ref[1:2, :])
    kv_ref[1] = (acc[:, 640:768] + change[:, 512:640]).astype(BF)
    for copy in pages:
        copy.wait()
    attend_half(0, length_ref, cache_ref, q_early, kv_ref, cached_ref, out_ref, m_ref, l_ref, sum_ref)


def first_half(lengths, cached, place, adapter, position, normed, weight, low, rope, gains, pages):
    hbm = pl.BlockSpec(memory_space=pl.ANY)
    return pl.pallas_call(
        first_body,
        out_shape=(
            jax.ShapeDtypeStruct((HALF, FEAT), BF),
            jax.ShapeDtypeStruct((GROUP, HALF, HEAD), BF),
            jax.ShapeDtypeStruct((2, TOK, HEAD), BF),
        ),
        grid_spec=pltpu.PrefetchScalarGridSpec(
            num_scalar_prefetch=5,
            grid=(1,),
            in_specs=[hbm] * 6,
            out_specs=(whole(HALF, FEAT), whole(GROUP, HALF, HEAD), whole(2, TOK, HEAD)),
            scratch_shapes=ATTEND_SCRATCH
            + [
                pltpu.VMEM((4, TOK, 1024), BF),
                pltpu.VMEM((4, 4, 256, 768), BF),
                pltpu.VMEM((128, 640), BF),
                pltpu.VMEM((TOK, 768), F32),
                pltpu.VMEM((GROUP, HALF, HEAD), BF),
                pltpu.VMEM((TOK, 128), BF),
                pltpu.VMEM((TOK, HEAD), F32),
                pltpu.VMEM((2, HEAD), F32),
                pltpu.SemaphoreType.DMA((51,)),
            ],
        ),
        compiler_params=vmem(32),
        name="first_half",
    )(
        lengths, cached, place, adapter, position,
        in_hbm(normed), in_hbm(weight), in_hbm(low), in_hbm(rope), in_hbm(gains), in_hbm(pages),
    )


def second_body(
    length_ref, cache_ref, place_ref, q_ref, kv_ref, pages_ref, out_ref, m_ref, l_ref, sum_ref, cached_ref, sems
):
    copies = page_copies(place_ref, pages_ref, cached_ref, sems, 0)
    for copy in copies:
        copy.start()
    for copy in copies:
        copy.wait()
    attend_half(1, length_ref, cache_ref, q_ref, kv_ref, cached_ref, out_ref, m_ref, l_ref, sum_ref)


def second_half(lengths, cached, place, q, kv, pages):
    return pl.pallas_call(
        second_body,
        out_shape=jax.ShapeDtypeStruct((HALF, FEAT), BF),
        grid_spec=pltpu.PrefetchScalarGridSpec(
            num_scalar_prefetch=3,
            grid=(1,),
            in_specs=[whole(GROUP, HALF, HEAD), whole(2, TOK, HEAD), pl.BlockSpec(memory_space=pl.ANY)],
            out_specs=whole(HALF, FEAT),
            scratch_shapes=ATTEND_SCRATCH + [pltpu.SemaphoreType.DMA((32,))],
        ),
        compiler_params=vmem(12),
        name="second_half",
    )(lengths, cached, place, q, kv, in_hbm(pages))


def out_body(half, me_ref, length_ref, adapter_ref, position_ref, *refs):
    blocks, maps = refs[:8], refs[8:16]
    weight_ref, hidden_ref = refs[16:18]
    out_ref, w, oup, sems = refs[-4:]
    order = col_order(me_ref[1])
    copies = []
    for b in range(8):
        rows = weight_ref.at[pl.ds(2 * order[b], 2), pl.ds(0, 256), pl.ds(768, FEAT)]
        copies.append(pltpu.make_async_copy(rows, w.at[b], sems.at[b]))
    for p in range(PROMPTS):
        slot = position_ref[adapter_ref[p]]
        rows = weight_ref.at[slot, pl.ds(256, 16), pl.ds(640, FEAT)]
        copies.append(pltpu.make_async_copy(rows, oup.at[pl.ds(p * 16, 16)], sems.at[8 + p]))
    for copy in copies:
        copy.start()
    low = jnp.zeros((HALF, 64), F32)
    for b in range(8):
        low += lax.dot_general(
            blocks[b][...], maps[b][128:192, :], (((1,), (1,)), ((), ())), preferred_element_type=F32
        )
    token = half * HALF + lax.broadcasted_iota(jnp.int32, low.shape, 0)
    prompt = per_token(prompt_rows(length_ref), range(PROMPTS), token)
    mine = lax.broadcasted_iota(jnp.int32, low.shape, 1) // 16 == prompt
    low = jnp.where(mine, low, 0.0)
    total = hidden_ref[...].astype(F32)
    for b in range(8):
        copies[b].wait()
        total += jnp.dot(blocks[b][...], w[b].reshape(FEAT, FEAT), preferred_element_type=F32)
    for copy in copies[8:]:
        copy.wait()
    change = jnp.dot(low, oup[...].astype(F32), precision=lax.Precision.HIGHEST, preferred_element_type=F32)
    out_ref[...] = (total + 0.5 * change).astype(BF)


def output(half, me, lengths, adapter, position, blocks, maps, weight, hidden, earlier=None):
    tok = pl.BlockSpec((HALF, FEAT), lambda i, *_: (half, 0))
    hbm = pl.BlockSpec(memory_space=pl.ANY)
    late = () if earlier is None else (earlier,)
    return pl.pallas_call(
        lambda *refs: out_body(half, *refs),
        out_shape=jax.ShapeDtypeStruct((TOK, FEAT), BF),
        grid_spec=pltpu.PrefetchScalarGridSpec(
            num_scalar_prefetch=4,
            grid=(1,),
            in_specs=[whole(HALF, FEAT)] * 8 + [whole(192, FEAT)] * 8 + [hbm, tok] + [hbm] * len(late),
            out_specs=tok,
            scratch_shapes=[
                pltpu.VMEM((8, 2, 256, FEAT), BF),
                pltpu.VMEM((64, FEAT), BF),
                pltpu.SemaphoreType.DMA((12,)),
            ],
        ),
        input_output_aliases={} if earlier is None else {22: 0},
        compiler_params=vmem(24),
        name="output_late" if late else "output_early",
    )(me, lengths, adapter, position, *blocks, *maps, in_hbm(weight), hidden, *late)


def on_device(
    hidden_input,
    input_norm_gain,
    query_norm_gain,
    key_norm_gain,
    query_key_value_weight,
    output_weight,
    adapter_down_maps,
    adapter_up_maps,
    output_down_maps,
    output_up_maps,
    prompt_adapter,
    adapter_position,
    prompt_length,
    cache_length,
    page_owner_row,
    page_store_index,
    cache_page_store,
):
    me = jnp.stack([lax.axis_index("row"), lax.axis_index("col")]).astype(jnp.int32)
    wide, slots = pack(
        me,
        query_key_value_weight,
        output_weight,
        adapter_up_maps,
        output_up_maps,
        adapter_down_maps,
        output_down_maps,
    )
    weight = lax.all_gather(wide, "row", axis=0)
    slots = lax.all_to_all(slots, "row", 0, 0)

    picked, place = pick_pages(me, page_owner_row, page_store_index, cache_page_store)
    picked, slots = lax.optimization_barrier((picked, slots))
    pages = lax.all_to_all(picked.reshape(16, 4 * PAGE, HEAD), "row", 0, 0).reshape(32, 2, PAGE, HEAD)

    blocks = gather_col(hidden_input, 256)

    maps = select_slots(prompt_adapter, adapter_position, slots)
    maps = gather_col(maps, 96)

    token = lax.broadcasted_iota(jnp.int32, (TOK, HEAD), 0)
    position, start = token, jnp.int32(0)
    for p in range(PROMPTS):
        end = start + prompt_length[0, p]
        position = jnp.where((token >= start) & (token < end), token - start + cache_length[p], position)
        start = end
    frequency = ROPE_BASE ** (-2.0 * jnp.arange(HEAD // 2, dtype=F32) / HEAD)
    angles = position.astype(F32) * jnp.concatenate([frequency, frequency])[None, :]
    front = lax.broadcasted_iota(jnp.int32, (TOK, HEAD), 1) < HEAD // 2
    rope = jnp.where(front, jnp.cos(angles), jnp.sin(angles))

    normed, low = norm_low(me, prompt_length, blocks, maps, input_norm_gain.reshape(8, 1, FEAT))
    gains = jnp.stack([query_norm_gain, key_norm_gain]).astype(F32)
    weight, normed, low, pages, rope, gains = lax.optimization_barrier((weight, normed, low, pages, rope, gains))
    early, q, new_cache = first_half(
        prompt_length,
        cache_length,
        place,
        prompt_adapter,
        adapter_position,
        normed,
        weight,
        low,
        rope,
        gains,
        pages,
    )
    quarter = HALF // 2
    other = swap(early)
    before = lax.ppermute(early, "col", perm_z(1))
    after = lax.ppermute(early, "col", perm_z(-1))
    q, other = lax.optimization_barrier((q, other))
    late = second_half(prompt_length, cache_length, place, q, new_cache, pages)
    before, after, late = lax.optimization_barrier((before, after, late))
    far = ring_far(before, after, "col", perm_z, quarter)
    early = [early, other, before, swap(before), after, swap(after), far, swap(far)]

    common = (me, prompt_length, prompt_adapter, adapter_position)
    hidden_output = output(0, *common, early, maps, weight, hidden_input)
    before, after, far = ring4(late, "col", perm_z, quarter)
    far, hidden_output = lax.optimization_barrier((far, hidden_output))
    late = [late, swap(late), before, swap(before), after, swap(after), far, swap(far)]
    hidden_output = output(1, *common, late, maps, weight, hidden_input, hidden_output)
    return hidden_output, new_cache


def solution(mesh):
    return jax.shard_map(
        on_device,
        mesh=mesh,
        in_specs=(
            P("row", "col"),
            P(),
            P(),
            P(),
            P("row", "col"),
            P("row", "col"),
            P("row", None, None),
            P("row", None, "col"),
            P("row", None, "col"),
            P("row", None, None),
            P("row"),
            P(),
            P("row", None),
            P("row"),
            P(),
            P(),
            P("row", None, None, "col"),
        ),
        out_specs=(P("row", "col"), P(None, "row", "col")),
        check_vma=False,
    )
```

```python
import math

import jax
import jax.numpy as jnp
from jax import lax
from jax.experimental import pallas as pl
from jax.experimental.pallas import tpu as pltpu
from jax.sharding import PartitionSpec as P

HEAD = 128
GROUP = 4
WIN = 1024
SINKS = 4
PAGE = 128
EPSILON = 1e-06
ROPE_BASE = 1000000.0
TOK = 512
FEAT = 512
PROMPTS = 4
BF = jnp.bfloat16
F32 = jnp.float32
NEG = -1e30


def perm_x(k):
    return [(i, (i // 4 + k) % 4 * 4 + i % 4) for i in range(16)]


def perm_y(k):
    return [(i, i // 4 * 4 + (i % 4 + k) % 4) for i in range(16)]


def perm_z(k):
    return [(i, (i // 2 + k) % 4 * 2 + i % 2) for i in range(8)]


SWAP = [(i, i ^ 1) for i in range(8)]


def ring_far(before, after, axis, perm, half):
    return lax.ppermute(before[:half], axis, perm(1)), lax.ppermute(after[half:], axis, perm(-1))


def ring4(block, axis, perm, half):
    before = lax.ppermute(block, axis, perm(1))
    after = lax.ppermute(block, axis, perm(-1))
    return before, after, jnp.concatenate(ring_far(before, after, axis, perm, half), axis=0)


def swap(block):
    return lax.ppermute(block, "col", SWAP)


def gather_col(block, half):
    out = [block, swap(block)]
    for piece in ring4(block, "col", perm_z, half):
        out += [piece, swap(piece)]
    return out


def col_order(col):
    chip, core = col // 2, col % 2
    return [lax.rem(chip + d, 4) * 2 + lax.rem(core + s, 2) for d in (0, 3, 1, 2) for s in (0, 1)]


def prompt_rows(length_ref):
    start, rows = jnp.int32(0), []
    for p in range(PROMPTS):
        rows.append((start, start + length_ref[0, p]))
        start = start + length_ref[0, p]
    return rows


def per_token(rows, values, token, default=0):
    out = jnp.full(token.shape, default, jnp.int32)
    for (start, end), value in zip(rows, values):
        out = jnp.where((token >= start) & (token < end), value, out)
    return out


def in_hbm(x):
    return pltpu.with_memory_space_constraint(x, pltpu.HBM)


def vmem(n):
    return pltpu.CompilerParams(vmem_limit_bytes=n << 20)


def whole(*shape):
    return pl.BlockSpec(shape, lambda *_: (0,) * len(shape))


def pick_body(me_ref, owner_ref, index_ref, store_ref, out_ref, place_ref):
    def group(r, carry):
        first, second, count = jnp.int32(0), jnp.int32(0), jnp.int32(0)
        for q in range(16):
            hit = owner_ref[r * 16 + q, 0] == me_ref[0]
            index = index_ref[r * 16 + q]
            first = jnp.where(hit & (count == 0), index, first)
            second = jnp.where(hit & (count == 1), index, second)
            count = count + hit.astype(jnp.int32)
        out_ref[r, 0] = store_ref[first]
        out_ref[r, 1] = store_ref[second]
        return carry

    lax.fori_loop(0, 16, group, 0)
    for i in range(16):
        holder, rank = owner_ref[me_ref[0] * 16 + i, 0], jnp.int32(0)
        for k in range(i):
            rank = jnp.where(owner_ref[me_ref[0] * 16 + k, 0] == holder, 1, rank)
        place_ref[i] = holder * 2 + rank


def pick_pages(me, owner, index, store):
    return pl.pallas_call(
        pick_body,
        out_shape=(
            jax.ShapeDtypeStruct((16, 2) + store.shape[1:], store.dtype),
            jax.ShapeDtypeStruct((16,), jnp.int32),
        ),
        grid_spec=pltpu.PrefetchScalarGridSpec(
            num_scalar_prefetch=3,
            grid=(1,),
            in_specs=[whole(*store.shape)],
            out_specs=(whole(16, 2, *store.shape[1:]), pl.BlockSpec(memory_space=pltpu.SMEM)),
        ),
        compiler_params=vmem(10),
        name="pick_pages",
    )(me, owner, index, store)


def pack_body(me_ref, qkv_ref, wo_ref, up_ref, oup_ref, down_ref, odown_ref, wide_ref, rest_ref, slots_ref):
    wide_ref[:256, :768] = qkv_ref[...]
    wide_ref[:256, 768:] = wo_ref[:, :256]
    wide_ref[256:, :640] = up_ref[0]
    wide_ref[256:, 640:] = jnp.zeros((16, 384), BF)
    rest_ref[:256, :] = wo_ref[:, 256:]
    rest_ref[256:272, :] = oup_ref[0, :, :256]
    rest_ref[272:, :] = oup_ref[0, :, 256:]
    for r in range(16):
        slots_ref[r, :32, :] = down_ref[0]
        slots_ref[r, 32:, :] = odown_ref[0]


def pack(me, qkv, wo, up, oup, down, odown):
    return pl.pallas_call(
        pack_body,
        out_shape=(
            jax.ShapeDtypeStruct((272, 1024), BF),
            jax.ShapeDtypeStruct((288, 256), BF),
            jax.ShapeDtypeStruct((16, 48, FEAT), BF),
        ),
        grid_spec=pltpu.PrefetchScalarGridSpec(
            num_scalar_prefetch=1,
            grid=(1,),
            in_specs=[
                whole(256, 768),
                whole(256, FEAT),
                whole(1, 16, 640),
                pl.BlockSpec((1, 16, FEAT), lambda i, me: (0, 0, me[1])),
                pl.BlockSpec((1, 32, FEAT), lambda i, me: (0, 0, me[1])),
                whole(1, 16, FEAT),
            ],
            out_specs=(whole(272, 1024), whole(288, 256), whole(16, 48, FEAT)),
        ),
        name="pack",
    )(me, qkv, wo, up, oup, down, odown)


def select_body(adapter_ref, position_ref, slots_ref, maps_ref):
    for p in range(PROMPTS):
        slot = position_ref[adapter_ref[p]]
        maps_ref[p * 32 : p * 32 + 32, :] = slots_ref[slot, :32, :]
        maps_ref[128 + p * 16 : 128 + p * 16 + 16, :] = slots_ref[slot, 32:, :]


def select_slots(adapter, position, slots):
    return pl.pallas_call(
        select_body,
        out_shape=jax.ShapeDtypeStruct((192, FEAT), BF),
        grid_spec=pltpu.PrefetchScalarGridSpec(
            num_scalar_prefetch=2,
            grid=(1,),
            in_specs=[whole(16, 48, FEAT)],
            out_specs=whole(192, FEAT),
        ),
        name="select_slots",
    )(adapter, position, slots)


def norm_body(me_ref, length_ref, *refs):
    blocks, maps = refs[:8], refs[8:16]
    gain_ref, normed_ref, low_ref = refs[16:]
    order = col_order(me_ref[1])
    values = [b[...].astype(F32) for b in blocks]
    total = sum(jnp.sum(v * v, axis=-1, keepdims=True) for v in values)
    scale = lax.rsqrt(total * (1.0 / (8 * FEAT)) + EPSILON)
    low = jnp.zeros(low_ref.shape, F32)
    for b in range(8):
        gain = gain_ref[order[b]].astype(F32)
        normed = (values[b] * scale * gain).astype(BF)
        normed_ref[order[b] // 2, :, pl.ds(pl.multiple_of(order[b] % 2 * FEAT, FEAT), FEAT)] = normed
        low += lax.dot_general(normed, maps[b][:128, :], (((1,), (1,)), ((), ())), preferred_element_type=F32)
    token = pl.program_id(0) * low.shape[0] + lax.broadcasted_iota(jnp.int32, low.shape, 0)
    prompt = per_token(prompt_rows(length_ref), range(PROMPTS), token)
    mine = lax.broadcasted_iota(jnp.int32, low.shape, 1) // 32 == prompt
    low_ref[...] = jnp.where(mine, low, 0.0).astype(BF)


def norm_low(me, lengths, blocks, maps, gain):
    rows = 128
    return pl.pallas_call(
        norm_body,
        out_shape=(pltpu.HBM((4, TOK, 2 * FEAT), BF), pltpu.HBM((TOK, 128), BF)),
        grid_spec=pltpu.PrefetchScalarGridSpec(
            num_scalar_prefetch=2,
            grid=(TOK // rows,),
            in_specs=[pl.BlockSpec((rows, FEAT), lambda i, *_: (i, 0))] * 8
            + [whole(192, FEAT)] * 8
            + [whole(8, 1, FEAT)],
            out_specs=(
                pl.BlockSpec((4, rows, 2 * FEAT), lambda i, *_: (0, i, 0)),
                pl.BlockSpec((rows, 128), lambda i, *_: (i, 0)),
            ),
        ),
        compiler_params=vmem(20),
        name="norm_low",
    )(me, lengths, *blocks, *maps, gain)


BLOCK = 64
HALF = TOK // 2
SCALE2 = math.log2(math.e) / math.sqrt(HEAD)


def page_copies(place_ref, pages_ref, cached_ref, sems, base):
    copies = []
    for i in range(16):
        for h in range(2):
            into = cached_ref.at[h, i // 8, pl.ds(i % 8 * PAGE, PAGE)]
            copies.append(pltpu.make_async_copy(pages_ref.at[place_ref[i], h], into, sems.at[base + 2 * i + h]))
    return copies


def attend_half(half, length_ref, cache_ref, q_ref, kv_ref, cached_ref, out_ref, m_ref, l_ref, acc_ref):
    rows, span = GROUP * BLOCK, 256 + BLOCK
    prompts = prompt_rows(length_ref)
    begins = [start for start, _ in prompts]
    count, ranks = jnp.int32(0), []
    for p in range(PROMPTS):
        has = cache_ref[p] > 0
        ranks.append(jnp.where(has, count, -1))
        count = count + has.astype(jnp.int32)
    owners = []
    for j in range(2):
        mine = [(ranks[p] == j).astype(jnp.int32) for p in range(PROMPTS)]
        owners.append(
            (
                sum(mine[p] * prompts[p][0] for p in range(PROMPTS)),
                sum(mine[p] * prompts[p][1] for p in range(PROMPTS)),
                sum(mine[p] * cache_ref[p] for p in range(PROMPTS)),
            )
        )

    def block(t, carry):
        local = pl.multiple_of(t * BLOCK, BLOCK)
        start = local + half * HALF
        lo = pl.multiple_of(jnp.maximum(start - 256, 0), BLOCK)
        cut = pl.ds(local, BLOCK)
        q = q_ref[:, cut, :].reshape(rows, HEAD)
        token = start + (lax.broadcasted_iota(jnp.int32, (rows, 1), 0) & (BLOCK - 1))
        begin = per_token(prompts, begins, token)
        s = lax.dot_general(q, kv_ref[0, pl.ds(lo, span), :], (((1,), (1,)), ((), ())), preferred_element_type=F32)
        key = lo + lax.broadcasted_iota(jnp.int32, (rows, span), 1)
        s = jnp.where((key <= token) & (key >= begin), s, NEG)
        m = jnp.max(s, axis=1, keepdims=True)
        w = jnp.exp2((s - m) * SCALE2)
        m_ref[...] = m
        l_ref[...] = jnp.sum(w, axis=1, keepdims=True)
        acc_ref[...] = jnp.dot(w.astype(BF), kv_ref[1, pl.ds(lo, span), :], preferred_element_type=F32)

        def cached(j):
            first, last, length = owners[j]
            mine = (token >= first) & (token < last)
            s = lax.dot_general(q, cached_ref[0, j], (((1,), (1,)), ((), ())), preferred_element_type=F32)
            at = lax.broadcasted_iota(jnp.int32, (rows, 256), 1)
            head = jnp.where((at > length + token - first - WIN) | (at < SINKS), s[:, :256], NEG)
            at = WIN - PAGE + lax.broadcasted_iota(jnp.int32, (rows, PAGE), 1)
            tail = jnp.where(at < length, s[:, WIN - PAGE :], NEG)
            s = jnp.concatenate([head, s[:, 256 : WIN - PAGE], tail], axis=1)
            m_old = m_ref[...]
            m_new = jnp.where(mine, jnp.maximum(m_old, jnp.max(s, axis=1, keepdims=True)), m_old)
            fade = jnp.exp2((m_old - m_new) * SCALE2)
            w = jnp.exp2((s - jnp.where(mine, m_new, -NEG)) * SCALE2)
            m_ref[...] = m_new
            l_ref[...] = l_ref[...] * fade + jnp.sum(w, axis=1, keepdims=True)
            acc_ref[...] = acc_ref[...] * fade + jnp.dot(w.astype(BF), cached_ref[1, j], preferred_element_type=F32)

        for j in range(2):
            pl.when((owners[j][0] < start + BLOCK) & (owners[j][1] > start))(lambda j=j: cached(j))

        done = (acc_ref[...] * (1.0 / l_ref[...])).astype(BF)
        for h in range(GROUP):
            out_ref[cut, h * HEAD : (h + 1) * HEAD] = done[h * BLOCK : (h + 1) * BLOCK, :]
        return carry

    lax.fori_loop(0, HALF // BLOCK, block, 0)


ATTEND_SCRATCH = [
    pltpu.VMEM((GROUP * BLOCK, 1), F32),
    pltpu.VMEM((GROUP * BLOCK, 1), F32),
    pltpu.VMEM((GROUP * BLOCK, HEAD), F32),
    pltpu.VMEM((2, 2, WIN, HEAD), BF),
]


def first_body(
    length_ref, cache_ref, place_ref, adapter_ref, position_ref,
    normed_ref, w_ref, low_hbm, rope_hbm, gains_hbm, pages_ref,
    out_ref, q_late_ref, kv_ref,
    m_ref, l_ref, sum_ref, cached_ref, x, w, up, acc, q_early, low_ref, rope_ref, gains_ref, sems,
):
    def chunk(k):
        rows = w_ref.at[pl.ds(4 * k, 4), pl.ds(0, 256), pl.ds(0, 768)]
        return [
            pltpu.make_async_copy(normed_ref.at[k], x.at[k], sems.at[2 * k]),
            pltpu.make_async_copy(rows, w.at[k], sems.at[2 * k + 1]),
        ]

    chunks = [chunk(k) for k in range(4)]
    for copy in chunks[0]:
        copy.start()
    up[...] = jnp.zeros_like(up)
    maps = []
    for p in range(PROMPTS):
        slot = position_ref[adapter_ref[p]]
        q_part = w_ref.at[slot, pl.ds(256, 16), pl.ds(0, 512)]
        v_part = w_ref.at[slot, pl.ds(256, 16), pl.ds(512, HEAD)]
        maps.append(pltpu.make_async_copy(q_part, up.at[pl.ds(p * 32, 16), pl.ds(0, 512)], sems.at[8 + 2 * p]))
        maps.append(pltpu.make_async_copy(v_part, up.at[pl.ds(p * 32 + 16, 16), pl.ds(512, HEAD)], sems.at[9 + 2 * p]))
    maps.append(pltpu.make_async_copy(low_hbm, low_ref, sems.at[48]))
    maps.append(pltpu.make_async_copy(rope_hbm, rope_ref, sems.at[49]))
    maps.append(pltpu.make_async_copy(gains_hbm, gains_ref, sems.at[50]))
    for copy in chunks[1] + maps:
        copy.start()
    pages = page_copies(place_ref, pages_ref, cached_ref, sems, 16)
    for k in range(4):
        for copy in chunks[k]:
            copy.wait()
        if k + 2 < 4:
            for copy in chunks[k + 2]:
                copy.start()
        if k == 2:
            for copy in pages:
                copy.start()
        part = jnp.dot(x[k], w[k].reshape(1024, 768), preferred_element_type=F32)
        if k == 0:
            acc[...] = part
        else:
            acc[...] += part
    for copy in maps:
        copy.wait()
    change = 0.5 * jnp.dot(low_ref[...], up[...], preferred_element_type=F32)
    rope = rope_ref[...]
    front = lax.broadcasted_iota(jnp.int32, rope.shape, 1) < HEAD // 2
    swapped = pltpu.roll(rope, HEAD // 2, 1)
    cos, sin = jnp.where(front, rope, swapped), jnp.where(front, -swapped, rope)

    def finish(raw, gain):
        scale = lax.rsqrt(jnp.mean(raw * raw, axis=-1, keepdims=True) + EPSILON)
        x = raw * scale * gain
        return (x * cos + pltpu.roll(x, HEAD // 2, 1) * sin).astype(BF)

    for h in range(GROUP):
        cut = slice(h * HEAD, (h + 1) * HEAD)
        q = finish(acc[:, cut] + change[:, cut], gains_ref[0:1, :])
        q_early[h] = q[:HALF]
        q_late_ref[h] = q[HALF:]
    kv_ref[0] = finish(acc[:, 512:640], gains_ref[1:2, :])
    kv_ref[1] = (acc[:, 640:768] + change[:, 512:640]).astype(BF)
    for copy in pages:
        copy.wait()
    attend_half(0, length_ref, cache_ref, q_early, kv_ref, cached_ref, out_ref, m_ref, l_ref, sum_ref)


def first_half(lengths, cached, place, adapter, position, normed, weight, low, rope, gains, pages):
    hbm = pl.BlockSpec(memory_space=pl.ANY)
    return pl.pallas_call(
        first_body,
        out_shape=(
            jax.ShapeDtypeStruct((HALF, FEAT), BF),
            jax.ShapeDtypeStruct((GROUP, HALF, HEAD), BF),
            jax.ShapeDtypeStruct((2, TOK, HEAD), BF),
        ),
        grid_spec=pltpu.PrefetchScalarGridSpec(
            num_scalar_prefetch=5,
            grid=(1,),
            in_specs=[hbm] * 6,
            out_specs=(whole(HALF, FEAT), whole(GROUP, HALF, HEAD), whole(2, TOK, HEAD)),
            scratch_shapes=ATTEND_SCRATCH
            + [
                pltpu.VMEM((4, TOK, 1024), BF),
                pltpu.VMEM((4, 4, 256, 768), BF),
                pltpu.VMEM((128, 640), BF),
                pltpu.VMEM((TOK, 768), F32),
                pltpu.VMEM((GROUP, HALF, HEAD), BF),
                pltpu.VMEM((TOK, 128), BF),
                pltpu.VMEM((TOK, HEAD), F32),
                pltpu.VMEM((2, HEAD), F32),
                pltpu.SemaphoreType.DMA((51,)),
            ],
        ),
        compiler_params=vmem(32),
        name="first_half",
    )(
        lengths, cached, place, adapter, position,
        in_hbm(normed), in_hbm(weight), in_hbm(low), in_hbm(rope), in_hbm(gains), in_hbm(pages),
    )


def second_body(
    length_ref, cache_ref, place_ref, q_ref, kv_ref, pages_ref, out_ref, m_ref, l_ref, sum_ref, cached_ref, sems
):
    copies = page_copies(place_ref, pages_ref, cached_ref, sems, 0)
    for copy in copies:
        copy.start()
    for copy in copies:
        copy.wait()
    attend_half(1, length_ref, cache_ref, q_ref, kv_ref, cached_ref, out_ref, m_ref, l_ref, sum_ref)


def second_half(lengths, cached, place, q, kv, pages):
    return pl.pallas_call(
        second_body,
        out_shape=jax.ShapeDtypeStruct((HALF, FEAT), BF),
        grid_spec=pltpu.PrefetchScalarGridSpec(
            num_scalar_prefetch=3,
            grid=(1,),
            in_specs=[whole(GROUP, HALF, HEAD), whole(2, TOK, HEAD), pl.BlockSpec(memory_space=pl.ANY)],
            out_specs=whole(HALF, FEAT),
            scratch_shapes=ATTEND_SCRATCH + [pltpu.SemaphoreType.DMA((32,))],
        ),
        compiler_params=vmem(12),
        name="second_half",
    )(lengths, cached, place, q, kv, in_hbm(pages))


def out_body(half, me_ref, length_ref, adapter_ref, position_ref, *refs):
    blocks = [ref[...] for ref in refs[:6]] + [jnp.concatenate([refs[i][...], refs[i + 1][...]], axis=0) for i in (6, 8)]
    maps = refs[10:18]
    weight_ref, rest_ref, hidden_ref = refs[18:21]
    out_ref, w, oup, sems = refs[-4:]
    order = col_order(me_ref[1])
    copies = []
    for b in range(8):
        for n, ref in enumerate((weight_ref.at[:, :, pl.ds(768, 256)], rest_ref)):
            rows = ref.at[pl.ds(2 * order[b], 2), pl.ds(0, 256)]
            copies.append(pltpu.make_async_copy(rows, w.at[n, b], sems.at[2 * b + n]))
    for p in range(PROMPTS):
        slot = position_ref[adapter_ref[p]]
        for n in range(2):
            rows = rest_ref.at[slot, pl.ds(256 + 16 * n, 16)]
            into = oup.at[pl.ds(p * 16, 16), pl.ds(256 * n, 256)]
            copies.append(pltpu.make_async_copy(rows, into, sems.at[16 + 2 * p + n]))
    for copy in copies:
        copy.start()
    low = jnp.zeros((HALF, 64), F32)
    for b in range(8):
        low += lax.dot_general(
            blocks[b], maps[b][128:192, :], (((1,), (1,)), ((), ())), preferred_element_type=F32
        )
    token = half * HALF + lax.broadcasted_iota(jnp.int32, low.shape, 0)
    prompt = per_token(prompt_rows(length_ref), range(PROMPTS), token)
    mine = lax.broadcasted_iota(jnp.int32, low.shape, 1) // 16 == prompt
    low = jnp.where(mine, low, 0.0)
    total = hidden_ref[...].astype(F32)
    for b in range(8):
        parts = []
        for n in range(2):
            copies[2 * b + n].wait()
            parts.append(jnp.dot(blocks[b], w[n, b].reshape(FEAT, 256), preferred_element_type=F32))
        total += jnp.concatenate(parts, axis=1)
    for copy in copies[16:]:
        copy.wait()
    change = jnp.dot(low, oup[...].astype(F32), precision=lax.Precision.HIGHEST, preferred_element_type=F32)
    out_ref[...] = (total + 0.5 * change).astype(BF)


def output(half, me, lengths, adapter, position, blocks, maps, weight, rest, hidden, earlier=None):
    tok = pl.BlockSpec((HALF, FEAT), lambda i, *_: (half, 0))
    hbm = pl.BlockSpec(memory_space=pl.ANY)
    late = () if earlier is None else (earlier,)
    return pl.pallas_call(
        lambda *refs: out_body(half, *refs),
        out_shape=jax.ShapeDtypeStruct((TOK, FEAT), BF),
        grid_spec=pltpu.PrefetchScalarGridSpec(
            num_scalar_prefetch=4,
            grid=(1,),
            in_specs=[whole(HALF, FEAT)] * 6
            + [whole(HALF // 2, FEAT)] * 4
            + [whole(192, FEAT)] * 8
            + [hbm, hbm, tok]
            + [hbm] * len(late),
            out_specs=tok,
            scratch_shapes=[
                pltpu.VMEM((2, 8, 2, 256, 256), BF),
                pltpu.VMEM((64, FEAT), BF),
                pltpu.SemaphoreType.DMA((24,)),
            ],
        ),
        input_output_aliases={} if earlier is None else {25: 0},
        compiler_params=vmem(24),
        name="output_late" if late else "output_early",
    )(
        me, lengths, adapter, position,
        *map(in_hbm, blocks), *map(in_hbm, maps), in_hbm(weight), in_hbm(rest), in_hbm(hidden), *late,
    )


def on_device(
    hidden_input,
    input_norm_gain,
    query_norm_gain,
    key_norm_gain,
    query_key_value_weight,
    output_weight,
    adapter_down_maps,
    adapter_up_maps,
    output_down_maps,
    output_up_maps,
    prompt_adapter,
    adapter_position,
    prompt_length,
    cache_length,
    page_owner_row,
    page_store_index,
    cache_page_store,
):
    me = jnp.stack([lax.axis_index("row"), lax.axis_index("col")]).astype(jnp.int32)
    wide, rest, slots = pack(
        me,
        query_key_value_weight,
        output_weight,
        adapter_up_maps,
        output_up_maps,
        adapter_down_maps,
        output_down_maps,
    )
    weight = lax.all_gather(wide, "row", axis=0)
    slots = lax.all_to_all(slots, "row", 0, 0)

    picked, place = pick_pages(me, page_owner_row, page_store_index, cache_page_store)
    picked, slots, rest = lax.optimization_barrier((picked, slots, rest))
    rest = lax.all_gather(rest, "row", axis=0)
    pages = lax.all_to_all(picked.reshape(16, 4 * PAGE, HEAD), "row", 0, 0).reshape(32, 2, PAGE, HEAD)

    blocks = gather_col(hidden_input, 256)

    maps = select_slots(prompt_adapter, adapter_position, slots)
    maps = gather_col(maps, 96)

    token = lax.broadcasted_iota(jnp.int32, (TOK, HEAD), 0)
    position, start = token, jnp.int32(0)
    for p in range(PROMPTS):
        end = start + prompt_length[0, p]
        position = jnp.where((token >= start) & (token < end), token - start + cache_length[p], position)
        start = end
    frequency = ROPE_BASE ** (-2.0 * jnp.arange(HEAD // 2, dtype=F32) / HEAD)
    angles = position.astype(F32) * jnp.concatenate([frequency, frequency])[None, :]
    front = lax.broadcasted_iota(jnp.int32, (TOK, HEAD), 1) < HEAD // 2
    rope = jnp.where(front, jnp.cos(angles), jnp.sin(angles))

    normed, low = norm_low(me, prompt_length, blocks, maps, input_norm_gain.reshape(8, 1, FEAT))
    gains = jnp.stack([query_norm_gain, key_norm_gain]).astype(F32)
    weight, normed, low, pages, rope, gains = lax.optimization_barrier((weight, normed, low, pages, rope, gains))
    early, q, new_cache = first_half(
        prompt_length,
        cache_length,
        place,
        prompt_adapter,
        adapter_position,
        normed,
        weight,
        low,
        rope,
        gains,
        pages,
    )
    quarter = HALF // 2
    other = swap(early)
    before = lax.ppermute(early, "col", perm_z(1))
    after = lax.ppermute(early, "col", perm_z(-1))
    q, other = lax.optimization_barrier((q, other))
    late = second_half(prompt_length, cache_length, place, q, new_cache, pages)
    before, after, late = lax.optimization_barrier((before, after, late))
    low_far, high_far = ring_far(before, after, "col", perm_z, quarter)
    early = [early, other, before, swap(before), after, swap(after), low_far, high_far, swap(low_far), swap(high_far)]

    common = (me, prompt_length, prompt_adapter, adapter_position)
    hidden_output = output(0, *common, early, maps, weight, rest, hidden_input)
    before = lax.ppermute(late, "col", perm_z(1))
    after = lax.ppermute(late, "col", perm_z(-1))
    low_far, high_far = ring_far(before, after, "col", perm_z, quarter)
    low_far, high_far, hidden_output = lax.optimization_barrier((low_far, high_far, hidden_output))
    late = [late, swap(late), before, swap(before), after, swap(after), low_far, high_far, swap(low_far), swap(high_far)]
    hidden_output = output(1, *common, late, maps, weight, rest, hidden_input, hidden_output)
    return hidden_output, new_cache


def solution(mesh):
    return jax.shard_map(
        on_device,
        mesh=mesh,
        in_specs=(
            P("row", "col"),
            P(),
            P(),
            P(),
            P("row", "col"),
            P("row", "col"),
            P("row", None, None),
            P("row", None, "col"),
            P("row", None, "col"),
            P("row", None, None),
            P("row"),
            P(),
            P("row", None),
            P("row"),
            P(),
            P(),
            P("row", None, None, "col"),
        ),
        out_specs=(P("row", "col"), P(None, "row", "col")),
        check_vma=False,
    )
```

```python
import math

import jax
import jax.numpy as jnp
from jax import lax
from jax.experimental import pallas as pl
from jax.experimental.pallas import tpu as pltpu
from jax.sharding import PartitionSpec as P

HEAD = 128
GROUP = 4
WIN = 1024
SINKS = 4
PAGE = 128
EPSILON = 1e-06
ROPE_BASE = 1000000.0
TOK = 512
FEAT = 512
PROMPTS = 4
BF = jnp.bfloat16
F32 = jnp.float32
NEG = -1e30


def perm_x(k):
    return [(i, (i // 4 + k) % 4 * 4 + i % 4) for i in range(16)]


def perm_y(k):
    return [(i, i // 4 * 4 + (i % 4 + k) % 4) for i in range(16)]


def perm_z(k):
    return [(i, (i // 2 + k) % 4 * 2 + i % 2) for i in range(8)]


SWAP = [(i, i ^ 1) for i in range(8)]


def ring_far(before, after, axis, perm, half):
    return lax.ppermute(before[:half], axis, perm(1)), lax.ppermute(after[half:], axis, perm(-1))


def ring4(block, axis, perm, half):
    before = lax.ppermute(block, axis, perm(1))
    after = lax.ppermute(block, axis, perm(-1))
    return before, after, jnp.concatenate(ring_far(before, after, axis, perm, half), axis=0)


def swap(block):
    return lax.ppermute(block, "col", SWAP)


def gather_col(block, half):
    out = [block, swap(block)]
    for piece in ring4(block, "col", perm_z, half):
        out += [piece, swap(piece)]
    return out


def col_order(col):
    chip, core = col // 2, col % 2
    return [lax.rem(chip + d, 4) * 2 + lax.rem(core + s, 2) for d in (0, 3, 1, 2) for s in (0, 1)]


def prompt_rows(length_ref):
    start, rows = jnp.int32(0), []
    for p in range(PROMPTS):
        rows.append((start, start + length_ref[0, p]))
        start = start + length_ref[0, p]
    return rows


def per_token(rows, values, token, default=0):
    out = jnp.full(token.shape, default, jnp.int32)
    for (start, end), value in zip(rows, values):
        out = jnp.where((token >= start) & (token < end), value, out)
    return out


def in_hbm(x):
    return pltpu.with_memory_space_constraint(x, pltpu.HBM)


def vmem(n):
    return pltpu.CompilerParams(vmem_limit_bytes=n << 20)


def whole(*shape):
    return pl.BlockSpec(shape, lambda *_: (0,) * len(shape))


def pick_body(me_ref, owner_ref, index_ref, store_ref, out_ref, place_ref):
    def group(r, carry):
        first, second, count = jnp.int32(0), jnp.int32(0), jnp.int32(0)
        for q in range(16):
            hit = owner_ref[r * 16 + q, 0] == me_ref[0]
            index = index_ref[r * 16 + q]
            first = jnp.where(hit & (count == 0), index, first)
            second = jnp.where(hit & (count == 1), index, second)
            count = count + hit.astype(jnp.int32)
        out_ref[r, 0] = store_ref[first]
        out_ref[r, 1] = store_ref[second]
        return carry

    lax.fori_loop(0, 16, group, 0)
    for i in range(16):
        holder, rank = owner_ref[me_ref[0] * 16 + i, 0], jnp.int32(0)
        for k in range(i):
            rank = jnp.where(owner_ref[me_ref[0] * 16 + k, 0] == holder, 1, rank)
        place_ref[i] = holder * 2 + rank


def pick_pages(me, owner, index, store):
    return pl.pallas_call(
        pick_body,
        out_shape=(
            jax.ShapeDtypeStruct((16, 2) + store.shape[1:], store.dtype),
            jax.ShapeDtypeStruct((16,), jnp.int32),
        ),
        grid_spec=pltpu.PrefetchScalarGridSpec(
            num_scalar_prefetch=3,
            grid=(1,),
            in_specs=[whole(*store.shape)],
            out_specs=(whole(16, 2, *store.shape[1:]), pl.BlockSpec(memory_space=pltpu.SMEM)),
        ),
        compiler_params=vmem(10),
        name="pick_pages",
    )(me, owner, index, store)


def pack_body(me_ref, qkv_ref, wo_ref, up_ref, oup_ref, down_ref, odown_ref, wide_ref, rest_ref, slots_ref):
    wide_ref[:256, :] = qkv_ref[...]
    wide_ref[256:, :640] = up_ref[0]
    wide_ref[256:, 640:] = jnp.zeros((16, 128), BF)
    rest_ref[:256, :] = wo_ref[...]
    rest_ref[256:, :] = oup_ref[0]
    for r in range(16):
        slots_ref[r, :32, :] = down_ref[0]
        slots_ref[r, 32:, :] = odown_ref[0]


def pack(me, qkv, wo, up, oup, down, odown):
    return pl.pallas_call(
        pack_body,
        out_shape=(
            jax.ShapeDtypeStruct((272, 768), BF),
            jax.ShapeDtypeStruct((272, FEAT), BF),
            jax.ShapeDtypeStruct((16, 48, FEAT), BF),
        ),
        grid_spec=pltpu.PrefetchScalarGridSpec(
            num_scalar_prefetch=1,
            grid=(1,),
            in_specs=[
                whole(256, 768),
                whole(256, FEAT),
                whole(1, 16, 640),
                pl.BlockSpec((1, 16, FEAT), lambda i, me: (0, 0, me[1])),
                pl.BlockSpec((1, 32, FEAT), lambda i, me: (0, 0, me[1])),
                whole(1, 16, FEAT),
            ],
            out_specs=(whole(272, 768), whole(272, FEAT), whole(16, 48, FEAT)),
        ),
        name="pack",
    )(me, qkv, wo, up, oup, down, odown)


DOWN, ODOWN, BLOCK_ROWS = TOK, TOK + 128, TOK + 192


def select_body(adapter_ref, position_ref, slots_ref, hidden_ref, out_ref):
    out_ref[:TOK, :] = hidden_ref[...]
    for p in range(PROMPTS):
        slot = position_ref[adapter_ref[p]]
        out_ref[DOWN + p * 32 : DOWN + p * 32 + 32, :] = slots_ref[slot, :32, :]
        out_ref[ODOWN + p * 16 : ODOWN + p * 16 + 16, :] = slots_ref[slot, 32:, :]


def select_slots(adapter, position, slots, hidden):
    return pl.pallas_call(
        select_body,
        out_shape=jax.ShapeDtypeStruct((BLOCK_ROWS, FEAT), BF),
        grid_spec=pltpu.PrefetchScalarGridSpec(
            num_scalar_prefetch=2,
            grid=(1,),
            in_specs=[whole(16, 48, FEAT), whole(TOK, FEAT)],
            out_specs=whole(BLOCK_ROWS, FEAT),
        ),
        name="select_slots",
    )(adapter, position, slots, hidden)


def norm_body(me_ref, length_ref, *refs):
    blocks, maps = refs[:8], refs[8:16]
    gain_ref, normed_ref, low_ref = refs[16:]
    order = col_order(me_ref[1])
    values = [b[...].astype(F32) for b in blocks]
    total = sum(jnp.sum(v * v, axis=-1, keepdims=True) for v in values)
    scale = lax.rsqrt(total * (1.0 / (8 * FEAT)) + EPSILON)
    low = jnp.zeros(low_ref.shape, F32)
    for b in range(8):
        gain = gain_ref[order[b]].astype(F32)
        normed = (values[b] * scale * gain).astype(BF)
        normed_ref[order[b] // 2, :, pl.ds(pl.multiple_of(order[b] % 2 * FEAT, FEAT), FEAT)] = normed
        low += lax.dot_general(normed, maps[b][...], (((1,), (1,)), ((), ())), preferred_element_type=F32)
    token = pl.program_id(0) * low.shape[0] + lax.broadcasted_iota(jnp.int32, low.shape, 0)
    prompt = per_token(prompt_rows(length_ref), range(PROMPTS), token)
    mine = lax.broadcasted_iota(jnp.int32, low.shape, 1) // 32 == prompt
    low_ref[...] = jnp.where(mine, low, 0.0).astype(BF)


def norm_low(me, lengths, blocks, gain):
    rows = 128
    return pl.pallas_call(
        norm_body,
        out_shape=(pltpu.HBM((4, TOK, 2 * FEAT), BF), pltpu.HBM((TOK, 128), BF)),
        grid_spec=pltpu.PrefetchScalarGridSpec(
            num_scalar_prefetch=2,
            grid=(TOK // rows,),
            in_specs=[pl.BlockSpec((rows, FEAT), lambda i, *_: (i, 0))] * 8
            + [pl.BlockSpec((128, FEAT), lambda i, *_: (DOWN // 128, 0))] * 8
            + [whole(8, 1, FEAT)],
            out_specs=(
                pl.BlockSpec((4, rows, 2 * FEAT), lambda i, *_: (0, i, 0)),
                pl.BlockSpec((rows, 128), lambda i, *_: (i, 0)),
            ),
        ),
        compiler_params=vmem(20),
        name="norm_low",
    )(me, lengths, *blocks, *blocks, gain)


BLOCK = 64
SCALE2 = math.log2(math.e) / math.sqrt(HEAD)


def page_copies(place_ref, pages_ref, cached_ref, sems, base):
    copies = []
    for i in range(16):
        for h in range(2):
            into = cached_ref.at[h, i // 8, pl.ds(i % 8 * PAGE, PAGE)]
            copies.append(pltpu.make_async_copy(pages_ref.at[place_ref[i], h], into, sems.at[base + 2 * i + h]))
    return copies


def attend(length_ref, cache_ref, q_ref, kv_ref, cached_ref, out_ref, m_ref, l_ref, acc_ref):
    rows, span = GROUP * BLOCK, 256 + BLOCK
    prompts = prompt_rows(length_ref)
    begins = [start for start, _ in prompts]
    count, ranks = jnp.int32(0), []
    for p in range(PROMPTS):
        has = cache_ref[p] > 0
        ranks.append(jnp.where(has, count, -1))
        count = count + has.astype(jnp.int32)
    owners = []
    for j in range(2):
        mine = [(ranks[p] == j).astype(jnp.int32) for p in range(PROMPTS)]
        owners.append(
            (
                sum(mine[p] * prompts[p][0] for p in range(PROMPTS)),
                sum(mine[p] * prompts[p][1] for p in range(PROMPTS)),
                sum(mine[p] * cache_ref[p] for p in range(PROMPTS)),
            )
        )

    def block(t, carry):
        start = pl.multiple_of(t * BLOCK, BLOCK)
        lo = pl.multiple_of(jnp.maximum(start - 256, 0), BLOCK)
        cut = pl.ds(start, BLOCK)
        q = q_ref[:, cut, :].reshape(rows, HEAD)
        token = start + (lax.broadcasted_iota(jnp.int32, (rows, 1), 0) & (BLOCK - 1))
        begin = per_token(prompts, begins, token)
        s = lax.dot_general(q, kv_ref[0, pl.ds(lo, span), :], (((1,), (1,)), ((), ())), preferred_element_type=F32)
        key = lo + lax.broadcasted_iota(jnp.int32, (rows, span), 1)
        s = jnp.where((key <= token) & (key >= begin), s, NEG)
        m = jnp.max(s, axis=1, keepdims=True)
        w = jnp.exp2((s - m) * SCALE2)
        m_ref[...] = m
        l_ref[...] = jnp.sum(w, axis=1, keepdims=True)
        acc_ref[...] = jnp.dot(w.astype(BF), kv_ref[1, pl.ds(lo, span), :], preferred_element_type=F32)

        def cached(j):
            first, last, length = owners[j]
            mine = (token >= first) & (token < last)
            s = lax.dot_general(q, cached_ref[0, j], (((1,), (1,)), ((), ())), preferred_element_type=F32)
            at = lax.broadcasted_iota(jnp.int32, (rows, 256), 1)
            head = jnp.where((at > length + token - first - WIN) | (at < SINKS), s[:, :256], NEG)
            at = WIN - PAGE + lax.broadcasted_iota(jnp.int32, (rows, PAGE), 1)
            tail = jnp.where(at < length, s[:, WIN - PAGE :], NEG)
            s = jnp.concatenate([head, s[:, 256 : WIN - PAGE], tail], axis=1)
            m_old = m_ref[...]
            m_new = jnp.where(mine, jnp.maximum(m_old, jnp.max(s, axis=1, keepdims=True)), m_old)
            fade = jnp.exp2((m_old - m_new) * SCALE2)
            w = jnp.exp2((s - jnp.where(mine, m_new, -NEG)) * SCALE2)
            m_ref[...] = m_new
            l_ref[...] = l_ref[...] * fade + jnp.sum(w, axis=1, keepdims=True)
            acc_ref[...] = acc_ref[...] * fade + jnp.dot(w.astype(BF), cached_ref[1, j], preferred_element_type=F32)

        for j in range(2):
            pl.when((owners[j][0] < start + BLOCK) & (owners[j][1] > start))(lambda j=j: cached(j))

        done = (acc_ref[...] * (1.0 / l_ref[...])).astype(BF)
        for h in range(GROUP):
            out_ref[cut, h * HEAD : (h + 1) * HEAD] = done[h * BLOCK : (h + 1) * BLOCK, :]
        return carry

    lax.fori_loop(0, TOK // BLOCK, block, 0)


ATTEND_SCRATCH = [
    pltpu.VMEM((GROUP * BLOCK, 1), F32),
    pltpu.VMEM((GROUP * BLOCK, 1), F32),
    pltpu.VMEM((GROUP * BLOCK, HEAD), F32),
    pltpu.VMEM((2, 2, WIN, HEAD), BF),
]


def attention_body(
    length_ref, cache_ref, place_ref, adapter_ref, position_ref,
    normed_ref, w_ref, low_hbm, rope_hbm, gains_hbm, pages_ref,
    out_ref, kv_ref,
    m_ref, l_ref, sum_ref, cached_ref, x, w, up, acc, q_ref, low_ref, rope_ref, gains_ref, sems,
):
    def chunk(k):
        rows = w_ref.at[pl.ds(4 * k, 4), pl.ds(0, 256), pl.ds(0, 768)]
        return [
            pltpu.make_async_copy(normed_ref.at[k], x.at[k], sems.at[2 * k]),
            pltpu.make_async_copy(rows, w.at[k], sems.at[2 * k + 1]),
        ]

    chunks = [chunk(k) for k in range(4)]
    for copy in chunks[0]:
        copy.start()
    up[...] = jnp.zeros_like(up)
    maps = []
    for p in range(PROMPTS):
        slot = position_ref[adapter_ref[p]]
        q_part = w_ref.at[slot, pl.ds(256, 16), pl.ds(0, 512)]
        v_part = w_ref.at[slot, pl.ds(256, 16), pl.ds(512, HEAD)]
        maps.append(pltpu.make_async_copy(q_part, up.at[pl.ds(p * 32, 16), pl.ds(0, 512)], sems.at[8 + 2 * p]))
        maps.append(pltpu.make_async_copy(v_part, up.at[pl.ds(p * 32 + 16, 16), pl.ds(512, HEAD)], sems.at[9 + 2 * p]))
    maps.append(pltpu.make_async_copy(low_hbm, low_ref, sems.at[48]))
    maps.append(pltpu.make_async_copy(rope_hbm, rope_ref, sems.at[49]))
    maps.append(pltpu.make_async_copy(gains_hbm, gains_ref, sems.at[50]))
    for copy in chunks[1] + maps:
        copy.start()
    pages = page_copies(place_ref, pages_ref, cached_ref, sems, 16)
    for k in range(4):
        for copy in chunks[k]:
            copy.wait()
        if k + 2 < 4:
            for copy in chunks[k + 2]:
                copy.start()
        if k == 2:
            for copy in pages:
                copy.start()
        part = jnp.dot(x[k], w[k].reshape(1024, 768), preferred_element_type=F32)
        if k == 0:
            acc[...] = part
        else:
            acc[...] += part
    for copy in maps:
        copy.wait()
    change = 0.5 * jnp.dot(low_ref[...], up[...], preferred_element_type=F32)
    rope = rope_ref[...]
    front = lax.broadcasted_iota(jnp.int32, rope.shape, 1) < HEAD // 2
    swapped = pltpu.roll(rope, HEAD // 2, 1)
    cos, sin = jnp.where(front, rope, swapped), jnp.where(front, -swapped, rope)

    def finish(raw, gain):
        scale = lax.rsqrt(jnp.mean(raw * raw, axis=-1, keepdims=True) + EPSILON)
        x = raw * scale * gain
        return (x * cos + pltpu.roll(x, HEAD // 2, 1) * sin).astype(BF)

    for h in range(GROUP):
        cut = slice(h * HEAD, (h + 1) * HEAD)
        q_ref[h] = finish(acc[:, cut] + change[:, cut], gains_ref[0:1, :])
    kv_ref[0] = finish(acc[:, 512:640], gains_ref[1:2, :])
    kv_ref[1] = (acc[:, 640:768] + change[:, 512:640]).astype(BF)
    for copy in pages:
        copy.wait()
    attend(length_ref, cache_ref, q_ref, kv_ref, cached_ref, out_ref, m_ref, l_ref, sum_ref)


def attention(lengths, cached, place, adapter, position, normed, weight, low, rope, gains, pages):
    hbm = pl.BlockSpec(memory_space=pl.ANY)
    return pl.pallas_call(
        attention_body,
        out_shape=(
            jax.ShapeDtypeStruct((TOK, FEAT), BF),
            jax.ShapeDtypeStruct((2, TOK, HEAD), BF),
        ),
        grid_spec=pltpu.PrefetchScalarGridSpec(
            num_scalar_prefetch=5,
            grid=(1,),
            in_specs=[hbm] * 6,
            out_specs=(whole(TOK, FEAT), whole(2, TOK, HEAD)),
            scratch_shapes=ATTEND_SCRATCH
            + [
                pltpu.VMEM((4, TOK, 1024), BF),
                pltpu.VMEM((4, 4, 256, 768), BF),
                pltpu.VMEM((128, 640), BF),
                pltpu.VMEM((TOK, 768), F32),
                pltpu.VMEM((GROUP, TOK, HEAD), BF),
                pltpu.VMEM((TOK, 128), BF),
                pltpu.VMEM((TOK, HEAD), F32),
                pltpu.VMEM((2, HEAD), F32),
                pltpu.SemaphoreType.DMA((51,)),
            ],
        ),
        compiler_params=vmem(32),
        name="attention",
    )(
        lengths, cached, place, adapter, position,
        in_hbm(normed), in_hbm(weight), in_hbm(low), in_hbm(rope), in_hbm(gains), in_hbm(pages),
    )


def out_body(
    me_ref, length_ref, adapter_ref, position_ref, *refs
):
    blocks, sources = refs[:8], refs[8:16]
    weight_ref, hidden_hbm, out_ref, x, w, od, oup, hidden, acc, sems = refs[16:]
    order = col_order(me_ref[1])
    copies = []
    for b in range(8):
        side = pl.ds(b % 2 * FEAT, FEAT)
        rows = weight_ref.at[pl.ds(2 * order[b], 2), pl.ds(0, 256)]
        copies.append(pltpu.make_async_copy(rows, w.at[b // 2, pl.ds(b % 2 * 2, 2)], sems.at[b]))
        copies.append(pltpu.make_async_copy(blocks[b], x.at[b // 2, :, side], sems.at[8 + b]))
        copies.append(pltpu.make_async_copy(sources[b].at[pl.ds(ODOWN, 64)], od.at[b // 2, :, side], sems.at[16 + b]))
    last = [pltpu.make_async_copy(hidden_hbm, hidden, sems.at[24])]
    for p in range(PROMPTS):
        slot = position_ref[adapter_ref[p]]
        rows = weight_ref.at[slot, pl.ds(256, 16)]
        last.append(pltpu.make_async_copy(rows, oup.at[pl.ds(p * 16, 16)], sems.at[25 + p]))
    for copy in copies + last:
        copy.start()
    low = jnp.zeros((TOK, 64), F32)
    for i in range(4):
        for copy in copies[6 * i : 6 * i + 6]:
            copy.wait()
        part = jnp.dot(x[i], w[i].reshape(2 * FEAT, FEAT), preferred_element_type=F32)
        if i == 0:
            acc[...] = part
        else:
            acc[...] += part
        low += lax.dot_general(x[i], od[i], (((1,), (1,)), ((), ())), preferred_element_type=F32)
    token = lax.broadcasted_iota(jnp.int32, low.shape, 0)
    prompt = per_token(prompt_rows(length_ref), range(PROMPTS), token)
    mine = lax.broadcasted_iota(jnp.int32, low.shape, 1) // 16 == prompt
    low = jnp.where(mine, low, 0.0)
    for copy in last:
        copy.wait()
    change = jnp.dot(low, oup[...].astype(F32), precision=lax.Precision.HIGHEST, preferred_element_type=F32)
    out_ref[...] = (hidden[...].astype(F32) + acc[...] + 0.5 * change).astype(BF)


def output(me, lengths, adapter, position, blocks, sources, weight, hidden):
    hbm = pl.BlockSpec(memory_space=pl.ANY)
    return pl.pallas_call(
        out_body,
        out_shape=jax.ShapeDtypeStruct((TOK, FEAT), BF),
        grid_spec=pltpu.PrefetchScalarGridSpec(
            num_scalar_prefetch=4,
            grid=(1,),
            in_specs=[hbm] * 18,
            out_specs=whole(TOK, FEAT),
            scratch_shapes=[
                pltpu.VMEM((4, TOK, 2 * FEAT), BF),
                pltpu.VMEM((4, 4, 256, FEAT), BF),
                pltpu.VMEM((4, 64, 2 * FEAT), BF),
                pltpu.VMEM((64, FEAT), BF),
                pltpu.VMEM((TOK, FEAT), BF),
                pltpu.VMEM((TOK, FEAT), F32),
                pltpu.SemaphoreType.DMA((29,)),
            ],
        ),
        compiler_params=vmem(24),
        name="output",
    )(
        me, lengths, adapter, position,
        *map(in_hbm, blocks), *map(in_hbm, sources), in_hbm(weight), in_hbm(hidden),
    )


def on_device(
    hidden_input,
    input_norm_gain,
    query_norm_gain,
    key_norm_gain,
    query_key_value_weight,
    output_weight,
    adapter_down_maps,
    adapter_up_maps,
    output_down_maps,
    output_up_maps,
    prompt_adapter,
    adapter_position,
    prompt_length,
    cache_length,
    page_owner_row,
    page_store_index,
    cache_page_store,
):
    me = jnp.stack([lax.axis_index("row"), lax.axis_index("col")]).astype(jnp.int32)
    wide, rest, slots = pack(
        me,
        query_key_value_weight,
        output_weight,
        adapter_up_maps,
        output_up_maps,
        adapter_down_maps,
        output_down_maps,
    )
    weight = lax.all_gather(wide, "row", axis=0)
    slots = lax.all_to_all(slots, "row", 0, 0)

    picked, place = pick_pages(me, page_owner_row, page_store_index, cache_page_store)
    picked, slots, rest = lax.optimization_barrier((picked, slots, rest))
    rest = lax.all_gather(rest, "row", axis=0)
    pages = lax.all_to_all(picked.reshape(16, 4 * PAGE, HEAD), "row", 0, 0).reshape(32, 2, PAGE, HEAD)

    blocks = gather_col(select_slots(prompt_adapter, adapter_position, slots, hidden_input), BLOCK_ROWS // 2)

    token = lax.broadcasted_iota(jnp.int32, (TOK, HEAD), 0)
    position, start = token, jnp.int32(0)
    for p in range(PROMPTS):
        end = start + prompt_length[0, p]
        position = jnp.where((token >= start) & (token < end), token - start + cache_length[p], position)
        start = end
    frequency = ROPE_BASE ** (-2.0 * jnp.arange(HEAD // 2, dtype=F32) / HEAD)
    angles = position.astype(F32) * jnp.concatenate([frequency, frequency])[None, :]
    front = lax.broadcasted_iota(jnp.int32, (TOK, HEAD), 1) < HEAD // 2
    rope = jnp.where(front, jnp.cos(angles), jnp.sin(angles))

    normed, low = norm_low(me, prompt_length, blocks, input_norm_gain.reshape(8, 1, FEAT))
    gains = jnp.stack([query_norm_gain, key_norm_gain]).astype(F32)
    weight, normed, low, pages, rope, gains = lax.optimization_barrier((weight, normed, low, pages, rope, gains))
    attended, new_cache = attention(
        prompt_length,
        cache_length,
        place,
        prompt_adapter,
        adapter_position,
        normed,
        weight,
        low,
        rope,
        gains,
        pages,
    )
    attended = gather_col(attended, 256)
    hidden_output = output(
        me, prompt_length, prompt_adapter, adapter_position, attended, blocks, rest, hidden_input
    )
    return hidden_output, new_cache


def solution(mesh):
    return jax.shard_map(
        on_device,
        mesh=mesh,
        in_specs=(
            P("row", "col"),
            P(),
            P(),
            P(),
            P("row", "col"),
            P("row", "col"),
            P("row", None, None),
            P("row", None, "col"),
            P("row", None, "col"),
            P("row", None, None),
            P("row"),
            P(),
            P("row", None),
            P("row"),
            P(),
            P(),
            P("row", None, None, "col"),
        ),
        out_specs=(P("row", "col"), P(None, "row", "col")),
        check_vma=False,
    )
```

```python
import math

import jax
import jax.numpy as jnp
from jax import lax
from jax.experimental import pallas as pl
from jax.experimental.pallas import tpu as pltpu
from jax.sharding import PartitionSpec as P

HEAD = 128
GROUP = 4
WIN = 1024
SINKS = 4
PAGE = 128
EPSILON = 1e-06
ROPE_BASE = 1000000.0
TOK = 512
FEAT = 512
PROMPTS = 4
BF = jnp.bfloat16
F32 = jnp.float32
NEG = -1e30


def perm_x(k):
    return [(i, (i // 4 + k) % 4 * 4 + i % 4) for i in range(16)]


def perm_y(k):
    return [(i, i // 4 * 4 + (i % 4 + k) % 4) for i in range(16)]


def perm_z(k):
    return [(i, (i // 2 + k) % 4 * 2 + i % 2) for i in range(8)]


SWAP = [(i, i ^ 1) for i in range(8)]


def ring_far(before, after, axis, perm, half):
    return lax.ppermute(before[:half], axis, perm(1)), lax.ppermute(after[half:], axis, perm(-1))


def ring4(block, axis, perm, half):
    before = lax.ppermute(block, axis, perm(1))
    after = lax.ppermute(block, axis, perm(-1))
    return before, after, jnp.concatenate(ring_far(before, after, axis, perm, half), axis=0)


def swap(block):
    return lax.ppermute(block, "col", SWAP)


def gather_col(block, half):
    out = [block, swap(block)]
    for piece in ring4(block, "col", perm_z, half):
        out += [piece, swap(piece)]
    return out


def col_order(col):
    chip, core = col // 2, col % 2
    return [lax.rem(chip + d, 4) * 2 + lax.rem(core + s, 2) for d in (0, 3, 1, 2) for s in (0, 1)]


def prompt_rows(length_ref):
    start, rows = jnp.int32(0), []
    for p in range(PROMPTS):
        rows.append((start, start + length_ref[0, p]))
        start = start + length_ref[0, p]
    return rows


def per_token(rows, values, token, default=0):
    out = jnp.full(token.shape, default, jnp.int32)
    for (start, end), value in zip(rows, values):
        out = jnp.where((token >= start) & (token < end), value, out)
    return out


def in_hbm(x):
    return pltpu.with_memory_space_constraint(x, pltpu.HBM)


def vmem(n):
    return pltpu.CompilerParams(vmem_limit_bytes=n << 20)


def whole(*shape):
    return pl.BlockSpec(shape, lambda *_: (0,) * len(shape))


def pick_body(me_ref, owner_ref, index_ref, store_ref, out_ref, place_ref):
    def group(r, carry):
        first, second, count = jnp.int32(0), jnp.int32(0), jnp.int32(0)
        for q in range(16):
            hit = owner_ref[r * 16 + q, 0] == me_ref[0]
            index = index_ref[r * 16 + q]
            first = jnp.where(hit & (count == 0), index, first)
            second = jnp.where(hit & (count == 1), index, second)
            count = count + hit.astype(jnp.int32)
        out_ref[r, 0] = store_ref[first]
        out_ref[r, 1] = store_ref[second]
        return carry

    lax.fori_loop(0, 16, group, 0)
    for i in range(16):
        holder, rank = owner_ref[me_ref[0] * 16 + i, 0], jnp.int32(0)
        for k in range(i):
            rank = jnp.where(owner_ref[me_ref[0] * 16 + k, 0] == holder, 1, rank)
        place_ref[i] = holder * 2 + rank


def pick_pages(me, owner, index, store):
    return pl.pallas_call(
        pick_body,
        out_shape=(
            jax.ShapeDtypeStruct((16, 2) + store.shape[1:], store.dtype),
            jax.ShapeDtypeStruct((16,), jnp.int32),
        ),
        grid_spec=pltpu.PrefetchScalarGridSpec(
            num_scalar_prefetch=3,
            grid=(1,),
            in_specs=[whole(*store.shape)],
            out_specs=(whole(16, 2, *store.shape[1:]), pl.BlockSpec(memory_space=pltpu.SMEM)),
        ),
        compiler_params=vmem(10),
        name="pick_pages",
    )(me, owner, index, store)


def pack_body(me_ref, wo_ref, up_ref, oup_ref, down_ref, odown_ref, rest_ref, slots_ref):
    rest_ref[:256, :] = wo_ref[...]
    rest_ref[256:, :] = oup_ref[0]
    for r in range(16):
        for j in range(4):
            slots_ref[r, j * 48 : j * 48 + 32, :] = down_ref[0, :, j * HEAD : (j + 1) * HEAD]
            slots_ref[r, j * 48 + 32 : j * 48 + 48, :] = odown_ref[0, :, j * HEAD : (j + 1) * HEAD]
        for j in range(5):
            slots_ref[r, 192 + j * 16 : 208 + j * 16, :] = up_ref[0, :, j * HEAD : (j + 1) * HEAD]


def pack(me, wo, up, oup, down, odown):
    return pl.pallas_call(
        pack_body,
        out_shape=(jax.ShapeDtypeStruct((272, FEAT), BF), jax.ShapeDtypeStruct((16, 272, HEAD), BF)),
        grid_spec=pltpu.PrefetchScalarGridSpec(
            num_scalar_prefetch=1,
            grid=(1,),
            in_specs=[
                whole(256, FEAT),
                whole(1, 16, 640),
                pl.BlockSpec((1, 16, FEAT), lambda i, me: (0, 0, me[1])),
                pl.BlockSpec((1, 32, FEAT), lambda i, me: (0, 0, me[1])),
                whole(1, 16, FEAT),
            ],
            out_specs=(whole(272, FEAT), whole(16, 272, HEAD)),
        ),
        name="pack",
    )(me, wo, up, oup, down, odown)


DOWN, ODOWN, BLOCK_ROWS = TOK, TOK + 128, TOK + 192


def select_body(adapter_ref, position_ref, slots_ref, hidden_ref, out_ref, up_ref):
    out_ref[:TOK, :] = hidden_ref[...]
    up_ref[...] = jnp.zeros_like(up_ref)
    for p in range(PROMPTS):
        slot = position_ref[adapter_ref[p]]
        for j in range(4):
            cut = slice(j * HEAD, (j + 1) * HEAD)
            out_ref[DOWN + p * 32 : DOWN + p * 32 + 32, cut] = slots_ref[slot, j * 48 : j * 48 + 32, :]
            out_ref[ODOWN + p * 16 : ODOWN + p * 16 + 16, cut] = slots_ref[slot, j * 48 + 32 : j * 48 + 48, :]
            up_ref[p * 32 : p * 32 + 16, cut] = slots_ref[slot, 192 + j * 16 : 208 + j * 16, :]
        up_ref[p * 32 + 16 : p * 32 + 32, 512:] = slots_ref[slot, 256:272, :]


def select_slots(adapter, position, slots, hidden):
    return pl.pallas_call(
        select_body,
        out_shape=(jax.ShapeDtypeStruct((BLOCK_ROWS, FEAT), BF), pltpu.HBM((128, 640), BF)),
        grid_spec=pltpu.PrefetchScalarGridSpec(
            num_scalar_prefetch=2,
            grid=(1,),
            in_specs=[whole(16, 272, HEAD), whole(TOK, FEAT)],
            out_specs=(whole(BLOCK_ROWS, FEAT), whole(128, 640)),
        ),
        name="select_slots",
    )(adapter, position, slots, hidden)


def norm_body(me_ref, length_ref, *refs):
    blocks, maps = refs[:8], refs[8:16]
    outs = refs[16:24]
    gain_ref, normed_ref, low_ref, turned_ref = refs[24:]
    order = col_order(me_ref[1])
    values = [b[...].astype(F32) for b in blocks]
    total = sum(jnp.sum(v * v, axis=-1, keepdims=True) for v in values)
    scale = lax.rsqrt(total * (1.0 / (8 * FEAT)) + EPSILON)
    low = jnp.zeros(low_ref.shape, F32)
    for b in range(8):
        gain = gain_ref[order[b]].astype(F32)
        normed = (values[b] * scale * gain).astype(BF)
        normed_ref[order[b] // 2, :, pl.ds(pl.multiple_of(order[b] % 2 * FEAT, FEAT), FEAT)] = normed
        low += lax.dot_general(normed, maps[b][...], (((1,), (1,)), ((), ())), preferred_element_type=F32)
    token = pl.program_id(0) * low.shape[0] + lax.broadcasted_iota(jnp.int32, low.shape, 0)
    prompt = per_token(prompt_rows(length_ref), range(PROMPTS), token)
    mine = lax.broadcasted_iota(jnp.int32, low.shape, 1) // 32 == prompt
    low_ref[...] = jnp.where(mine, low, 0.0).astype(BF)
    for k in range(4):

        @pl.when(pl.program_id(0) == k)
        def _():
            for b in range(2):
                down = outs[2 * k + b][...].astype(F32)
                turned = jnp.concatenate([down, down], axis=0).T.astype(BF)
                turned_ref[b, 0], turned_ref[b, 1] = turned[:256], turned[256:]


def norm_low(me, lengths, blocks, gain):
    rows = 128
    return pl.pallas_call(
        norm_body,
        out_shape=(
            pltpu.HBM((4, TOK, 2 * FEAT), BF),
            pltpu.HBM((TOK, 128), BF),
            pltpu.HBM((8, 2, 256, 128), BF),
        ),
        grid_spec=pltpu.PrefetchScalarGridSpec(
            num_scalar_prefetch=2,
            grid=(TOK // rows,),
            in_specs=[pl.BlockSpec((rows, FEAT), lambda i, *_: (i, 0))] * 8
            + [pl.BlockSpec((128, FEAT), lambda i, *_: (DOWN // 128, 0))] * 8
            + [pl.BlockSpec((64, FEAT), lambda i, *_: (ODOWN // 64, 0))] * 8
            + [whole(8, 1, FEAT)],
            out_specs=(
                pl.BlockSpec((4, rows, 2 * FEAT), lambda i, *_: (0, i, 0)),
                pl.BlockSpec((rows, 128), lambda i, *_: (i, 0)),
                pl.BlockSpec((2, 2, 256, 128), lambda i, *_: (i, 0, 0, 0)),
            ),
        ),
        compiler_params=vmem(20),
        name="norm_low",
    )(me, lengths, *blocks, *blocks, *blocks, gain)


BLOCK = 64
SCALE2 = math.log2(math.e) / math.sqrt(HEAD)


def page_copies(place_ref, pages_ref, cached_ref, sems, base):
    copies = []
    for i in range(16):
        for h in range(2):
            into = cached_ref.at[h, i // 8, pl.ds(i % 8 * PAGE, PAGE)]
            copies.append(pltpu.make_async_copy(pages_ref.at[place_ref[i], h], into, sems.at[base + 2 * i + h]))
    return copies


def attend(length_ref, cache_ref, q_ref, kv_ref, cached_ref, out_ref, m_ref, l_ref, acc_ref):
    rows, span = GROUP * BLOCK, 256 + BLOCK
    prompts = prompt_rows(length_ref)
    begins = [start for start, _ in prompts]
    count, ranks = jnp.int32(0), []
    for p in range(PROMPTS):
        has = cache_ref[p] > 0
        ranks.append(jnp.where(has, count, -1))
        count = count + has.astype(jnp.int32)
    owners = []
    for j in range(2):
        mine = [(ranks[p] == j).astype(jnp.int32) for p in range(PROMPTS)]
        owners.append(
            (
                sum(mine[p] * prompts[p][0] for p in range(PROMPTS)),
                sum(mine[p] * prompts[p][1] for p in range(PROMPTS)),
                sum(mine[p] * cache_ref[p] for p in range(PROMPTS)),
            )
        )

    def block(t, carry):
        start = pl.multiple_of(t * BLOCK, BLOCK)
        lo = pl.multiple_of(jnp.maximum(start - 256, 0), BLOCK)
        cut = pl.ds(start, BLOCK)
        q = q_ref[:, cut, :].reshape(rows, HEAD)
        token = start + (lax.broadcasted_iota(jnp.int32, (rows, 1), 0) & (BLOCK - 1))
        begin = per_token(prompts, begins, token)
        s = lax.dot_general(q, kv_ref[0, pl.ds(lo, span), :], (((1,), (1,)), ((), ())), preferred_element_type=F32)
        key = lo + lax.broadcasted_iota(jnp.int32, (rows, span), 1)
        s = jnp.where((key <= token) & (key >= begin), s, NEG)
        m = jnp.max(s, axis=1, keepdims=True)
        w = jnp.exp2((s - m) * SCALE2)
        m_ref[...] = m
        l_ref[...] = jnp.sum(w, axis=1, keepdims=True)
        acc_ref[...] = jnp.dot(w.astype(BF), kv_ref[1, pl.ds(lo, span), :], preferred_element_type=F32)

        def cached(j):
            first, last, length = owners[j]
            mine = (token >= first) & (token < last)
            s = lax.dot_general(q, cached_ref[0, j], (((1,), (1,)), ((), ())), preferred_element_type=F32)
            at = lax.broadcasted_iota(jnp.int32, (rows, 256), 1)
            head = jnp.where((at > length + token - first - WIN) | (at < SINKS), s[:, :256], NEG)
            at = WIN - PAGE + lax.broadcasted_iota(jnp.int32, (rows, PAGE), 1)
            tail = jnp.where(at < length, s[:, WIN - PAGE :], NEG)
            s = jnp.concatenate([head, s[:, 256 : WIN - PAGE], tail], axis=1)
            m_old = m_ref[...]
            m_new = jnp.where(mine, jnp.maximum(m_old, jnp.max(s, axis=1, keepdims=True)), m_old)
            fade = jnp.exp2((m_old - m_new) * SCALE2)
            w = jnp.exp2((s - jnp.where(mine, m_new, -NEG)) * SCALE2)
            m_ref[...] = m_new
            l_ref[...] = l_ref[...] * fade + jnp.sum(w, axis=1, keepdims=True)
            acc_ref[...] = acc_ref[...] * fade + jnp.dot(w.astype(BF), cached_ref[1, j], preferred_element_type=F32)

        for j in range(2):
            pl.when((owners[j][0] < start + BLOCK) & (owners[j][1] > start))(lambda j=j: cached(j))

        done = (acc_ref[...] * (1.0 / l_ref[...])).astype(BF)
        for h in range(GROUP):
            out_ref[cut, h * HEAD : (h + 1) * HEAD] = done[h * BLOCK : (h + 1) * BLOCK, :]
        return carry

    lax.fori_loop(0, TOK // BLOCK, block, 0)


ATTEND_SCRATCH = [
    pltpu.VMEM((GROUP * BLOCK, 1), F32),
    pltpu.VMEM((GROUP * BLOCK, 1), F32),
    pltpu.VMEM((GROUP * BLOCK, HEAD), F32),
    pltpu.VMEM((2, 2, WIN, HEAD), BF),
]


def attention_body(
    length_ref, cache_ref, place_ref,
    normed_ref, w_ref, up_hbm, low_hbm, rope_hbm, gains_hbm, pages_ref,
    out_ref, kv_ref,
    m_ref, l_ref, sum_ref, cached_ref, x, w, up, acc, q_ref, low_ref, rope_ref, gains_ref, sems,
):
    def chunk(k):
        rows = w_ref.at[pl.ds(4 * k, 4)]
        return [
            pltpu.make_async_copy(normed_ref.at[k], x.at[k], sems.at[2 * k]),
            pltpu.make_async_copy(rows, w.at[k], sems.at[2 * k + 1]),
        ]

    chunks = [chunk(k) for k in range(4)]
    for copy in chunks[0]:
        copy.start()
    maps = [pltpu.make_async_copy(up_hbm, up, sems.at[8])]
    maps.append(pltpu.make_async_copy(low_hbm, low_ref, sems.at[48]))
    maps.append(pltpu.make_async_copy(rope_hbm, rope_ref, sems.at[49]))
    maps.append(pltpu.make_async_copy(gains_hbm, gains_ref, sems.at[50]))
    for copy in chunks[1] + maps:
        copy.start()
    pages = page_copies(place_ref, pages_ref, cached_ref, sems, 16)
    for k in range(4):
        for copy in chunks[k]:
            copy.wait()
        if k + 2 < 4:
            for copy in chunks[k + 2]:
                copy.start()
        if k == 2:
            for copy in pages:
                copy.start()
        part = jnp.dot(x[k], w[k].reshape(1024, 768), preferred_element_type=F32)
        if k == 0:
            acc[...] = part
        else:
            acc[...] += part
    for copy in maps:
        copy.wait()
    change = 0.5 * jnp.dot(low_ref[...], up[...], preferred_element_type=F32)
    rope = rope_ref[...]
    front = lax.broadcasted_iota(jnp.int32, rope.shape, 1) < HEAD // 2
    swapped = pltpu.roll(rope, HEAD // 2, 1)
    cos, sin = jnp.where(front, rope, swapped), jnp.where(front, -swapped, rope)

    def finish(raw, gain):
        scale = lax.rsqrt(jnp.mean(raw * raw, axis=-1, keepdims=True) + EPSILON)
        x = raw * scale * gain
        return (x * cos + pltpu.roll(x, HEAD // 2, 1) * sin).astype(BF)

    for h in range(GROUP):
        cut = slice(h * HEAD, (h + 1) * HEAD)
        q_ref[h] = finish(acc[:, cut] + change[:, cut], gains_ref[0:1, :])
    kv_ref[0] = finish(acc[:, 512:640], gains_ref[1:2, :])
    kv_ref[1] = (acc[:, 640:768] + change[:, 512:640]).astype(BF)
    for copy in pages:
        copy.wait()
    attend(length_ref, cache_ref, q_ref, kv_ref, cached_ref, out_ref, m_ref, l_ref, sum_ref)


def attention(lengths, cached, place, normed, weight, up, low, rope, gains, pages):
    hbm = pl.BlockSpec(memory_space=pl.ANY)
    return pl.pallas_call(
        attention_body,
        out_shape=(
            jax.ShapeDtypeStruct((TOK, FEAT), BF),
            jax.ShapeDtypeStruct((2, TOK, HEAD), BF),
        ),
        grid_spec=pltpu.PrefetchScalarGridSpec(
            num_scalar_prefetch=3,
            grid=(1,),
            in_specs=[hbm] * 7,
            out_specs=(whole(TOK, FEAT), whole(2, TOK, HEAD)),
            scratch_shapes=ATTEND_SCRATCH
            + [
                pltpu.VMEM((4, TOK, 1024), BF),
                pltpu.VMEM((4, 4, 256, 768), BF),
                pltpu.VMEM((128, 640), BF),
                pltpu.VMEM((TOK, 768), F32),
                pltpu.VMEM((GROUP, TOK, HEAD), BF),
                pltpu.VMEM((TOK, 128), BF),
                pltpu.VMEM((TOK, HEAD), F32),
                pltpu.VMEM((2, HEAD), F32),
                pltpu.SemaphoreType.DMA((51,)),
            ],
        ),
        compiler_params=vmem(32),
        name="attention",
    )(
        lengths, cached, place,
        in_hbm(normed), in_hbm(weight), in_hbm(up), in_hbm(low), in_hbm(rope), in_hbm(gains), in_hbm(pages),
    )


def out_body(me_ref, length_ref, adapter_ref, position_ref, *refs):
    blocks = refs[:8]
    turned_ref, weight_ref, hidden_hbm, out_ref, x, w, oup, hidden, acc, sems = refs[8:]
    order = col_order(me_ref[1])
    copies = []
    for b in range(8):
        part = w.at[b // 2, pl.ds(b % 2 * 2, 2)]
        rows = weight_ref.at[pl.ds(2 * order[b], 2), pl.ds(0, 256)]
        copies.append(pltpu.make_async_copy(rows, part.at[:, :, pl.ds(0, FEAT)], sems.at[b]))
        side = pl.ds(b % 2 * FEAT, FEAT)
        copies.append(pltpu.make_async_copy(blocks[b], x.at[b // 2, :, side], sems.at[8 + b]))
        copies.append(pltpu.make_async_copy(turned_ref.at[b], part.at[:, :, pl.ds(FEAT, 128)], sems.at[16 + b]))
    last = [pltpu.make_async_copy(hidden_hbm, hidden, sems.at[24])]
    for p in range(PROMPTS):
        slot = position_ref[adapter_ref[p]]
        rows = weight_ref.at[slot, pl.ds(256, 16)]
        last.append(pltpu.make_async_copy(rows, oup.at[pl.ds(p * 16, 16)], sems.at[25 + p]))
    for copy in copies + last:
        copy.start()
    for i in range(4):
        for copy in copies[6 * i : 6 * i + 6]:
            copy.wait()
        part = jnp.dot(x[i], w[i].reshape(2 * FEAT, FEAT + 128), preferred_element_type=F32)
        if i == 0:
            acc[...] = part
        else:
            acc[...] += part
    for copy in last:
        copy.wait()
    low = acc[:, FEAT:]
    token = lax.broadcasted_iota(jnp.int32, low.shape, 0)
    lane = lax.broadcasted_iota(jnp.int32, low.shape, 1)
    prompt = per_token(prompt_rows(length_ref), range(PROMPTS), token)
    low = jnp.where((lane & 63) // 16 == prompt, low, 0.0)
    high = low.astype(BF)
    rest = low - high.astype(F32)
    middle = rest.astype(BF)
    least = (rest - middle.astype(F32)).astype(BF)
    maps = jnp.concatenate([oup[...], oup[...]], axis=0)
    change = jnp.dot(jnp.where(lane < 64, high, middle), maps, preferred_element_type=F32)
    change += jnp.dot(jnp.where(lane < 64, least, jnp.zeros_like(least)), maps, preferred_element_type=F32)
    out_ref[...] = (hidden[...].astype(F32) + acc[:, :FEAT] + 0.5 * change).astype(BF)


def output(me, lengths, adapter, position, blocks, turned, weight, hidden):
    hbm = pl.BlockSpec(memory_space=pl.ANY)
    return pl.pallas_call(
        out_body,
        out_shape=jax.ShapeDtypeStruct((TOK, FEAT), BF),
        grid_spec=pltpu.PrefetchScalarGridSpec(
            num_scalar_prefetch=4,
            grid=(1,),
            in_specs=[hbm] * 11,
            out_specs=whole(TOK, FEAT),
            scratch_shapes=[
                pltpu.VMEM((4, TOK, 2 * FEAT), BF),
                pltpu.VMEM((4, 4, 256, FEAT + 128), BF),
                pltpu.VMEM((64, FEAT), BF),
                pltpu.VMEM((TOK, FEAT), BF),
                pltpu.VMEM((TOK, FEAT + 128), F32),
                pltpu.SemaphoreType.DMA((29,)),
            ],
        ),
        compiler_params=vmem(24),
        name="output",
    )(
        me, lengths, adapter, position,
        *map(in_hbm, blocks), in_hbm(turned), in_hbm(weight), in_hbm(hidden),
    )


def on_device(
    hidden_input,
    input_norm_gain,
    query_norm_gain,
    key_norm_gain,
    query_key_value_weight,
    output_weight,
    adapter_down_maps,
    adapter_up_maps,
    output_down_maps,
    output_up_maps,
    prompt_adapter,
    adapter_position,
    prompt_length,
    cache_length,
    page_owner_row,
    page_store_index,
    cache_page_store,
):
    me = jnp.stack([lax.axis_index("row"), lax.axis_index("col")]).astype(jnp.int32)
    weight = lax.all_gather(query_key_value_weight, "row", axis=0)
    rest, slots = pack(
        me, output_weight, adapter_up_maps, output_up_maps, adapter_down_maps, output_down_maps
    )
    slots = lax.all_to_all(slots, "row", 0, 0)

    picked, place = pick_pages(me, page_owner_row, page_store_index, cache_page_store)
    picked, slots, rest = lax.optimization_barrier((picked, slots, rest))
    rest = lax.all_gather(rest, "row", axis=0)
    pages = lax.all_to_all(picked.reshape(16, 4 * PAGE, HEAD), "row", 0, 0).reshape(32, 2, PAGE, HEAD)

    block, up = select_slots(prompt_adapter, adapter_position, slots, hidden_input)
    blocks = gather_col(block, BLOCK_ROWS // 2)

    token = lax.broadcasted_iota(jnp.int32, (TOK, HEAD), 0)
    position, start = token, jnp.int32(0)
    for p in range(PROMPTS):
        end = start + prompt_length[0, p]
        position = jnp.where((token >= start) & (token < end), token - start + cache_length[p], position)
        start = end
    frequency = ROPE_BASE ** (-2.0 * jnp.arange(HEAD // 2, dtype=F32) / HEAD)
    angles = position.astype(F32) * jnp.concatenate([frequency, frequency])[None, :]
    front = lax.broadcasted_iota(jnp.int32, (TOK, HEAD), 1) < HEAD // 2
    rope = jnp.where(front, jnp.cos(angles), jnp.sin(angles))

    normed, low, turned = norm_low(me, prompt_length, blocks, input_norm_gain.reshape(8, 1, FEAT))
    gains = jnp.stack([query_norm_gain, key_norm_gain]).astype(F32)
    weight, normed, low, pages, rope, gains = lax.optimization_barrier((weight, normed, low, pages, rope, gains))
    attended, new_cache = attention(
        prompt_length,
        cache_length,
        place,
        normed,
        weight,
        up,
        low,
        rope,
        gains,
        pages,
    )
    attended = gather_col(attended, 256)
    hidden_output = output(
        me, prompt_length, prompt_adapter, adapter_position, attended, turned, rest, hidden_input
    )
    return hidden_output, new_cache


def solution(mesh):
    return jax.shard_map(
        on_device,
        mesh=mesh,
        in_specs=(
            P("row", "col"),
            P(),
            P(),
            P(),
            P("row", "col"),
            P("row", "col"),
            P("row", None, None),
            P("row", None, "col"),
            P("row", None, "col"),
            P("row", None, None),
            P("row"),
            P(),
            P("row", None),
            P("row"),
            P(),
            P(),
            P("row", None, None, "col"),
        ),
        out_specs=(P("row", "col"), P(None, "row", "col")),
        check_vma=False,
    )
```

```python
import math

import jax
import jax.numpy as jnp
from jax import lax
from jax.experimental import pallas as pl
from jax.experimental.pallas import tpu as pltpu
from jax.sharding import PartitionSpec as P

HEAD = 128
GROUP = 4
WIN = 1024
SINKS = 4
PAGE = 128
EPSILON = 1e-06
ROPE_BASE = 1000000.0
TOK = 512
FEAT = 512
PROMPTS = 4
BF = jnp.bfloat16
F32 = jnp.float32
NEG = -1e30


def perm_x(k):
    return [(i, (i // 4 + k) % 4 * 4 + i % 4) for i in range(16)]


def perm_y(k):
    return [(i, i // 4 * 4 + (i % 4 + k) % 4) for i in range(16)]


def perm_z(k):
    return [(i, (i // 2 + k) % 4 * 2 + i % 2) for i in range(8)]


SWAP = [(i, i ^ 1) for i in range(8)]


def ring_far(before, after, axis, perm, half):
    return lax.ppermute(before[:half], axis, perm(1)), lax.ppermute(after[half:], axis, perm(-1))


def ring4(block, axis, perm, half):
    before = lax.ppermute(block, axis, perm(1))
    after = lax.ppermute(block, axis, perm(-1))
    return before, after, jnp.concatenate(ring_far(before, after, axis, perm, half), axis=0)


def swap(block):
    return lax.ppermute(block, "col", SWAP)


def gather_col(block, half):
    out = [block, swap(block)]
    for piece in ring4(block, "col", perm_z, half):
        out += [piece, swap(piece)]
    return out


def col_order(col):
    chip, core = col // 2, col % 2
    return [lax.rem(chip + d, 4) * 2 + lax.rem(core + s, 2) for d in (0, 3, 1, 2) for s in (0, 1)]


def prompt_rows(length_ref):
    start, rows = jnp.int32(0), []
    for p in range(PROMPTS):
        rows.append((start, start + length_ref[0, p]))
        start = start + length_ref[0, p]
    return rows


def per_token(rows, values, token, default=0):
    out = jnp.full(token.shape, default, jnp.int32)
    for (start, end), value in zip(rows, values):
        out = jnp.where((token >= start) & (token < end), value, out)
    return out


def in_hbm(x):
    return pltpu.with_memory_space_constraint(x, pltpu.HBM)


def vmem(n):
    return pltpu.CompilerParams(vmem_limit_bytes=n << 20)


def whole(*shape):
    return pl.BlockSpec(shape, lambda *_: (0,) * len(shape))


def pick_body(me_ref, owner_ref, index_ref, store_ref, out_ref, place_ref):
    def group(r, carry):
        first, second, count = jnp.int32(0), jnp.int32(0), jnp.int32(0)
        for q in range(16):
            hit = owner_ref[r * 16 + q, 0] == me_ref[0]
            index = index_ref[r * 16 + q]
            first = jnp.where(hit & (count == 0), index, first)
            second = jnp.where(hit & (count == 1), index, second)
            count = count + hit.astype(jnp.int32)
        out_ref[r, 0] = store_ref[first]
        out_ref[r, 1] = store_ref[second]
        return carry

    lax.fori_loop(0, 16, group, 0)
    for i in range(16):
        holder, rank = owner_ref[me_ref[0] * 16 + i, 0], jnp.int32(0)
        for k in range(i):
            rank = jnp.where(owner_ref[me_ref[0] * 16 + k, 0] == holder, 1, rank)
        place_ref[i] = holder * 2 + rank


def pick_pages(me, owner, index, store):
    return pl.pallas_call(
        pick_body,
        out_shape=(
            jax.ShapeDtypeStruct((16, 2) + store.shape[1:], store.dtype),
            jax.ShapeDtypeStruct((16,), jnp.int32),
        ),
        grid_spec=pltpu.PrefetchScalarGridSpec(
            num_scalar_prefetch=3,
            grid=(1,),
            in_specs=[whole(*store.shape)],
            out_specs=(whole(16, 2, *store.shape[1:]), pl.BlockSpec(memory_space=pltpu.SMEM)),
        ),
        compiler_params=vmem(10),
        name="pick_pages",
    )(me, owner, index, store)


def pack_body(me_ref, qkv_ref, wo_ref, up_ref, oup_ref, down_ref, odown_ref, wide_ref, rest_ref, slots_ref):
    wide_ref[:256, :] = qkv_ref[...]
    wide_ref[256:, :640] = up_ref[0]
    wide_ref[256:, 640:] = jnp.zeros((16, 128), BF)
    rest_ref[:256, :] = wo_ref[...]
    rest_ref[256:, :] = oup_ref[0]
    for r in range(16):
        slots_ref[r, :32, :] = down_ref[0]
        slots_ref[r, 32:, :] = odown_ref[0]


def pack(me, qkv, wo, up, oup, down, odown):
    return pl.pallas_call(
        pack_body,
        out_shape=(
            jax.ShapeDtypeStruct((272, 768), BF),
            jax.ShapeDtypeStruct((272, FEAT), BF),
            jax.ShapeDtypeStruct((16, 48, FEAT), BF),
        ),
        grid_spec=pltpu.PrefetchScalarGridSpec(
            num_scalar_prefetch=1,
            grid=(1,),
            in_specs=[
                whole(256, 768),
                whole(256, FEAT),
                whole(1, 16, 640),
                pl.BlockSpec((1, 16, FEAT), lambda i, me: (0, 0, me[1])),
                pl.BlockSpec((1, 32, FEAT), lambda i, me: (0, 0, me[1])),
                whole(1, 16, FEAT),
            ],
            out_specs=(whole(272, 768), whole(272, FEAT), whole(16, 48, FEAT)),
        ),
        name="pack",
    )(me, qkv, wo, up, oup, down, odown)


DOWN, ODOWN, BLOCK_ROWS = TOK, TOK + 128, TOK + 192


def select_body(adapter_ref, position_ref, slots_ref, hidden_ref, out_ref):
    out_ref[:TOK, :] = hidden_ref[...]
    for p in range(PROMPTS):
        slot = position_ref[adapter_ref[p]]
        out_ref[DOWN + p * 32 : DOWN + p * 32 + 32, :] = slots_ref[slot, :32, :]
        out_ref[ODOWN + p * 16 : ODOWN + p * 16 + 16, :] = slots_ref[slot, 32:, :]


def select_slots(adapter, position, slots, hidden):
    return pl.pallas_call(
        select_body,
        out_shape=jax.ShapeDtypeStruct((BLOCK_ROWS, FEAT), BF),
        grid_spec=pltpu.PrefetchScalarGridSpec(
            num_scalar_prefetch=2,
            grid=(1,),
            in_specs=[whole(16, 48, FEAT), whole(TOK, FEAT)],
            out_specs=whole(BLOCK_ROWS, FEAT),
        ),
        name="select_slots",
    )(adapter, position, slots, hidden)


def norm_body(me_ref, length_ref, *refs):
    blocks, maps = refs[:8], refs[8:16]
    outs = refs[16:24]
    gain_ref, normed_ref, low_ref, turned_ref = refs[24:]
    order = col_order(me_ref[1])
    values = [b[...].astype(F32) for b in blocks]
    total = sum(jnp.sum(v * v, axis=-1, keepdims=True) for v in values)
    scale = lax.rsqrt(total * (1.0 / (8 * FEAT)) + EPSILON)
    low = jnp.zeros(low_ref.shape, F32)
    for b in range(8):
        gain = gain_ref[order[b]].astype(F32)
        normed = (values[b] * scale * gain).astype(BF)
        normed_ref[order[b] // 2, :, pl.ds(pl.multiple_of(order[b] % 2 * FEAT, FEAT), FEAT)] = normed
        low += lax.dot_general(normed, maps[b][...], (((1,), (1,)), ((), ())), preferred_element_type=F32)
    token = pl.program_id(0) * low.shape[0] + lax.broadcasted_iota(jnp.int32, low.shape, 0)
    prompt = per_token(prompt_rows(length_ref), range(PROMPTS), token)
    mine = lax.broadcasted_iota(jnp.int32, low.shape, 1) // 32 == prompt
    low_ref[...] = jnp.where(mine, low, 0.0).astype(BF)
    for k in range(4):

        @pl.when(pl.program_id(0) == k)
        def _():
            for b in range(2):
                down = outs[2 * k + b][...].astype(F32)
                turned = jnp.concatenate([down, down], axis=0).T.astype(BF)
                turned_ref[b, 0], turned_ref[b, 1] = turned[:256], turned[256:]


def norm_low(me, lengths, blocks, gain):
    rows = 128
    return pl.pallas_call(
        norm_body,
        out_shape=(
            pltpu.HBM((4, TOK, 2 * FEAT), BF),
            pltpu.HBM((TOK, 128), BF),
            pltpu.HBM((8, 2, 256, 128), BF),
        ),
        grid_spec=pltpu.PrefetchScalarGridSpec(
            num_scalar_prefetch=2,
            grid=(TOK // rows,),
            in_specs=[pl.BlockSpec((rows, FEAT), lambda i, *_: (i, 0))] * 8
            + [pl.BlockSpec((128, FEAT), lambda i, *_: (DOWN // 128, 0))] * 8
            + [pl.BlockSpec((64, FEAT), lambda i, *_: (ODOWN // 64, 0))] * 8
            + [whole(8, 1, FEAT)],
            out_specs=(
                pl.BlockSpec((4, rows, 2 * FEAT), lambda i, *_: (0, i, 0)),
                pl.BlockSpec((rows, 128), lambda i, *_: (i, 0)),
                pl.BlockSpec((2, 2, 256, 128), lambda i, *_: (i, 0, 0, 0)),
            ),
        ),
        compiler_params=vmem(20),
        name="norm_low",
    )(me, lengths, *blocks, *blocks, *blocks, gain)


BLOCK = 64
SCALE2 = math.log2(math.e) / math.sqrt(HEAD)


def page_copies(place_ref, pages_ref, cached_ref, sems, base):
    copies = []
    for i in range(16):
        for h in range(2):
            into = cached_ref.at[h, i // 8, pl.ds(i % 8 * PAGE, PAGE)]
            copies.append(pltpu.make_async_copy(pages_ref.at[place_ref[i], h], into, sems.at[base + 2 * i + h]))
    return copies


def attend(length_ref, cache_ref, q_ref, kv_ref, cached_ref, out_ref, m_ref, l_ref, acc_ref):
    rows, span = GROUP * BLOCK, 256 + BLOCK
    prompts = prompt_rows(length_ref)
    begins = [start for start, _ in prompts]
    count, ranks = jnp.int32(0), []
    for p in range(PROMPTS):
        has = cache_ref[p] > 0
        ranks.append(jnp.where(has, count, -1))
        count = count + has.astype(jnp.int32)
    owners = []
    for j in range(2):
        mine = [(ranks[p] == j).astype(jnp.int32) for p in range(PROMPTS)]
        owners.append(
            (
                sum(mine[p] * prompts[p][0] for p in range(PROMPTS)),
                sum(mine[p] * prompts[p][1] for p in range(PROMPTS)),
                sum(mine[p] * cache_ref[p] for p in range(PROMPTS)),
            )
        )

    def block(t, carry):
        start = pl.multiple_of(t * BLOCK, BLOCK)
        lo = pl.multiple_of(jnp.maximum(start - 256, 0), BLOCK)
        cut = pl.ds(start, BLOCK)
        q = q_ref[:, cut, :].reshape(rows, HEAD)
        token = start + (lax.broadcasted_iota(jnp.int32, (rows, 1), 0) & (BLOCK - 1))
        begin = per_token(prompts, begins, token)
        s = lax.dot_general(q, kv_ref[0, pl.ds(lo, span), :], (((1,), (1,)), ((), ())), preferred_element_type=F32)
        key = lo + lax.broadcasted_iota(jnp.int32, (rows, span), 1)
        s = jnp.where((key <= token) & (key >= begin), s, NEG)
        m = jnp.max(s, axis=1, keepdims=True)
        w = jnp.exp2((s - m) * SCALE2)
        m_ref[...] = m
        l_ref[...] = jnp.sum(w, axis=1, keepdims=True)
        acc_ref[...] = jnp.dot(w.astype(BF), kv_ref[1, pl.ds(lo, span), :], preferred_element_type=F32)

        def cached(j):
            first, last, length = owners[j]
            mine = (token >= first) & (token < last)
            s = lax.dot_general(q, cached_ref[0, j], (((1,), (1,)), ((), ())), preferred_element_type=F32)
            at = lax.broadcasted_iota(jnp.int32, (rows, 256), 1)
            head = jnp.where((at > length + token - first - WIN) | (at < SINKS), s[:, :256], NEG)
            at = WIN - PAGE + lax.broadcasted_iota(jnp.int32, (rows, PAGE), 1)
            tail = jnp.where(at < length, s[:, WIN - PAGE :], NEG)
            s = jnp.concatenate([head, s[:, 256 : WIN - PAGE], tail], axis=1)
            m_old = m_ref[...]
            m_new = jnp.where(mine, jnp.maximum(m_old, jnp.max(s, axis=1, keepdims=True)), m_old)
            fade = jnp.exp2((m_old - m_new) * SCALE2)
            w = jnp.exp2((s - jnp.where(mine, m_new, -NEG)) * SCALE2)
            m_ref[...] = m_new
            l_ref[...] = l_ref[...] * fade + jnp.sum(w, axis=1, keepdims=True)
            acc_ref[...] = acc_ref[...] * fade + jnp.dot(w.astype(BF), cached_ref[1, j], preferred_element_type=F32)

        for j in range(2):
            pl.when((owners[j][0] < start + BLOCK) & (owners[j][1] > start))(lambda j=j: cached(j))

        done = (acc_ref[...] * (1.0 / l_ref[...])).astype(BF)
        for h in range(GROUP):
            out_ref[cut, h * HEAD : (h + 1) * HEAD] = done[h * BLOCK : (h + 1) * BLOCK, :]
        return carry

    lax.fori_loop(0, TOK // BLOCK, block, 0)


ATTEND_SCRATCH = [
    pltpu.VMEM((GROUP * BLOCK, 1), F32),
    pltpu.VMEM((GROUP * BLOCK, 1), F32),
    pltpu.VMEM((GROUP * BLOCK, HEAD), F32),
    pltpu.VMEM((2, 2, WIN, HEAD), BF),
]


def attention_body(
    length_ref, cache_ref, place_ref, adapter_ref, position_ref,
    normed_ref, w_ref, low_hbm, rope_hbm, gains_hbm, pages_ref,
    out_ref, kv_ref,
    m_ref, l_ref, sum_ref, cached_ref, x, w, up, acc, q_ref, low_ref, rope_ref, gains_ref, sems,
):
    def chunk(k):
        rows = w_ref.at[pl.ds(4 * k, 4), pl.ds(0, 256), pl.ds(0, 768)]
        return [
            pltpu.make_async_copy(normed_ref.at[k], x.at[k], sems.at[2 * k]),
            pltpu.make_async_copy(rows, w.at[k], sems.at[2 * k + 1]),
        ]

    chunks = [chunk(k) for k in range(4)]
    for copy in chunks[0]:
        copy.start()
    up[...] = jnp.zeros_like(up)
    maps = []
    for p in range(PROMPTS):
        slot = position_ref[adapter_ref[p]]
        q_part = w_ref.at[slot, pl.ds(256, 16), pl.ds(0, 512)]
        v_part = w_ref.at[slot, pl.ds(256, 16), pl.ds(512, HEAD)]
        maps.append(pltpu.make_async_copy(q_part, up.at[pl.ds(p * 32, 16), pl.ds(0, 512)], sems.at[8 + 2 * p]))
        maps.append(pltpu.make_async_copy(v_part, up.at[pl.ds(p * 32 + 16, 16), pl.ds(512, HEAD)], sems.at[9 + 2 * p]))
    maps.append(pltpu.make_async_copy(low_hbm, low_ref, sems.at[48]))
    maps.append(pltpu.make_async_copy(rope_hbm, rope_ref, sems.at[49]))
    maps.append(pltpu.make_async_copy(gains_hbm, gains_ref, sems.at[50]))
    for copy in chunks[1] + maps:
        copy.start()
    pages = page_copies(place_ref, pages_ref, cached_ref, sems, 16)
    for k in range(4):
        for copy in chunks[k]:
            copy.wait()
        if k + 2 < 4:
            for copy in chunks[k + 2]:
                copy.start()
        if k == 2:
            for copy in pages:
                copy.start()
        part = jnp.dot(x[k], w[k].reshape(1024, 768), preferred_element_type=F32)
        if k == 0:
            acc[...] = part
        else:
            acc[...] += part
    for copy in maps:
        copy.wait()
    change = 0.5 * jnp.dot(low_ref[...], up[...], preferred_element_type=F32)
    rope = rope_ref[...]
    front = lax.broadcasted_iota(jnp.int32, rope.shape, 1) < HEAD // 2
    swapped = pltpu.roll(rope, HEAD // 2, 1)
    cos, sin = jnp.where(front, rope, swapped), jnp.where(front, -swapped, rope)

    def finish(raw, gain):
        scale = lax.rsqrt(jnp.mean(raw * raw, axis=-1, keepdims=True) + EPSILON)
        x = raw * scale * gain
        return (x * cos + pltpu.roll(x, HEAD // 2, 1) * sin).astype(BF)

    for h in range(GROUP):
        cut = slice(h * HEAD, (h + 1) * HEAD)
        q_ref[h] = finish(acc[:, cut] + change[:, cut], gains_ref[0:1, :])
    kv_ref[0] = finish(acc[:, 512:640], gains_ref[1:2, :])
    kv_ref[1] = (acc[:, 640:768] + change[:, 512:640]).astype(BF)
    for copy in pages:
        copy.wait()
    attend(length_ref, cache_ref, q_ref, kv_ref, cached_ref, out_ref, m_ref, l_ref, sum_ref)


def attention(lengths, cached, place, adapter, position, normed, weight, low, rope, gains, pages):
    hbm = pl.BlockSpec(memory_space=pl.ANY)
    return pl.pallas_call(
        attention_body,
        out_shape=(
            jax.ShapeDtypeStruct((TOK, FEAT), BF),
            jax.ShapeDtypeStruct((2, TOK, HEAD), BF),
        ),
        grid_spec=pltpu.PrefetchScalarGridSpec(
            num_scalar_prefetch=5,
            grid=(1,),
            in_specs=[hbm] * 6,
            out_specs=(whole(TOK, FEAT), whole(2, TOK, HEAD)),
            scratch_shapes=ATTEND_SCRATCH
            + [
                pltpu.VMEM((4, TOK, 1024), BF),
                pltpu.VMEM((4, 4, 256, 768), BF),
                pltpu.VMEM((128, 640), BF),
                pltpu.VMEM((TOK, 768), F32),
                pltpu.VMEM((GROUP, TOK, HEAD), BF),
                pltpu.VMEM((TOK, 128), BF),
                pltpu.VMEM((TOK, HEAD), F32),
                pltpu.VMEM((2, HEAD), F32),
                pltpu.SemaphoreType.DMA((51,)),
            ],
        ),
        compiler_params=vmem(32),
        name="attention",
    )(
        lengths, cached, place, adapter, position,
        in_hbm(normed), in_hbm(weight), in_hbm(low), in_hbm(rope), in_hbm(gains), in_hbm(pages),
    )


def low_body(length_ref, *refs):
    blocks, turned_ref, low_ref = refs[:8], refs[8], refs[9]
    low = jnp.zeros((TOK, 128), F32)
    for b in range(8):
        low += jnp.dot(blocks[b][...], turned_ref[b].reshape(FEAT, 128), preferred_element_type=F32)
    token = lax.broadcasted_iota(jnp.int32, low.shape, 0)
    lane = lax.broadcasted_iota(jnp.int32, low.shape, 1)
    prompt = per_token(prompt_rows(length_ref), range(PROMPTS), token)
    low = jnp.where((lane & 63) // 16 == prompt, low, 0.0)
    high = low.astype(BF)
    rest = low - high.astype(F32)
    middle = rest.astype(BF)
    least = (rest - middle.astype(F32)).astype(BF)
    low_ref[:, :128] = jnp.where(lane < 64, high, middle)
    low_ref[:, 128:] = jnp.where(lane < 64, least, jnp.zeros_like(least))


def output_low(lengths, blocks, turned):
    return pl.pallas_call(
        low_body,
        out_shape=pltpu.HBM((TOK, 256), BF),
        grid_spec=pltpu.PrefetchScalarGridSpec(
            num_scalar_prefetch=1,
            grid=(1,),
            in_specs=[whole(TOK, FEAT)] * 8 + [whole(8, 2, 256, 128)],
            out_specs=whole(TOK, 256),
        ),
        compiler_params=vmem(20),
        name="output_low",
    )(lengths, *blocks, in_hbm(turned))


def out_body(me_ref, adapter_ref, position_ref, *refs):
    blocks = refs[:8]
    low_hbm, weight_ref, hidden_hbm, out_ref, x, w, oup, low_ref, hidden, acc, sems = refs[8:]
    order = col_order(me_ref[1])
    copies = []
    for b in range(8):
        rows = weight_ref.at[pl.ds(2 * order[b], 2), pl.ds(0, 256)]
        copies.append(pltpu.make_async_copy(rows, w.at[b // 2, pl.ds(b % 2 * 2, 2)], sems.at[b]))
        side = pl.ds(b % 2 * FEAT, FEAT)
        copies.append(pltpu.make_async_copy(blocks[b], x.at[b // 2, :, side], sems.at[8 + b]))
    last = [
        pltpu.make_async_copy(hidden_hbm, hidden, sems.at[16]),
        pltpu.make_async_copy(low_hbm, low_ref, sems.at[17]),
    ]
    for p in range(PROMPTS):
        slot = position_ref[adapter_ref[p]]
        rows = weight_ref.at[slot, pl.ds(256, 16)]
        last.append(pltpu.make_async_copy(rows, oup.at[pl.ds(p * 16, 16)], sems.at[18 + p]))
    for copy in copies + last:
        copy.start()
    for i in range(4):
        for copy in copies[4 * i : 4 * i + 4]:
            copy.wait()
        part = jnp.dot(x[i], w[i].reshape(2 * FEAT, FEAT), preferred_element_type=F32)
        if i == 0:
            acc[...] = part
        else:
            acc[...] += part
    for copy in last:
        copy.wait()
    maps = jnp.concatenate([oup[...]] * 4, axis=0)
    change = jnp.dot(low_ref[...], maps, preferred_element_type=F32)
    out_ref[...] = (hidden[...].astype(F32) + acc[...] + 0.5 * change).astype(BF)


def output(me, adapter, position, blocks, low, weight, hidden):
    hbm = pl.BlockSpec(memory_space=pl.ANY)
    return pl.pallas_call(
        out_body,
        out_shape=jax.ShapeDtypeStruct((TOK, FEAT), BF),
        grid_spec=pltpu.PrefetchScalarGridSpec(
            num_scalar_prefetch=3,
            grid=(1,),
            in_specs=[hbm] * 11,
            out_specs=whole(TOK, FEAT),
            scratch_shapes=[
                pltpu.VMEM((4, TOK, 2 * FEAT), BF),
                pltpu.VMEM((4, 4, 256, FEAT), BF),
                pltpu.VMEM((64, FEAT), BF),
                pltpu.VMEM((TOK, 256), BF),
                pltpu.VMEM((TOK, FEAT), BF),
                pltpu.VMEM((TOK, FEAT), F32),
                pltpu.SemaphoreType.DMA((22,)),
            ],
        ),
        compiler_params=vmem(24),
        name="output",
    )(
        me, adapter, position,
        *map(in_hbm, blocks), in_hbm(low), in_hbm(weight), in_hbm(hidden),
    )


def on_device(
    hidden_input,
    input_norm_gain,
    query_norm_gain,
    key_norm_gain,
    query_key_value_weight,
    output_weight,
    adapter_down_maps,
    adapter_up_maps,
    output_down_maps,
    output_up_maps,
    prompt_adapter,
    adapter_position,
    prompt_length,
    cache_length,
    page_owner_row,
    page_store_index,
    cache_page_store,
):
    me = jnp.stack([lax.axis_index("row"), lax.axis_index("col")]).astype(jnp.int32)
    wide, rest, slots = pack(
        me,
        query_key_value_weight,
        output_weight,
        adapter_up_maps,
        output_up_maps,
        adapter_down_maps,
        output_down_maps,
    )
    weight = lax.all_gather(wide, "row", axis=0)
    slots = lax.all_to_all(slots, "row", 0, 0)

    picked, place = pick_pages(me, page_owner_row, page_store_index, cache_page_store)
    picked, slots, rest = lax.optimization_barrier((picked, slots, rest))
    rest = lax.all_gather(rest, "row", axis=0)
    pages = lax.all_to_all(picked.reshape(16, 4 * PAGE, HEAD), "row", 0, 0).reshape(32, 2, PAGE, HEAD)

    blocks = gather_col(select_slots(prompt_adapter, adapter_position, slots, hidden_input), BLOCK_ROWS // 2)

    token = lax.broadcasted_iota(jnp.int32, (TOK, HEAD), 0)
    position, start = token, jnp.int32(0)
    for p in range(PROMPTS):
        end = start + prompt_length[0, p]
        position = jnp.where((token >= start) & (token < end), token - start + cache_length[p], position)
        start = end
    frequency = ROPE_BASE ** (-2.0 * jnp.arange(HEAD // 2, dtype=F32) / HEAD)
    angles = position.astype(F32) * jnp.concatenate([frequency, frequency])[None, :]
    front = lax.broadcasted_iota(jnp.int32, (TOK, HEAD), 1) < HEAD // 2
    rope = jnp.where(front, jnp.cos(angles), jnp.sin(angles))

    normed, low, turned = norm_low(me, prompt_length, blocks, input_norm_gain.reshape(8, 1, FEAT))
    gains = jnp.stack([query_norm_gain, key_norm_gain]).astype(F32)
    weight, normed, low, pages, rope, gains = lax.optimization_barrier((weight, normed, low, pages, rope, gains))
    attended, new_cache = attention(
        prompt_length,
        cache_length,
        place,
        prompt_adapter,
        adapter_position,
        normed,
        weight,
        low,
        rope,
        gains,
        pages,
    )
    attended = gather_col(attended, 256)
    low = output_low(prompt_length, attended, turned)
    rest, low = lax.optimization_barrier((rest, low))
    hidden_output = output(me, prompt_adapter, adapter_position, attended, low, rest, hidden_input)
    return hidden_output, new_cache


def solution(mesh):
    return jax.shard_map(
        on_device,
        mesh=mesh,
        in_specs=(
            P("row", "col"),
            P(),
            P(),
            P(),
            P("row", "col"),
            P("row", "col"),
            P("row", None, None),
            P("row", None, "col"),
            P("row", None, "col"),
            P("row", None, None),
            P("row"),
            P(),
            P("row", None),
            P("row"),
            P(),
            P(),
            P("row", None, None, "col"),
        ),
        out_specs=(P("row", "col"), P(None, "row", "col")),
        check_vma=False,
    )
```

```python
import math

import jax
import jax.numpy as jnp
from jax import lax
from jax.experimental import pallas as pl
from jax.experimental.pallas import tpu as pltpu
from jax.sharding import PartitionSpec as P

HEAD = 128
GROUP = 4
WIN = 1024
SINKS = 4
PAGE = 128
EPSILON = 1e-06
ROPE_BASE = 1000000.0
TOK = 512
FEAT = 512
PROMPTS = 4
BF = jnp.bfloat16
F32 = jnp.float32
NEG = -1e30


def perm_x(k):
    return [(i, (i // 4 + k) % 4 * 4 + i % 4) for i in range(16)]


def perm_y(k):
    return [(i, i // 4 * 4 + (i % 4 + k) % 4) for i in range(16)]


def perm_z(k):
    return [(i, (i // 2 + k) % 4 * 2 + i % 2) for i in range(8)]


SWAP = [(i, i ^ 1) for i in range(8)]


def ring_far(before, after, axis, perm, half):
    return lax.ppermute(before[:half], axis, perm(1)), lax.ppermute(after[half:], axis, perm(-1))


def ring4(block, axis, perm, half):
    before = lax.ppermute(block, axis, perm(1))
    after = lax.ppermute(block, axis, perm(-1))
    return before, after, jnp.concatenate(ring_far(before, after, axis, perm, half), axis=0)


def swap(block):
    return lax.ppermute(block, "col", SWAP)


def gather_col(block, half):
    out = [block, swap(block)]
    for piece in ring4(block, "col", perm_z, half):
        out += [piece, swap(piece)]
    return out


def col_order(col):
    chip, core = col // 2, col % 2
    return [lax.rem(chip + d, 4) * 2 + lax.rem(core + s, 2) for d in (0, 3, 1, 2) for s in (0, 1)]


def prompt_rows(length_ref):
    start, rows = jnp.int32(0), []
    for p in range(PROMPTS):
        rows.append((start, start + length_ref[0, p]))
        start = start + length_ref[0, p]
    return rows


def per_token(rows, values, token, default=0):
    out = jnp.full(token.shape, default, jnp.int32)
    for (start, end), value in zip(rows, values):
        out = jnp.where((token >= start) & (token < end), value, out)
    return out


def in_hbm(x):
    return pltpu.with_memory_space_constraint(x, pltpu.HBM)


def vmem(n):
    return pltpu.CompilerParams(vmem_limit_bytes=n << 20)


def whole(*shape):
    return pl.BlockSpec(shape, lambda *_: (0,) * len(shape))


def pick_body(me_ref, owner_ref, index_ref, store_ref, out_ref, place_ref):
    def group(r, carry):
        first, second, count = jnp.int32(0), jnp.int32(0), jnp.int32(0)
        for q in range(16):
            hit = owner_ref[r * 16 + q, 0] == me_ref[0]
            index = index_ref[r * 16 + q]
            first = jnp.where(hit & (count == 0), index, first)
            second = jnp.where(hit & (count == 1), index, second)
            count = count + hit.astype(jnp.int32)
        out_ref[r, 0] = store_ref[first]
        out_ref[r, 1] = store_ref[second]
        return carry

    lax.fori_loop(0, 16, group, 0)
    for i in range(16):
        holder, rank = owner_ref[me_ref[0] * 16 + i, 0], jnp.int32(0)
        for k in range(i):
            rank = jnp.where(owner_ref[me_ref[0] * 16 + k, 0] == holder, 1, rank)
        place_ref[i] = holder * 2 + rank


def pick_pages(me, owner, index, store):
    return pl.pallas_call(
        pick_body,
        out_shape=(
            jax.ShapeDtypeStruct((16, 2) + store.shape[1:], store.dtype),
            jax.ShapeDtypeStruct((16,), jnp.int32),
        ),
        grid_spec=pltpu.PrefetchScalarGridSpec(
            num_scalar_prefetch=3,
            grid=(1,),
            in_specs=[whole(*store.shape)],
            out_specs=(whole(16, 2, *store.shape[1:]), pl.BlockSpec(memory_space=pltpu.SMEM)),
        ),
        compiler_params=vmem(10),
        name="pick_pages",
    )(me, owner, index, store)


def pack_body(me_ref, qkv_ref, wo_ref, up_ref, oup_ref, down_ref, odown_ref, wide_ref, rest_ref, slots_ref):
    wide_ref[:256, :] = qkv_ref[...]
    wide_ref[256:, :640] = up_ref[0]
    wide_ref[256:, 640:] = jnp.zeros((16, 128), BF)
    rest_ref[:256, :] = wo_ref[...]
    rest_ref[256:, :] = oup_ref[0]
    slots_ref[:32, :] = down_ref[0]
    slots_ref[32:, :] = odown_ref[0]


def pack(me, qkv, wo, up, oup, down, odown):
    return pl.pallas_call(
        pack_body,
        out_shape=(
            jax.ShapeDtypeStruct((272, 768), BF),
            jax.ShapeDtypeStruct((272, FEAT), BF),
            jax.ShapeDtypeStruct((48, FEAT), BF),
        ),
        grid_spec=pltpu.PrefetchScalarGridSpec(
            num_scalar_prefetch=1,
            grid=(1,),
            in_specs=[
                whole(256, 768),
                whole(256, FEAT),
                whole(1, 16, 640),
                pl.BlockSpec((1, 16, FEAT), lambda i, me: (0, 0, me[1])),
                pl.BlockSpec((1, 32, FEAT), lambda i, me: (0, 0, me[1])),
                whole(1, 16, FEAT),
            ],
            out_specs=(whole(272, 768), whole(272, FEAT), whole(48, FEAT)),
        ),
        name="pack",
    )(me, qkv, wo, up, oup, down, odown)


DOWN, ODOWN, BLOCK_ROWS = TOK, TOK + 128, TOK + 192


def select_body(me_ref, adapter_ref, position_ref, y0, y1, y2, y3, hidden_ref, out_ref):
    def place(index, mine):
        d = lax.rem(index - mine + 4, 4)
        return jnp.where(d == 0, 0, jnp.where(d == 3, 1, d + 1))

    out_ref[:TOK, :] = hidden_ref[...]
    for p in range(PROMPTS):
        slot = position_ref[adapter_ref[p]]
        x = place(lax.div(slot, 4), lax.div(me_ref[0], 4))
        y = place(lax.rem(slot, 4), lax.rem(me_ref[0], 4))
        for k, ref in enumerate((y0, y1, y2, y3)):

            @pl.when(y == k)
            def _():
                out_ref[DOWN + p * 32 : DOWN + p * 32 + 32, :] = ref[x, :32, :]
                out_ref[ODOWN + p * 16 : ODOWN + p * 16 + 16, :] = ref[x, 32:, :]


def select_slots(me, adapter, position, pieces, hidden):
    return pl.pallas_call(
        select_body,
        out_shape=jax.ShapeDtypeStruct((BLOCK_ROWS, FEAT), BF),
        grid_spec=pltpu.PrefetchScalarGridSpec(
            num_scalar_prefetch=3,
            grid=(1,),
            in_specs=[whole(4, 48, FEAT)] * 4 + [whole(TOK, FEAT)],
            out_specs=whole(BLOCK_ROWS, FEAT),
        ),
        name="select_slots",
    )(me, adapter, position, *pieces, hidden)


def norm_body(me_ref, length_ref, *refs):
    blocks, maps = refs[:8], refs[8:16]
    outs = refs[16:24]
    gain_ref, normed_ref, low_ref, turned_ref = refs[24:]
    order = col_order(me_ref[1])
    values = [b[...].astype(F32) for b in blocks]
    total = sum(jnp.sum(v * v, axis=-1, keepdims=True) for v in values)
    scale = lax.rsqrt(total * (1.0 / (8 * FEAT)) + EPSILON)
    low = jnp.zeros(low_ref.shape, F32)
    for b in range(8):
        gain = gain_ref[order[b]].astype(F32)
        normed = (values[b] * scale * gain).astype(BF)
        normed_ref[order[b] // 2, :, pl.ds(pl.multiple_of(order[b] % 2 * FEAT, FEAT), FEAT)] = normed
        low += lax.dot_general(normed, maps[b][...], (((1,), (1,)), ((), ())), preferred_element_type=F32)
    token = pl.program_id(0) * low.shape[0] + lax.broadcasted_iota(jnp.int32, low.shape, 0)
    prompt = per_token(prompt_rows(length_ref), range(PROMPTS), token)
    mine = lax.broadcasted_iota(jnp.int32, low.shape, 1) // 32 == prompt
    low_ref[...] = jnp.where(mine, low, 0.0).astype(BF)
    for k in range(4):

        @pl.when(pl.program_id(0) == k)
        def _():
            for b in range(2):
                down = outs[2 * k + b][...].astype(F32)
                turned = jnp.concatenate([down, down], axis=0).T.astype(BF)
                turned_ref[b, 0], turned_ref[b, 1] = turned[:256], turned[256:]


def norm_low(me, lengths, blocks, gain):
    rows = 128
    return pl.pallas_call(
        norm_body,
        out_shape=(
            pltpu.HBM((4, TOK, 2 * FEAT), BF),
            pltpu.HBM((TOK, 128), BF),
            pltpu.HBM((8, 2, 256, 128), BF),
        ),
        grid_spec=pltpu.PrefetchScalarGridSpec(
            num_scalar_prefetch=2,
            grid=(TOK // rows,),
            in_specs=[pl.BlockSpec((rows, FEAT), lambda i, *_: (i, 0))] * 8
            + [pl.BlockSpec((128, FEAT), lambda i, *_: (DOWN // 128, 0))] * 8
            + [pl.BlockSpec((64, FEAT), lambda i, *_: (ODOWN // 64, 0))] * 8
            + [whole(8, 1, FEAT)],
            out_specs=(
                pl.BlockSpec((4, rows, 2 * FEAT), lambda i, *_: (0, i, 0)),
                pl.BlockSpec((rows, 128), lambda i, *_: (i, 0)),
                pl.BlockSpec((2, 2, 256, 128), lambda i, *_: (i, 0, 0, 0)),
            ),
        ),
        compiler_params=vmem(20),
        name="norm_low",
    )(me, lengths, *blocks, *blocks, *blocks, gain)


BLOCK = 64
SCALE2 = math.log2(math.e) / math.sqrt(HEAD)


def page_copies(place_ref, pages_ref, cached_ref, sems, base):
    copies = []
    for i in range(16):
        for h in range(2):
            into = cached_ref.at[h, i // 8, pl.ds(i % 8 * PAGE, PAGE)]
            copies.append(pltpu.make_async_copy(pages_ref.at[place_ref[i], h], into, sems.at[base + 2 * i + h]))
    return copies


def attend(length_ref, cache_ref, q_ref, kv_ref, cached_ref, out_ref, m_ref, l_ref, acc_ref):
    rows, span = GROUP * BLOCK, 256 + BLOCK
    prompts = prompt_rows(length_ref)
    begins = [start for start, _ in prompts]
    count, ranks = jnp.int32(0), []
    for p in range(PROMPTS):
        has = cache_ref[p] > 0
        ranks.append(jnp.where(has, count, -1))
        count = count + has.astype(jnp.int32)
    owners = []
    for j in range(2):
        mine = [(ranks[p] == j).astype(jnp.int32) for p in range(PROMPTS)]
        owners.append(
            (
                sum(mine[p] * prompts[p][0] for p in range(PROMPTS)),
                sum(mine[p] * prompts[p][1] for p in range(PROMPTS)),
                sum(mine[p] * cache_ref[p] for p in range(PROMPTS)),
            )
        )

    def block(t, carry):
        start = pl.multiple_of(t * BLOCK, BLOCK)
        lo = pl.multiple_of(jnp.maximum(start - 256, 0), BLOCK)
        cut = pl.ds(start, BLOCK)
        q = q_ref[:, cut, :].reshape(rows, HEAD)
        token = start + (lax.broadcasted_iota(jnp.int32, (rows, 1), 0) & (BLOCK - 1))
        begin = per_token(prompts, begins, token)
        s = lax.dot_general(q, kv_ref[0, pl.ds(lo, span), :], (((1,), (1,)), ((), ())), preferred_element_type=F32)
        key = lo + lax.broadcasted_iota(jnp.int32, (rows, span), 1)
        s = jnp.where((key <= token) & (key >= begin), s, NEG)
        m = jnp.max(s, axis=1, keepdims=True)
        w = jnp.exp2((s - m) * SCALE2)
        m_ref[...] = m
        l_ref[...] = jnp.sum(w, axis=1, keepdims=True)
        acc_ref[...] = jnp.dot(w.astype(BF), kv_ref[1, pl.ds(lo, span), :], preferred_element_type=F32)

        def cached(j):
            first, last, length = owners[j]
            mine = (token >= first) & (token < last)
            s = lax.dot_general(q, cached_ref[0, j], (((1,), (1,)), ((), ())), preferred_element_type=F32)
            at = lax.broadcasted_iota(jnp.int32, (rows, 256), 1)
            head = jnp.where((at > length + token - first - WIN) | (at < SINKS), s[:, :256], NEG)
            at = WIN - PAGE + lax.broadcasted_iota(jnp.int32, (rows, PAGE), 1)
            tail = jnp.where(at < length, s[:, WIN - PAGE :], NEG)
            s = jnp.concatenate([head, s[:, 256 : WIN - PAGE], tail], axis=1)
            m_old = m_ref[...]
            m_new = jnp.where(mine, jnp.maximum(m_old, jnp.max(s, axis=1, keepdims=True)), m_old)
            fade = jnp.exp2((m_old - m_new) * SCALE2)
            w = jnp.exp2((s - jnp.where(mine, m_new, -NEG)) * SCALE2)
            m_ref[...] = m_new
            l_ref[...] = l_ref[...] * fade + jnp.sum(w, axis=1, keepdims=True)
            acc_ref[...] = acc_ref[...] * fade + jnp.dot(w.astype(BF), cached_ref[1, j], preferred_element_type=F32)

        for j in range(2):
            pl.when((owners[j][0] < start + BLOCK) & (owners[j][1] > start))(lambda j=j: cached(j))

        done = (acc_ref[...] * (1.0 / l_ref[...])).astype(BF)
        for h in range(GROUP):
            out_ref[cut, h * HEAD : (h + 1) * HEAD] = done[h * BLOCK : (h + 1) * BLOCK, :]
        return carry

    lax.fori_loop(0, TOK // BLOCK, block, 0)


ATTEND_SCRATCH = [
    pltpu.VMEM((GROUP * BLOCK, 1), F32),
    pltpu.VMEM((GROUP * BLOCK, 1), F32),
    pltpu.VMEM((GROUP * BLOCK, HEAD), F32),
    pltpu.VMEM((2, 2, WIN, HEAD), BF),
]


def attention_body(
    length_ref, cache_ref, place_ref, adapter_ref, position_ref,
    normed_ref, w_ref, low_hbm, rope_hbm, gains_hbm, pages_ref,
    out_ref, kv_ref,
    m_ref, l_ref, sum_ref, cached_ref, x, w, up, acc, q_ref, low_ref, rope_ref, gains_ref, sems,
):
    def chunk(k):
        rows = w_ref.at[pl.ds(4 * k, 4), pl.ds(0, 256), pl.ds(0, 768)]
        return [
            pltpu.make_async_copy(normed_ref.at[k], x.at[k], sems.at[2 * k]),
            pltpu.make_async_copy(rows, w.at[k], sems.at[2 * k + 1]),
        ]

    chunks = [chunk(k) for k in range(4)]
    for copy in chunks[0]:
        copy.start()
    up[...] = jnp.zeros_like(up)
    maps = []
    for p in range(PROMPTS):
        slot = position_ref[adapter_ref[p]]
        q_part = w_ref.at[slot, pl.ds(256, 16), pl.ds(0, 512)]
        v_part = w_ref.at[slot, pl.ds(256, 16), pl.ds(512, HEAD)]
        maps.append(pltpu.make_async_copy(q_part, up.at[pl.ds(p * 32, 16), pl.ds(0, 512)], sems.at[8 + 2 * p]))
        maps.append(pltpu.make_async_copy(v_part, up.at[pl.ds(p * 32 + 16, 16), pl.ds(512, HEAD)], sems.at[9 + 2 * p]))
    maps.append(pltpu.make_async_copy(low_hbm, low_ref, sems.at[48]))
    maps.append(pltpu.make_async_copy(rope_hbm, rope_ref, sems.at[49]))
    maps.append(pltpu.make_async_copy(gains_hbm, gains_ref, sems.at[50]))
    for copy in chunks[1] + maps:
        copy.start()
    pages = page_copies(place_ref, pages_ref, cached_ref, sems, 16)
    for k in range(4):
        for copy in chunks[k]:
            copy.wait()
        if k + 2 < 4:
            for copy in chunks[k + 2]:
                copy.start()
        if k == 2:
            for copy in pages:
                copy.start()
        part = jnp.dot(x[k], w[k].reshape(1024, 768), preferred_element_type=F32)
        if k == 0:
            acc[...] = part
        else:
            acc[...] += part
    for copy in maps:
        copy.wait()
    change = 0.5 * jnp.dot(low_ref[...], up[...], preferred_element_type=F32)
    rope = rope_ref[...]
    front = lax.broadcasted_iota(jnp.int32, rope.shape, 1) < HEAD // 2
    swapped = pltpu.roll(rope, HEAD // 2, 1)
    cos, sin = jnp.where(front, rope, swapped), jnp.where(front, -swapped, rope)

    def finish(raw, gain):
        scale = lax.rsqrt(jnp.mean(raw * raw, axis=-1, keepdims=True) + EPSILON)
        x = raw * scale * gain
        return (x * cos + pltpu.roll(x, HEAD // 2, 1) * sin).astype(BF)

    for h in range(GROUP):
        cut = slice(h * HEAD, (h + 1) * HEAD)
        q_ref[h] = finish(acc[:, cut] + change[:, cut], gains_ref[0:1, :])
    kv_ref[0] = finish(acc[:, 512:640], gains_ref[1:2, :])
    kv_ref[1] = (acc[:, 640:768] + change[:, 512:640]).astype(BF)
    for copy in pages:
        copy.wait()
    attend(length_ref, cache_ref, q_ref, kv_ref, cached_ref, out_ref, m_ref, l_ref, sum_ref)


def attention(lengths, cached, place, adapter, position, normed, weight, low, rope, gains, pages):
    hbm = pl.BlockSpec(memory_space=pl.ANY)
    return pl.pallas_call(
        attention_body,
        out_shape=(
            jax.ShapeDtypeStruct((TOK, FEAT), BF),
            jax.ShapeDtypeStruct((2, TOK, HEAD), BF),
        ),
        grid_spec=pltpu.PrefetchScalarGridSpec(
            num_scalar_prefetch=5,
            grid=(1,),
            in_specs=[hbm] * 6,
            out_specs=(whole(TOK, FEAT), whole(2, TOK, HEAD)),
            scratch_shapes=ATTEND_SCRATCH
            + [
                pltpu.VMEM((4, TOK, 1024), BF),
                pltpu.VMEM((4, 4, 256, 768), BF),
                pltpu.VMEM((128, 640), BF),
                pltpu.VMEM((TOK, 768), F32),
                pltpu.VMEM((GROUP, TOK, HEAD), BF),
                pltpu.VMEM((TOK, 128), BF),
                pltpu.VMEM((TOK, HEAD), F32),
                pltpu.VMEM((2, HEAD), F32),
                pltpu.SemaphoreType.DMA((51,)),
            ],
        ),
        compiler_params=vmem(32),
        name="attention",
    )(
        lengths, cached, place, adapter, position,
        in_hbm(normed), in_hbm(weight), in_hbm(low), in_hbm(rope), in_hbm(gains), in_hbm(pages),
    )


def low_body(length_ref, *refs):
    blocks, turned_ref, low_ref = refs[:8], refs[8], refs[9]
    low = jnp.zeros((TOK, 128), F32)
    for b in range(8):
        low += jnp.dot(blocks[b][...], turned_ref[b].reshape(FEAT, 128), preferred_element_type=F32)
    token = lax.broadcasted_iota(jnp.int32, low.shape, 0)
    lane = lax.broadcasted_iota(jnp.int32, low.shape, 1)
    prompt = per_token(prompt_rows(length_ref), range(PROMPTS), token)
    low = jnp.where((lane & 63) // 16 == prompt, low, 0.0)
    high = low.astype(BF)
    rest = low - high.astype(F32)
    middle = rest.astype(BF)
    least = (rest - middle.astype(F32)).astype(BF)
    low_ref[:, :128] = jnp.where(lane < 64, high, middle)
    low_ref[:, 128:] = jnp.where(lane < 64, least, jnp.zeros_like(least))


def output_low(lengths, blocks, turned):
    return pl.pallas_call(
        low_body,
        out_shape=pltpu.HBM((TOK, 256), BF),
        grid_spec=pltpu.PrefetchScalarGridSpec(
            num_scalar_prefetch=1,
            grid=(1,),
            in_specs=[whole(TOK, FEAT)] * 8 + [whole(8, 2, 256, 128)],
            out_specs=whole(TOK, 256),
        ),
        compiler_params=vmem(20),
        name="output_low",
    )(lengths, *blocks, in_hbm(turned))


def out_body(me_ref, adapter_ref, position_ref, *refs):
    blocks = refs[:8]
    low_hbm, weight_ref, hidden_hbm, out_ref, x, w, oup, low_ref, hidden, acc, sems = refs[8:]
    order = col_order(me_ref[1])
    copies = []
    for b in range(8):
        rows = weight_ref.at[pl.ds(2 * order[b], 2), pl.ds(0, 256)]
        copies.append(pltpu.make_async_copy(rows, w.at[b // 2, pl.ds(b % 2 * 2, 2)], sems.at[b]))
        side = pl.ds(b % 2 * FEAT, FEAT)
        copies.append(pltpu.make_async_copy(blocks[b], x.at[b // 2, :, side], sems.at[8 + b]))
    last = [
        pltpu.make_async_copy(hidden_hbm, hidden, sems.at[16]),
        pltpu.make_async_copy(low_hbm, low_ref, sems.at[17]),
    ]
    for p in range(PROMPTS):
        slot = position_ref[adapter_ref[p]]
        rows = weight_ref.at[slot, pl.ds(256, 16)]
        last.append(pltpu.make_async_copy(rows, oup.at[pl.ds(p * 16, 16)], sems.at[18 + p]))
    for copy in copies + last:
        copy.start()
    for i in range(4):
        for copy in copies[4 * i : 4 * i + 4]:
            copy.wait()
        part = jnp.dot(x[i], w[i].reshape(2 * FEAT, FEAT), preferred_element_type=F32)
        if i == 0:
            acc[...] = part
        else:
            acc[...] += part
    for copy in last:
        copy.wait()
    maps = jnp.concatenate([oup[...]] * 4, axis=0)
    change = jnp.dot(low_ref[...], maps, preferred_element_type=F32)
    out_ref[...] = (hidden[...].astype(F32) + acc[...] + 0.5 * change).astype(BF)


def output(me, adapter, position, blocks, low, weight, hidden):
    hbm = pl.BlockSpec(memory_space=pl.ANY)
    return pl.pallas_call(
        out_body,
        out_shape=jax.ShapeDtypeStruct((TOK, FEAT), BF),
        grid_spec=pltpu.PrefetchScalarGridSpec(
            num_scalar_prefetch=3,
            grid=(1,),
            in_specs=[hbm] * 11,
            out_specs=whole(TOK, FEAT),
            scratch_shapes=[
                pltpu.VMEM((4, TOK, 2 * FEAT), BF),
                pltpu.VMEM((4, 4, 256, FEAT), BF),
                pltpu.VMEM((64, FEAT), BF),
                pltpu.VMEM((TOK, 256), BF),
                pltpu.VMEM((TOK, FEAT), BF),
                pltpu.VMEM((TOK, FEAT), F32),
                pltpu.SemaphoreType.DMA((22,)),
            ],
        ),
        compiler_params=vmem(24),
        name="output",
    )(
        me, adapter, position,
        *map(in_hbm, blocks), in_hbm(low), in_hbm(weight), in_hbm(hidden),
    )


def on_device(
    hidden_input,
    input_norm_gain,
    query_norm_gain,
    key_norm_gain,
    query_key_value_weight,
    output_weight,
    adapter_down_maps,
    adapter_up_maps,
    output_down_maps,
    output_up_maps,
    prompt_adapter,
    adapter_position,
    prompt_length,
    cache_length,
    page_owner_row,
    page_store_index,
    cache_page_store,
):
    me = jnp.stack([lax.axis_index("row"), lax.axis_index("col")]).astype(jnp.int32)
    wide, rest, slots = pack(
        me,
        query_key_value_weight,
        output_weight,
        adapter_up_maps,
        output_up_maps,
        adapter_down_maps,
        output_down_maps,
    )
    weight = lax.all_gather(wide, "row", axis=0)
    along = [slots] + [lax.ppermute(slots, "row", perm_x(k)) for k in (1, -1, 2)]
    along = jnp.concatenate(along, axis=0)
    before, after, far = ring4(along, "row", perm_y, 96)
    far, rest = lax.optimization_barrier((far, rest))
    pieces = [piece.reshape(4, 48, FEAT) for piece in (along, before, after, far)]

    picked, place = pick_pages(me, page_owner_row, page_store_index, cache_page_store)
    rest = lax.all_gather(rest, "row", axis=0)
    pages = lax.all_to_all(picked.reshape(16, 4 * PAGE, HEAD), "row", 0, 0).reshape(32, 2, PAGE, HEAD)

    blocks = gather_col(select_slots(me, prompt_adapter, adapter_position, pieces, hidden_input), BLOCK_ROWS // 2)

    token = lax.broadcasted_iota(jnp.int32, (TOK, HEAD), 0)
    position, start = token, jnp.int32(0)
    for p in range(PROMPTS):
        end = start + prompt_length[0, p]
        position = jnp.where((token >= start) & (token < end), token - start + cache_length[p], position)
        start = end
    frequency = ROPE_BASE ** (-2.0 * jnp.arange(HEAD // 2, dtype=F32) / HEAD)
    angles = position.astype(F32) * jnp.concatenate([frequency, frequency])[None, :]
    front = lax.broadcasted_iota(jnp.int32, (TOK, HEAD), 1) < HEAD // 2
    rope = jnp.where(front, jnp.cos(angles), jnp.sin(angles))

    normed, low, turned = norm_low(me, prompt_length, blocks, input_norm_gain.reshape(8, 1, FEAT))
    gains = jnp.stack([query_norm_gain, key_norm_gain]).astype(F32)
    weight, normed, low, pages, rope, gains = lax.optimization_barrier((weight, normed, low, pages, rope, gains))
    attended, new_cache = attention(
        prompt_length,
        cache_length,
        place,
        prompt_adapter,
        adapter_position,
        normed,
        weight,
        low,
        rope,
        gains,
        pages,
    )
    attended = gather_col(attended, 256)
    low = output_low(prompt_length, attended, turned)
    rest, low = lax.optimization_barrier((rest, low))
    hidden_output = output(me, prompt_adapter, adapter_position, attended, low, rest, hidden_input)
    return hidden_output, new_cache


def solution(mesh):
    return jax.shard_map(
        on_device,
        mesh=mesh,
        in_specs=(
            P("row", "col"),
            P(),
            P(),
            P(),
            P("row", "col"),
            P("row", "col"),
            P("row", None, None),
            P("row", None, "col"),
            P("row", None, "col"),
            P("row", None, None),
            P("row"),
            P(),
            P("row", None),
            P("row"),
            P(),
            P(),
            P("row", None, None, "col"),
        ),
        out_specs=(P("row", "col"), P(None, "row", "col")),
        check_vma=False,
    )
```

```python
import math

import jax
import jax.numpy as jnp
from jax import lax
from jax.experimental import pallas as pl
from jax.experimental.pallas import tpu as pltpu
from jax.sharding import PartitionSpec as P

HEAD = 128
GROUP = 4
WIN = 1024
SINKS = 4
PAGE = 128
EPSILON = 1e-06
ROPE_BASE = 1000000.0
TOK = 512
FEAT = 512
PROMPTS = 4
BF = jnp.bfloat16
F32 = jnp.float32
NEG = -1e30


def perm_x(k):
    return [(i, (i // 4 + k) % 4 * 4 + i % 4) for i in range(16)]


def perm_y(k):
    return [(i, i // 4 * 4 + (i % 4 + k) % 4) for i in range(16)]


def perm_z(k):
    return [(i, (i // 2 + k) % 4 * 2 + i % 2) for i in range(8)]


SWAP = [(i, i ^ 1) for i in range(8)]


def ring_far(before, after, axis, perm, half):
    return lax.ppermute(before[:half], axis, perm(1)), lax.ppermute(after[half:], axis, perm(-1))


def ring4(block, axis, perm, half):
    before = lax.ppermute(block, axis, perm(1))
    after = lax.ppermute(block, axis, perm(-1))
    return before, after, jnp.concatenate(ring_far(before, after, axis, perm, half), axis=0)


def swap(block):
    return lax.ppermute(block, "col", SWAP)


def gather_col(block, half):
    out = [block, swap(block)]
    for piece in ring4(block, "col", perm_z, half):
        out += [piece, swap(piece)]
    return out


def col_order(col):
    chip, core = col // 2, col % 2
    return [lax.rem(chip + d, 4) * 2 + lax.rem(core + s, 2) for d in (0, 3, 1, 2) for s in (0, 1)]


def prompt_rows(length_ref):
    start, rows = jnp.int32(0), []
    for p in range(PROMPTS):
        rows.append((start, start + length_ref[0, p]))
        start = start + length_ref[0, p]
    return rows


def per_token(rows, values, token, default=0):
    out = jnp.full(token.shape, default, jnp.int32)
    for (start, end), value in zip(rows, values):
        out = jnp.where((token >= start) & (token < end), value, out)
    return out


def in_hbm(x):
    return pltpu.with_memory_space_constraint(x, pltpu.HBM)


def vmem(n):
    return pltpu.CompilerParams(vmem_limit_bytes=n << 20)


def whole(*shape):
    return pl.BlockSpec(shape, lambda *_: (0,) * len(shape))


def pick_body(me_ref, owner_ref, index_ref, store_ref, out_ref, place_ref):
    def group(r, carry):
        first, second, count = jnp.int32(0), jnp.int32(0), jnp.int32(0)
        for q in range(16):
            hit = owner_ref[r * 16 + q, 0] == me_ref[0]
            index = index_ref[r * 16 + q]
            first = jnp.where(hit & (count == 0), index, first)
            second = jnp.where(hit & (count == 1), index, second)
            count = count + hit.astype(jnp.int32)
        out_ref[r, 0] = store_ref[first]
        out_ref[r, 1] = store_ref[second]
        return carry

    lax.fori_loop(0, 16, group, 0)
    for i in range(16):
        holder, rank = owner_ref[me_ref[0] * 16 + i, 0], jnp.int32(0)
        for k in range(i):
            rank = jnp.where(owner_ref[me_ref[0] * 16 + k, 0] == holder, 1, rank)
        place_ref[i] = holder * 2 + rank


def pick_pages(me, owner, index, store):
    return pl.pallas_call(
        pick_body,
        out_shape=(
            jax.ShapeDtypeStruct((16, 2) + store.shape[1:], store.dtype),
            jax.ShapeDtypeStruct((16,), jnp.int32),
        ),
        grid_spec=pltpu.PrefetchScalarGridSpec(
            num_scalar_prefetch=3,
            grid=(1,),
            in_specs=[whole(*store.shape)],
            out_specs=(whole(16, 2, *store.shape[1:]), pl.BlockSpec(memory_space=pltpu.SMEM)),
        ),
        compiler_params=vmem(10),
        name="pick_pages",
    )(me, owner, index, store)


def pack_body(me_ref, qkv_ref, wo_ref, up_ref, oup_ref, down_ref, odown_ref, wide_ref, rest_ref, slots_ref):
    wide_ref[:256, :] = qkv_ref[...]
    wide_ref[256:, :640] = up_ref[0]
    wide_ref[256:, 640:] = jnp.zeros((16, 128), BF)
    rest_ref[:256, :] = wo_ref[...]
    rest_ref[256:, :] = oup_ref[0]
    for r in range(16):
        slots_ref[r, :32, :] = down_ref[0]
        slots_ref[r, 32:, :] = odown_ref[0]


def pack(me, qkv, wo, up, oup, down, odown):
    return pl.pallas_call(
        pack_body,
        out_shape=(
            jax.ShapeDtypeStruct((272, 768), BF),
            jax.ShapeDtypeStruct((272, FEAT), BF),
            jax.ShapeDtypeStruct((16, 48, FEAT), BF),
        ),
        grid_spec=pltpu.PrefetchScalarGridSpec(
            num_scalar_prefetch=1,
            grid=(1,),
            in_specs=[
                whole(256, 768),
                whole(256, FEAT),
                whole(1, 16, 640),
                pl.BlockSpec((1, 16, FEAT), lambda i, me: (0, 0, me[1])),
                pl.BlockSpec((1, 32, FEAT), lambda i, me: (0, 0, me[1])),
                whole(1, 16, FEAT),
            ],
            out_specs=(whole(272, 768), whole(272, FEAT), whole(16, 48, FEAT)),
        ),
        name="pack",
    )(me, qkv, wo, up, oup, down, odown)


DOWN, ODOWN, BLOCK_ROWS = TOK, TOK + 128, TOK + 192


def select_body(adapter_ref, position_ref, slots_ref, hidden_ref, out_ref):
    out_ref[:TOK, :] = hidden_ref[...]
    for p in range(PROMPTS):
        slot = position_ref[adapter_ref[p]]
        out_ref[DOWN + p * 32 : DOWN + p * 32 + 32, :] = slots_ref[slot, :32, :]
        out_ref[ODOWN + p * 16 : ODOWN + p * 16 + 16, :] = slots_ref[slot, 32:, :]


def select_slots(adapter, position, slots, hidden):
    return pl.pallas_call(
        select_body,
        out_shape=jax.ShapeDtypeStruct((BLOCK_ROWS, FEAT), BF),
        grid_spec=pltpu.PrefetchScalarGridSpec(
            num_scalar_prefetch=2,
            grid=(1,),
            in_specs=[whole(16, 48, FEAT), whole(TOK, FEAT)],
            out_specs=whole(BLOCK_ROWS, FEAT),
        ),
        name="select_slots",
    )(adapter, position, slots, hidden)


def norm_body(me_ref, length_ref, *refs):
    blocks, maps = refs[:8], refs[8:16]
    outs = refs[16:24]
    gain_ref, normed_ref, low_ref, turned_ref = refs[24:]
    order = col_order(me_ref[1])
    values = [b[...].astype(F32) for b in blocks]
    total = sum(jnp.sum(v * v, axis=-1, keepdims=True) for v in values)
    scale = lax.rsqrt(total * (1.0 / (8 * FEAT)) + EPSILON)
    low = jnp.zeros(low_ref.shape, F32)
    for b in range(8):
        gain = gain_ref[order[b]].astype(F32)
        normed = (values[b] * scale * gain).astype(BF)
        normed_ref[order[b] // 2, :, pl.ds(pl.multiple_of(order[b] % 2 * FEAT, FEAT), FEAT)] = normed
        low += lax.dot_general(normed, maps[b][...], (((1,), (1,)), ((), ())), preferred_element_type=F32)
    token = pl.program_id(0) * low.shape[0] + lax.broadcasted_iota(jnp.int32, low.shape, 0)
    prompt = per_token(prompt_rows(length_ref), range(PROMPTS), token)
    mine = lax.broadcasted_iota(jnp.int32, low.shape, 1) // 32 == prompt
    low_ref[...] = jnp.where(mine, low, 0.0).astype(BF)
    for k in range(4):

        @pl.when(pl.program_id(0) == k)
        def _():
            for b in range(2):
                down = outs[2 * k + b][...].astype(F32)
                turned = jnp.concatenate([down, down], axis=0).T.astype(BF)
                turned_ref[b, 0], turned_ref[b, 1] = turned[:256], turned[256:]


def norm_low(me, lengths, blocks, gain):
    rows = 128
    return pl.pallas_call(
        norm_body,
        out_shape=(
            pltpu.HBM((4, TOK, 2 * FEAT), BF),
            pltpu.HBM((TOK, 128), BF),
            pltpu.HBM((8, 2, 256, 128), BF),
        ),
        grid_spec=pltpu.PrefetchScalarGridSpec(
            num_scalar_prefetch=2,
            grid=(TOK // rows,),
            in_specs=[pl.BlockSpec((rows, FEAT), lambda i, *_: (i, 0))] * 8
            + [pl.BlockSpec((128, FEAT), lambda i, *_: (DOWN // 128, 0))] * 8
            + [pl.BlockSpec((64, FEAT), lambda i, *_: (ODOWN // 64, 0))] * 8
            + [whole(8, 1, FEAT)],
            out_specs=(
                pl.BlockSpec((4, rows, 2 * FEAT), lambda i, *_: (0, i, 0)),
                pl.BlockSpec((rows, 128), lambda i, *_: (i, 0)),
                pl.BlockSpec((2, 2, 256, 128), lambda i, *_: (i, 0, 0, 0)),
            ),
        ),
        compiler_params=vmem(20),
        name="norm_low",
    )(me, lengths, *blocks, *blocks, *blocks, gain)


BLOCK = 64
SCALE2 = math.log2(math.e) / math.sqrt(HEAD)


def page_copies(place_ref, pages_ref, cached_ref, sems, base):
    copies = []
    for i in range(16):
        for h in range(2):
            into = cached_ref.at[h, i // 8, pl.ds(i % 8 * PAGE, PAGE)]
            copies.append(pltpu.make_async_copy(pages_ref.at[place_ref[i], h], into, sems.at[base + 2 * i + h]))
    return copies


def attend(length_ref, cache_ref, q_ref, kv_ref, cached_ref, out_ref, m_ref, l_ref, acc_ref):
    rows, span = GROUP * BLOCK, 256 + BLOCK
    prompts = prompt_rows(length_ref)
    begins = [start for start, _ in prompts]
    count, ranks = jnp.int32(0), []
    for p in range(PROMPTS):
        has = cache_ref[p] > 0
        ranks.append(jnp.where(has, count, -1))
        count = count + has.astype(jnp.int32)
    owners = []
    for j in range(2):
        mine = [(ranks[p] == j).astype(jnp.int32) for p in range(PROMPTS)]
        owners.append(
            (
                sum(mine[p] * prompts[p][0] for p in range(PROMPTS)),
                sum(mine[p] * prompts[p][1] for p in range(PROMPTS)),
                sum(mine[p] * cache_ref[p] for p in range(PROMPTS)),
            )
        )

    def block(t, carry):
        start = pl.multiple_of(t * BLOCK, BLOCK)
        lo = pl.multiple_of(jnp.maximum(start - 256, 0), BLOCK)
        cut = pl.ds(start, BLOCK)
        q = q_ref[:, cut, :].reshape(rows, HEAD)
        token = start + (lax.broadcasted_iota(jnp.int32, (rows, 1), 0) & (BLOCK - 1))
        begin = per_token(prompts, begins, token)
        s = lax.dot_general(q, kv_ref[0, pl.ds(lo, span), :], (((1,), (1,)), ((), ())), preferred_element_type=F32)
        key = lo + lax.broadcasted_iota(jnp.int32, (rows, span), 1)
        s = jnp.where((key <= token) & (key >= begin), s, NEG)
        m = jnp.max(s, axis=1, keepdims=True)
        w = jnp.exp2((s - m) * SCALE2)
        m_ref[...] = m
        l_ref[...] = jnp.sum(w, axis=1, keepdims=True)
        acc_ref[...] = jnp.dot(w.astype(BF), kv_ref[1, pl.ds(lo, span), :], preferred_element_type=F32)

        def cached(j):
            first, last, length = owners[j]
            mine = (token >= first) & (token < last)
            s = lax.dot_general(q, cached_ref[0, j], (((1,), (1,)), ((), ())), preferred_element_type=F32)
            at = lax.broadcasted_iota(jnp.int32, (rows, 256), 1)
            head = jnp.where((at > length + token - first - WIN) | (at < SINKS), s[:, :256], NEG)
            at = WIN - PAGE + lax.broadcasted_iota(jnp.int32, (rows, PAGE), 1)
            tail = jnp.where(at < length, s[:, WIN - PAGE :], NEG)
            s = jnp.concatenate([head, s[:, 256 : WIN - PAGE], tail], axis=1)
            m_old = m_ref[...]
            m_new = jnp.where(mine, jnp.maximum(m_old, jnp.max(s, axis=1, keepdims=True)), m_old)
            fade = jnp.exp2((m_old - m_new) * SCALE2)
            w = jnp.exp2((s - jnp.where(mine, m_new, -NEG)) * SCALE2)
            m_ref[...] = m_new
            l_ref[...] = l_ref[...] * fade + jnp.sum(w, axis=1, keepdims=True)
            acc_ref[...] = acc_ref[...] * fade + jnp.dot(w.astype(BF), cached_ref[1, j], preferred_element_type=F32)

        for j in range(2):
            pl.when((owners[j][0] < start + BLOCK) & (owners[j][1] > start))(lambda j=j: cached(j))

        done = (acc_ref[...] * (1.0 / l_ref[...])).astype(BF)
        for h in range(GROUP):
            out_ref[cut, h * HEAD : (h + 1) * HEAD] = done[h * BLOCK : (h + 1) * BLOCK, :]
        return carry

    lax.fori_loop(0, TOK // BLOCK, block, 0)


ATTEND_SCRATCH = [
    pltpu.VMEM((GROUP * BLOCK, 1), F32),
    pltpu.VMEM((GROUP * BLOCK, 1), F32),
    pltpu.VMEM((GROUP * BLOCK, HEAD), F32),
    pltpu.VMEM((2, 2, WIN, HEAD), BF),
]


def attention_body(
    length_ref, cache_ref, place_ref, adapter_ref, position_ref,
    normed_ref, w_ref, low_hbm, rope_hbm, gains_hbm, pages_ref,
    out_ref, kv_ref,
    m_ref, l_ref, sum_ref, cached_ref, x, w, up, acc, q_ref, low_ref, rope_ref, gains_ref, sems,
):
    def chunk(k):
        rows = w_ref.at[pl.ds(4 * k, 4), pl.ds(0, 256), pl.ds(0, 768)]
        return [
            pltpu.make_async_copy(normed_ref.at[k], x.at[k], sems.at[2 * k]),
            pltpu.make_async_copy(rows, w.at[k], sems.at[2 * k + 1]),
        ]

    chunks = [chunk(k) for k in range(4)]
    for copy in chunks[0]:
        copy.start()
    up[...] = jnp.zeros_like(up)
    maps = []
    for p in range(PROMPTS):
        slot = position_ref[adapter_ref[p]]
        q_part = w_ref.at[slot, pl.ds(256, 16), pl.ds(0, 512)]
        v_part = w_ref.at[slot, pl.ds(256, 16), pl.ds(512, HEAD)]
        maps.append(pltpu.make_async_copy(q_part, up.at[pl.ds(p * 32, 16), pl.ds(0, 512)], sems.at[8 + 2 * p]))
        maps.append(pltpu.make_async_copy(v_part, up.at[pl.ds(p * 32 + 16, 16), pl.ds(512, HEAD)], sems.at[9 + 2 * p]))
    maps.append(pltpu.make_async_copy(low_hbm, low_ref, sems.at[48]))
    maps.append(pltpu.make_async_copy(rope_hbm, rope_ref, sems.at[49]))
    maps.append(pltpu.make_async_copy(gains_hbm, gains_ref, sems.at[50]))
    for copy in chunks[1] + maps:
        copy.start()
    pages = page_copies(place_ref, pages_ref, cached_ref, sems, 16)
    for k in range(4):
        for copy in chunks[k]:
            copy.wait()
        if k + 2 < 4:
            for copy in chunks[k + 2]:
                copy.start()
        if k == 2:
            for copy in pages:
                copy.start()
        part = jnp.dot(x[k], w[k].reshape(1024, 768), preferred_element_type=F32)
        if k == 0:
            acc[...] = part
        else:
            acc[...] += part
    for copy in maps:
        copy.wait()
    change = 0.5 * jnp.dot(low_ref[...], up[...], preferred_element_type=F32)
    rope = rope_ref[...]
    front = lax.broadcasted_iota(jnp.int32, rope.shape, 1) < HEAD // 2
    swapped = pltpu.roll(rope, HEAD // 2, 1)
    cos, sin = jnp.where(front, rope, swapped), jnp.where(front, -swapped, rope)

    def finish(raw, gain):
        scale = lax.rsqrt(jnp.mean(raw * raw, axis=-1, keepdims=True) + EPSILON)
        x = raw * scale * gain
        return (x * cos + pltpu.roll(x, HEAD // 2, 1) * sin).astype(BF)

    for h in range(GROUP):
        cut = slice(h * HEAD, (h + 1) * HEAD)
        q_ref[h] = finish(acc[:, cut] + change[:, cut], gains_ref[0:1, :])
    kv_ref[0] = finish(acc[:, 512:640], gains_ref[1:2, :])
    kv_ref[1] = (acc[:, 640:768] + change[:, 512:640]).astype(BF)
    for copy in pages:
        copy.wait()
    attend(length_ref, cache_ref, q_ref, kv_ref, cached_ref, out_ref, m_ref, l_ref, sum_ref)


def attention(lengths, cached, place, adapter, position, normed, weight, low, rope, gains, pages):
    hbm = pl.BlockSpec(memory_space=pl.ANY)
    return pl.pallas_call(
        attention_body,
        out_shape=(
            jax.ShapeDtypeStruct((TOK, FEAT), BF),
            jax.ShapeDtypeStruct((2, TOK, HEAD), BF),
        ),
        grid_spec=pltpu.PrefetchScalarGridSpec(
            num_scalar_prefetch=5,
            grid=(1,),
            in_specs=[hbm] * 6,
            out_specs=(whole(TOK, FEAT), whole(2, TOK, HEAD)),
            scratch_shapes=ATTEND_SCRATCH
            + [
                pltpu.VMEM((4, TOK, 1024), BF),
                pltpu.VMEM((4, 4, 256, 768), BF),
                pltpu.VMEM((128, 640), BF),
                pltpu.VMEM((TOK, 768), F32),
                pltpu.VMEM((GROUP, TOK, HEAD), BF),
                pltpu.VMEM((TOK, 128), BF),
                pltpu.VMEM((TOK, HEAD), F32),
                pltpu.VMEM((2, HEAD), F32),
                pltpu.SemaphoreType.DMA((51,)),
            ],
        ),
        compiler_params=vmem(32),
        name="attention",
    )(
        lengths, cached, place, adapter, position,
        in_hbm(normed), in_hbm(weight), in_hbm(low), in_hbm(rope), in_hbm(gains), in_hbm(pages),
    )


def low_body(length_ref, *refs):
    blocks, turned_ref, low_ref = refs[:8], refs[8], refs[9]
    low = jnp.zeros((TOK, 128), F32)
    for b in range(8):
        low += jnp.dot(blocks[b][...], turned_ref[b].reshape(FEAT, 128), preferred_element_type=F32)
    token = lax.broadcasted_iota(jnp.int32, low.shape, 0)
    lane = lax.broadcasted_iota(jnp.int32, low.shape, 1)
    prompt = per_token(prompt_rows(length_ref), range(PROMPTS), token)
    low = jnp.where((lane & 63) // 16 == prompt, low, 0.0)
    high = low.astype(BF)
    rest = low - high.astype(F32)
    middle = rest.astype(BF)
    least = (rest - middle.astype(F32)).astype(BF)
    low_ref[:, :128] = jnp.where(lane < 64, high, middle)
    low_ref[:, 128:] = jnp.where(lane < 64, least, jnp.zeros_like(least))


def output_low(lengths, blocks, turned):
    return pl.pallas_call(
        low_body,
        out_shape=pltpu.HBM((TOK, 256), BF),
        grid_spec=pltpu.PrefetchScalarGridSpec(
            num_scalar_prefetch=1,
            grid=(1,),
            in_specs=[whole(TOK, FEAT)] * 8 + [whole(8, 2, 256, 128)],
            out_specs=whole(TOK, 256),
        ),
        compiler_params=vmem(20),
        name="output_low",
    )(lengths, *blocks, in_hbm(turned))


def out_body(me_ref, adapter_ref, position_ref, *refs):
    blocks = refs[:8]
    low_hbm, weight_ref, hidden_hbm, out_ref, x, w, oup, low_ref, hidden, acc, sems = refs[8:]
    order = col_order(me_ref[1])
    copies = []
    for b in range(8):
        rows = weight_ref.at[pl.ds(2 * order[b], 2), pl.ds(0, 256)]
        copies.append(pltpu.make_async_copy(rows, w.at[b], sems.at[b]))
        copies.append(pltpu.make_async_copy(blocks[b], x.at[b], sems.at[8 + b]))
    last = [
        pltpu.make_async_copy(hidden_hbm, hidden, sems.at[16]),
        pltpu.make_async_copy(low_hbm, low_ref, sems.at[17]),
    ]
    for p in range(PROMPTS):
        slot = position_ref[adapter_ref[p]]
        rows = weight_ref.at[slot, pl.ds(256, 16)]
        last.append(pltpu.make_async_copy(rows, oup.at[pl.ds(p * 16, 16)], sems.at[18 + p]))
    for copy in copies + last:
        copy.start()
    for i in range(8):
        for copy in copies[2 * i : 2 * i + 2]:
            copy.wait()
        part = jnp.dot(x[i], w[i].reshape(FEAT, FEAT), preferred_element_type=F32)
        if i == 0:
            acc[...] = part
        else:
            acc[...] += part
    for copy in last:
        copy.wait()
    maps = jnp.concatenate([oup[...]] * 4, axis=0)
    change = jnp.dot(low_ref[...], maps, preferred_element_type=F32)
    out_ref[...] = (hidden[...].astype(F32) + acc[...] + 0.5 * change).astype(BF)


def output(me, adapter, position, blocks, low, weight, hidden):
    hbm = pl.BlockSpec(memory_space=pl.ANY)
    return pl.pallas_call(
        out_body,
        out_shape=jax.ShapeDtypeStruct((TOK, FEAT), BF),
        grid_spec=pltpu.PrefetchScalarGridSpec(
            num_scalar_prefetch=3,
            grid=(1,),
            in_specs=[hbm] * 11,
            out_specs=whole(TOK, FEAT),
            scratch_shapes=[
                pltpu.VMEM((8, TOK, FEAT), BF),
                pltpu.VMEM((8, 2, 256, FEAT), BF),
                pltpu.VMEM((64, FEAT), BF),
                pltpu.VMEM((TOK, 256), BF),
                pltpu.VMEM((TOK, FEAT), BF),
                pltpu.VMEM((TOK, FEAT), F32),
                pltpu.SemaphoreType.DMA((22,)),
            ],
        ),
        compiler_params=vmem(24),
        name="output",
    )(
        me, adapter, position,
        *map(in_hbm, blocks), in_hbm(low), in_hbm(weight), in_hbm(hidden),
    )


def on_device(
    hidden_input,
    input_norm_gain,
    query_norm_gain,
    key_norm_gain,
    query_key_value_weight,
    output_weight,
    adapter_down_maps,
    adapter_up_maps,
    output_down_maps,
    output_up_maps,
    prompt_adapter,
    adapter_position,
    prompt_length,
    cache_length,
    page_owner_row,
    page_store_index,
    cache_page_store,
):
    me = jnp.stack([lax.axis_index("row"), lax.axis_index("col")]).astype(jnp.int32)
    wide, rest, slots = pack(
        me,
        query_key_value_weight,
        output_weight,
        adapter_up_maps,
        output_up_maps,
        adapter_down_maps,
        output_down_maps,
    )
    weight = lax.all_gather(wide, "row", axis=0)
    slots = lax.all_to_all(slots, "row", 0, 0)

    picked, place = pick_pages(me, page_owner_row, page_store_index, cache_page_store)
    picked, slots, rest = lax.optimization_barrier((picked, slots, rest))
    rest = lax.all_gather(rest, "row", axis=0)
    pages = lax.all_to_all(picked.reshape(16, 4 * PAGE, HEAD), "row", 0, 0).reshape(32, 2, PAGE, HEAD)

    blocks = gather_col(select_slots(prompt_adapter, adapter_position, slots, hidden_input), BLOCK_ROWS // 2)

    token = lax.broadcasted_iota(jnp.int32, (TOK, HEAD), 0)
    position, start = token, jnp.int32(0)
    for p in range(PROMPTS):
        end = start + prompt_length[0, p]
        position = jnp.where((token >= start) & (token < end), token - start + cache_length[p], position)
        start = end
    frequency = ROPE_BASE ** (-2.0 * jnp.arange(HEAD // 2, dtype=F32) / HEAD)
    angles = position.astype(F32) * jnp.concatenate([frequency, frequency])[None, :]
    front = lax.broadcasted_iota(jnp.int32, (TOK, HEAD), 1) < HEAD // 2
    rope = jnp.where(front, jnp.cos(angles), jnp.sin(angles))

    normed, low, turned = norm_low(me, prompt_length, blocks, input_norm_gain.reshape(8, 1, FEAT))
    gains = jnp.stack([query_norm_gain, key_norm_gain]).astype(F32)
    weight, normed, low, pages, rope, gains = lax.optimization_barrier((weight, normed, low, pages, rope, gains))
    attended, new_cache = attention(
        prompt_length,
        cache_length,
        place,
        prompt_adapter,
        adapter_position,
        normed,
        weight,
        low,
        rope,
        gains,
        pages,
    )
    attended = gather_col(attended, 256)
    low = output_low(prompt_length, attended, turned)
    rest, low = lax.optimization_barrier((rest, low))
    hidden_output = output(me, prompt_adapter, adapter_position, attended, low, rest, hidden_input)
    return hidden_output, new_cache


def solution(mesh):
    return jax.shard_map(
        on_device,
        mesh=mesh,
        in_specs=(
            P("row", "col"),
            P(),
            P(),
            P(),
            P("row", "col"),
            P("row", "col"),
            P("row", None, None),
            P("row", None, "col"),
            P("row", None, "col"),
            P("row", None, None),
            P("row"),
            P(),
            P("row", None),
            P("row"),
            P(),
            P(),
            P("row", None, None, "col"),
        ),
        out_specs=(P("row", "col"), P(None, "row", "col")),
        check_vma=False,
    )
```
